32 devices in a mesh: dp: 2 (over x), row: 4 (over y, core), col: 4 (over z).
Axes of the slice: x: 2, y: 2, z: 4, core: 2. Of those that a mesh axis runs over, the one named last changes fastest.
Arguments:
- tokens: bfloat16 [8, 64, 64, 768], P('dp', 'row', 'col'), may hold values from -6 to 6
- cls_token: bfloat16 [8, 768], P('dp'), may hold values from -6 to 6
- patch_mask: int32 [8, 64, 64], P('dp', 'row', 'col'), may hold values from 0 to 1, as said below
- loss_mask: int32 [8, 64, 64], P('dp', 'row', 'col'), may hold values 0 or 1
- mask_emb: float32 [768], replicated, may hold values from -5 to 5
- ln1_gain: float32 [768], replicated, may hold values from 0.5 to 1.5
- ln1_bias: float32 [768], replicated, may hold values from -1.5 to 1.5
- w_qkv: bfloat16 [768, 2304], replicated, may hold values from -0.21875 to 0.21875
- q_bias: float32 [768], replicated, may hold values from -2.5 to 2.5
- v_bias: float32 [768], replicated, may hold values from -2.5 to 2.5
- rel_table: float32 [12, 50], replicated, may hold values from -4 to 4
- w_out: bfloat16 [768, 768], replicated, may hold values from -0.875 to 0.875
- out_bias: float32 [768], replicated, may hold values from -1.5 to 1.5
- scale_attn: float32 [768], replicated, may hold values from 0.25 to 1.75
- ln2_gain: float32 [768], replicated, may hold values from 0.5 to 1.5
- ln2_bias: float32 [768], replicated, may hold values from -1.5 to 1.5
- w_up: bfloat16 [768, 3072], replicated, may hold values from -0.21875 to 0.21875
- up_bias: float32 [3072], replicated, may hold values from -2.5 to 2.5
- w_down: bfloat16 [3072, 768], replicated, may hold values from -0.109375 to 0.109375
- down_bias: float32 [768], replicated, may hold values from -1.5 to 1.5
- scale_mlp: float32 [768], replicated, may hold values from 0.25 to 1.75
- out_grad: bfloat16 [8, 64, 64, 768], P('dp', 'row', 'col'), may hold values from -6 to 6
Outputs:
- out: bfloat16 [8, 64, 64, 768], P('dp', 'row', 'col')
- out_cls: bfloat16 [8, 768], P('dp')
- d_tokens: float32 [8, 64, 64, 768], P('dp', 'row', 'col')
- d_cls: float32 [8, 768], P('dp')
- d_w_qkv: float32 [768, 2304], P(('row', 'col'), 'dp')
- d_w_out: float32 [768, 768], P(('row', 'col'), 'dp')
- d_w_up: float32 [768, 3072], P(('row', 'col'), 'dp')
- d_w_down: float32 [3072, 768], P(('row', 'col'), 'dp')
- d_mask_emb: float32 [768], replicated
- d_ln1_gain: float32 [768], replicated
- d_ln1_bias: float32 [768], replicated
- d_q_bias: float32 [768], replicated
- d_v_bias: float32 [768], replicated
- d_rel_table: float32 [12, 50], replicated
- d_out_bias: float32 [768], replicated
- d_scale_attn: float32 [768], replicated
- d_ln2_gain: float32 [768], replicated
- d_ln2_bias: float32 [768], replicated
- d_up_bias: float32 [3072], replicated
- d_down_bias: float32 [768], replicated
- d_scale_mlp: float32 [768], replicated
The draws below stay inside these ranges and needn't reach their ends.
Inputs may be any that keep to these rules, and one draw needn't show every extreme that they name: `patch_mask`: 1 marks a patch that is replaced by the mask embedding. Each page draws its own rate of ones, from 20 to 60 percent. `loss_mask`: 1 marks a patch whose loss counts where it is masked.
All inputs are finite; a program needn't handle non-finite values. No bound on the sum of `loss_mask` on one device may be relied on, other than what follows from the above.
Results may differ from the reference program's by a relative error of at most 0.012.
Values may be sent and summed in bfloat16 or wider, within the bound.
No kernel may reach another device: no remote copies, remote signals or barrier semaphores. Data moves between devices by JAX's collectives and lax.ppermute only.
A program may use at most 832 MiB of HBM per device.

```python
import math
import jax
import jax.numpy as jnp
from jax import lax

D = 768
HEADS = 12
HEAD = 64
FF = 3072
PAGES = 8
GRID_R = 64
GRID_C = 64


def draw_patch_mask(key, part):
    rate_key, roll_key = jax.random.split(key)
    page_rate = jax.random.randint(rate_key, (PAGES, 1, 1), 20, 61)
    page_roll = jax.random.randint(roll_key, (PAGES, GRID_R, GRID_C), 0, 100)
    return (page_roll < page_rate).astype(jnp.int32)


def set_ends(values, own_key, low, largest):
    index_at = [jax.random.randint(jax.random.fold_in(own_key, axis), (), 0, length) for axis, length in enumerate(values.shape)]
    widest = values.shape.index(max(values.shape))
    beside = index_at[:widest] + [(index_at[widest] + 1) % values.shape[widest]] + index_at[widest + 1:]
    return values.at[tuple(index_at)].set(low).at[tuple(beside)].set(largest)


def block_levels(key, shape, pieces, smallest, high):
    factor_of = 1.0
    for position, shards_of in pieces:
        draws = jax.random.uniform(jax.random.fold_in(jax.random.fold_in(key, 6), position), (shards_of,), jnp.float32, smallest / len(pieces), high / len(pieces))
        factor_of = factor_of * jnp.repeat(jnp.exp(draws), shape[position] // shards_of).reshape((-1,) + (1,) * (len(shape) - 1 - position))
    return factor_of


def gaussian(own_key, extent, scale, most, shards=(), held_as=jnp.bfloat16):
    loudness = block_levels(own_key, extent, shards, -0.22, 0.18) if shards else 1.0
    array = jax.random.normal(own_key, extent, jnp.float32) * scale * loudness
    return jnp.minimum(jnp.maximum(array, -most), most).astype(held_as)


def setup_inputs(seed: int = 0) -> dict:
    seeds = jax.random.split(jax.random.key(seed), 23)
    tokens = gaussian(seeds[0], (PAGES, GRID_R, GRID_C, D), 1.0, 6.0, ((0, 2), (1, 4), (2, 4)))
    cls_token = gaussian(seeds[1], (PAGES, D), 1.0, 6.0, ((0, 2),))
    patch_mask = draw_patch_mask(jax.random.fold_in(seeds[22], 71), 0)
    loss_mask = set_ends((jax.random.randint(seeds[3], (PAGES, GRID_R, GRID_C), 0, 4) < 3).astype(jnp.int32), jax.random.fold_in(seeds[3], 1), 0, 1)
    mask_emb = gaussian(seeds[4], (D,), 1.0, 5.0, (), jnp.float32)
    ln1_gain = jnp.clip(1.0 + 0.1 * jax.random.normal(seeds[5], (D,), jnp.float32), 0.5, 1.5)
    ln1_bias = gaussian(seeds[6], (D,), 0.3, 1.5, (), jnp.float32)
    w_qkv = gaussian(seeds[7], (D, 3 * D), D ** -0.5, 0.21875)
    q_bias = gaussian(seeds[8], (D,), 0.5, 2.5, (), jnp.float32)
    v_bias = gaussian(seeds[9], (D,), 0.5, 2.5, (), jnp.float32)
    rel_table = gaussian(seeds[10], (HEADS, 50), 1.0, 4.0, (), jnp.float32)
    w_out = gaussian(seeds[11], (D, D), (D // 16) ** -0.5, 0.875)
    out_bias = gaussian(seeds[12], (D,), 0.3, 1.5, (), jnp.float32)
    scale_attn = jnp.clip(1.0 + 0.15 * jax.random.normal(seeds[13], (D,), jnp.float32), 0.25, 1.75)
    ln2_gain = jnp.clip(1.0 + 0.1 * jax.random.normal(seeds[14], (D,), jnp.float32), 0.5, 1.5)
    ln2_bias = gaussian(seeds[15], (D,), 0.3, 1.5, (), jnp.float32)
    w_up = gaussian(seeds[16], (D, FF), D ** -0.5, 0.21875)
    up_bias = gaussian(seeds[17], (FF,), 0.5, 2.5, (), jnp.float32)
    w_down = gaussian(seeds[18], (FF, D), FF ** -0.5, 0.109375)
    down_bias = gaussian(seeds[19], (D,), 0.3, 1.5, (), jnp.float32)
    scale_mlp = jnp.clip(1.0 + 0.15 * jax.random.normal(seeds[20], (D,), jnp.float32), 0.25, 1.75)
    out_grad = gaussian(seeds[21], (PAGES, GRID_R, GRID_C, D), 1.0, 6.0, ((0, 2), (1, 4), (2, 4)))
    return {"tokens": tokens, "cls_token": cls_token, "patch_mask": patch_mask, "loss_mask": loss_mask, "mask_emb": mask_emb, "ln1_gain": ln1_gain, "ln1_bias": ln1_bias, "w_qkv": w_qkv, "q_bias": q_bias, "v_bias": v_bias, "rel_table": rel_table, "w_out": w_out, "out_bias": out_bias, "scale_attn": scale_attn, "ln2_gain": ln2_gain, "ln2_bias": ln2_bias, "w_up": w_up, "up_bias": up_bias, "w_down": w_down, "down_bias": down_bias, "scale_mlp": scale_mlp, "out_grad": out_grad}


@jax.custom_vjp
def low(v):
    return lax.optimization_barrier(v.astype(jnp.bfloat16)).astype(jnp.float32)

@jax.custom_vjp
def low_back(v):
    return v

def low_keep(v):
    return (low(v), None)

def low_pass(kept, grad):
    return (grad,)

def back_keep(v):
    return (v, None)

def back_low(kept, grad):
    return (low(grad),)
low.defvjp(low_keep, low_pass)
low_back.defvjp(back_keep, back_low)

def layer_norm(inputs, norm_gain, norm_bias):
    row_mean = lax.optimization_barrier(jnp.mean(inputs, axis=-1, keepdims=True))
    centred = inputs - row_mean
    variance = lax.optimization_barrier(jnp.mean(centred * centred, axis=-1, keepdims=True))
    return centred * lax.rsqrt(variance + 1e-06) * norm_gain + norm_bias

def soft_weights(scores):
    row_top = lax.optimization_barrier(jnp.max(scores, axis=-1, keepdims=True))
    exp_terms = jnp.exp(scores - row_top)
    return exp_terms / lax.optimization_barrier(jnp.sum(exp_terms, axis=-1, keepdims=True))

def page_forward(params, page_tokens, class_token, page_mask):
    grid_rows, grid_cols = page_mask.shape
    highest = lax.Precision.HIGHEST
    swapped = jnp.where(page_mask[:, :, None] == 1, params['mask_emb'], page_tokens)
    sequence = jnp.concatenate([class_token[None, :], swapped.reshape(grid_rows * grid_cols, D)], axis=0)
    normed = low(layer_norm(sequence, params['ln1_gain'], params['ln1_bias']))
    projected = jnp.dot(normed, params['w_qkv'], precision=highest)
    query_rows = low(low_back(projected[:, :D] + params['q_bias']))
    key_rows = low(low_back(projected[:, D:2 * D]))
    value_rows = low(low_back(projected[:, 2 * D:] + params['v_bias']))
    score_scale = 1.0 / math.sqrt(HEAD)
    patch_query = query_rows[1:].reshape(grid_rows, grid_cols, HEADS, HEAD)
    pad_width = ((3, 3), (3, 3), (0, 0), (0, 0))
    key_pad = jnp.pad(key_rows[1:].reshape(grid_rows, grid_cols, HEADS, HEAD), pad_width)
    value_pad = jnp.pad(value_rows[1:].reshape(grid_rows, grid_cols, HEADS, HEAD), pad_width)
    inside = jnp.pad(jnp.ones((grid_rows, grid_cols), jnp.float32), 3) > 0.5
    class_key = key_rows[0].reshape(HEADS, HEAD)
    class_value = value_rows[0].reshape(HEADS, HEAD)
    score_list = []
    for shift_r in range(7):
        for shift_c in range(7):
            key_part = key_pad[shift_r:shift_r + grid_rows, shift_c:shift_c + grid_cols]
            raw_score = jnp.einsum('ijhd,ijhd->ijh', patch_query, key_part, precision=highest)
            score_val = low_back(raw_score) * score_scale + params['rel_table'][:, shift_r * 7 + shift_c]
            window_ok = inside[shift_r:shift_r + grid_rows, shift_c:shift_c + grid_cols][:, :, None]
            score_list.append(jnp.where(window_ok, score_val, -1e+30))
    raw_score = jnp.einsum('ijhd,hd->ijh', patch_query, class_key, precision=highest)
    score_list.append(low_back(raw_score) * score_scale + params['rel_table'][:, 49])
    scores = jnp.stack(score_list, axis=-1)
    kept_probs = low(soft_weights(scores))
    mixed = jnp.einsum('ijh,hd->ijhd', kept_probs[..., 49], class_value, precision=highest)
    for shift_r in range(7):
        for shift_c in range(7):
            value_part = value_pad[shift_r:shift_r + grid_rows, shift_c:shift_c + grid_cols]
            mixed = mixed + kept_probs[..., shift_r * 7 + shift_c, None] * value_part
    class_query = query_rows[0].reshape(HEADS, HEAD)
    class_scores = jnp.einsum('nhd,hd->hn', key_rows.reshape(-1, HEADS, HEAD), class_query, precision=highest) * score_scale
    class_probs = soft_weights(class_scores)
    class_mixed = jnp.einsum('hn,nhd->hd', class_probs, value_rows.reshape(-1, HEADS, HEAD), precision=highest)
    attended = low(low_back(jnp.concatenate([class_mixed.reshape(1, D), mixed.reshape(grid_rows * grid_cols, D)], axis=0)))
    branch = low_back(jnp.dot(attended, params['w_out'], precision=highest) + params['out_bias'])
    residual = sequence + params['scale_attn'] * branch
    normed_two = low(layer_norm(residual, params['ln2_gain'], params['ln2_bias']))
    hidden = low_back(jnp.dot(normed_two, params['w_up'], precision=highest) + params['up_bias'])
    activated = low(jax.nn.gelu(hidden, approximate=False))
    mlp_out = low_back(jnp.dot(activated, params['w_down'], precision=highest) + params['down_bias'])
    block_out = residual + params['scale_mlp'] * mlp_out
    return (block_out[1:].reshape(grid_rows, grid_cols, D), block_out[0])

def add_trees(first_tree, second_tree):
    return jax.tree.map(jnp.add, first_tree, second_tree)

def reference(tokens, cls_token, patch_mask, loss_mask, mask_emb, ln1_gain, ln1_bias, w_qkv, q_bias, v_bias, rel_table, w_out, out_bias, scale_attn, ln2_gain, ln2_bias, w_up, up_bias, w_down, down_bias, scale_mlp, out_grad):
    params = {'mask_emb': mask_emb.astype(jnp.float32), 'ln1_gain': ln1_gain.astype(jnp.float32), 'ln1_bias': ln1_bias.astype(jnp.float32), 'w_qkv': w_qkv.astype(jnp.float32), 'q_bias': q_bias.astype(jnp.float32), 'v_bias': v_bias.astype(jnp.float32), 'rel_table': rel_table.astype(jnp.float32), 'w_out': w_out.astype(jnp.float32), 'out_bias': out_bias.astype(jnp.float32), 'scale_attn': scale_attn.astype(jnp.float32), 'ln2_gain': ln2_gain.astype(jnp.float32), 'ln2_bias': ln2_bias.astype(jnp.float32), 'w_up': w_up.astype(jnp.float32), 'up_bias': up_bias.astype(jnp.float32), 'w_down': w_down.astype(jnp.float32), 'down_bias': down_bias.astype(jnp.float32), 'scale_mlp': scale_mlp.astype(jnp.float32)}

    def one_page(running, page_data):
        page_tokens, class_token, page_mask, page_loss, page_grad = page_data

        def forward(param_tree, tokens_in, class_in):
            return page_forward(param_tree, tokens_in, class_in, page_mask)
        outputs, pullback = jax.vjp(forward, params, page_tokens.astype(jnp.float32), class_token.astype(jnp.float32))
        weight_mask = (page_mask * page_loss).astype(jnp.float32)[:, :, None]
        cotangent = (page_grad.astype(jnp.float32) * weight_mask, jnp.zeros((D,), jnp.float32))
        grads_param, grad_tokens, grad_class = pullback(cotangent)
        running = add_trees(running, grads_param)
        return (running, (outputs[0].astype(jnp.bfloat16), outputs[1].astype(jnp.bfloat16), grad_tokens, grad_class))
    start = jax.tree.map(jnp.zeros_like, params)
    totals, (out, out_cls, d_tokens, d_cls) = lax.scan(one_page, start, (tokens, cls_token, patch_mask, loss_mask, out_grad))
    return (out, out_cls, d_tokens, d_cls, totals['w_qkv'], totals['w_out'], totals['w_up'], totals['w_down'], totals['mask_emb'], totals['ln1_gain'], totals['ln1_bias'], totals['q_bias'], totals['v_bias'], totals['rel_table'], totals['out_bias'], totals['scale_attn'], totals['ln2_gain'], totals['ln2_bias'], totals['up_bias'], totals['down_bias'], totals['scale_mlp'])
```

```python
import functools
import math

import jax
import jax.numpy as jnp
import numpy as np
from jax import lax
from jax.experimental import pallas as pl
from jax.experimental.pallas import tpu as pltpu
from jax.sharding import PartitionSpec as P

F32 = jnp.float32
BF16 = jnp.bfloat16
NEG = -1e30
REACH = 3
SPAN = 7
BAND = 4
SIDE = 8
LANES = 128
FLAG = 1024.0
EPS = 1e-06
MIB = 1 << 20


def dot(a, b):
    return jnp.dot(a, b, preferred_element_type=F32)


def dot_t(a, b):
    return lax.dot_general(a, b, (((1,), (1,)), ((), ())), preferred_element_type=F32)


def dot_0(a, b):
    return lax.dot_general(a, b, (((0,), (0,)), ((), ())), preferred_element_type=F32)


def split3(x):
    hi = x.astype(BF16)
    rest = x - hi.astype(F32)
    mid = rest.astype(BF16)
    low = (rest - mid.astype(F32)).astype(BF16)
    return hi, mid, low


def norm_parts(x):
    c = x - jnp.mean(x, axis=-1, keepdims=True)
    inv = lax.rsqrt(jnp.mean(c * c, axis=-1, keepdims=True) + EPS)
    return c * inv, inv


def norm_pull(e, unit, inv):
    return inv * (
        e
        - jnp.mean(e, axis=-1, keepdims=True)
        - unit * jnp.mean(e * unit, axis=-1, keepdims=True)
    )


def unmask(x, emb):
    return jnp.where(x > FLAG / 2, emb, x)


class Geometry:
    def __init__(self, pages, rows, cols, width, heads):
        self.pages, self.rows, self.cols = pages, rows, cols
        self.width, self.heads = width, heads
        self.head = width // heads
        self.lanes = 256
        self.stack = self.lanes // self.head
        self.groups = width // self.lanes
        self.own = rows * cols
        self.edge = REACH * cols
        self.side = (rows + 2 * REACH) * SIDE
        self.halo = 2 * self.edge + self.side + 16
        self.bands = rows // BAND
        self.band = BAND * cols
        self.main = (BAND + 2 * REACH) * cols
        self.flank = (BAND + 2 * REACH) * SIDE
        self.slots = self.main + self.flank + 16
        self.cls_at = self.main + self.flank
        slot = np.arange(self.slots)
        r = np.where(slot < self.main, slot // cols, (slot - self.main) // SIDE)
        s = (slot - self.main) % SIDE
        c = np.where(
            slot < self.main,
            slot % cols,
            np.where(s < REACH, s - REACH, np.where(s < 2 * REACH, cols + s - REACH, -1000)),
        )
        is_cls = slot >= self.cls_at
        r = np.where(is_cls, -1000, r)
        c = np.where(is_cls, -1000, c)
        self.slot_row, self.slot_col = r, c
        q = np.arange(self.band)
        a = r[None, :] - (q // cols)[:, None]
        b = c[None, :] - (q % cols)[:, None] + REACH
        ok = (a >= 0) & (a < SPAN) & (b >= 0) & (b < SPAN)
        offset = np.where(ok, a * SPAN + b, -1)
        mirror = np.where(ok, SPAN * SPAN - 1 - offset, -1)
        offset[:, self.cls_at] = SPAN * SPAN
        self.offset = offset.astype(np.int32)
        self.mirror = mirror.astype(np.int32)
        fold = np.full((cols, self.slots), -1, np.int32)
        for i in range(cols):
            for lane in range(SPAN * cols):
                d = lane % cols - i + REACH
                if 0 <= d < SPAN:
                    fold[i, lane] = lane // cols * SPAN + d
            for lane in range(SPAN * SIDE):
                s1 = lane % SIDE
                if s1 < 2 * REACH:
                    col = s1 - REACH if s1 < REACH else cols + s1 - REACH
                    d = col - i + REACH
                    if 0 <= d < SPAN:
                        fold[i, self.main + lane] = lane // SIDE * SPAN + d
            fold[i, self.cls_at] = SPAN * SPAN
        self.fold = fold.T.copy()
        lane = np.arange(self.lanes) // self.head
        self.head_mask = (np.arange(16)[:, None] == lane[None, :]).astype(np.float32)
        stat = np.zeros((self.groups, 16, LANES), np.float32)
        for g in range(self.groups):
            for h in range(self.stack):
                for part in range(3):
                    stat[g, h, 16 * part + g * self.stack + h] = -1.0
                    stat[g, 8 + h, 48 + 16 * part + g * self.stack + h] = -1.0
        self.stat_mask = stat
        self.to_head = (np.arange(width)[:, None] // self.head == np.arange(LANES)[None, :]).astype(
            np.float32
        )

    def block(self, own, halo, b):
        lo, hi = b * self.band, b * self.band + self.main
        e, o = self.edge, self.own
        parts = []
        if lo < e:
            parts.append(halo[lo : min(hi, e)])
        parts.append(own[max(lo - e, 0) : min(hi - e, o)])
        if hi > e + o:
            parts.append(halo[e + max(lo - e - o, 0) : e + hi - e - o])
        at = 2 * e + b * BAND * SIDE
        parts.append(halo[at : at + self.flank])
        parts.append(halo[2 * e + self.side : 2 * e + self.side + 16])
        return jnp.concatenate(parts, axis=0)

    def stacked(self, x, mask):
        return jnp.concatenate([x * mask[h : h + 1] for h in range(self.stack)], axis=0)

    def unstacked(self, r):
        rows = r.shape[0] // self.stack
        lane = lax.broadcasted_iota(jnp.int32, (rows, self.lanes), 1) // self.head
        out = r[(self.stack - 1) * rows :]
        for h in range(self.stack - 1):
            out = jnp.where(lane == h, r[h * rows : (h + 1) * rows], out)
        return out


def full(shape):
    return pl.BlockSpec(shape, lambda *_: (0,) * len(shape))


def params(limit, sem=1):
    return pltpu.CompilerParams(
        dimension_semantics=("arbitrary",) * sem, vmem_limit_bytes=limit * MIB
    )


def bias_body(geo, table, off_ref, mir_ref, a_ref, b_ref):
    def one(index_ref, out_ref):
        def rows(i, carry):
            at = pl.multiple_of(i * 8, 8)
            index = index_ref[pl.ds(at, 8), :]
            acc = [jnp.full((8, geo.slots), NEG, F32) for _ in range(geo.heads)]
            for o in range(SPAN * SPAN + 1):
                hit = index == o
                for h in range(geo.heads):
                    acc[h] = jnp.where(hit, table[h, o], acc[h])
            for h in range(geo.heads):
                g, k = divmod(h, geo.stack)
                out_ref[g, pl.ds(k * geo.band + at, 8), :] = acc[h]
            return carry

        lax.fori_loop(0, geo.band // 8, rows, 0)

    one(off_ref, a_ref)
    one(mir_ref, b_ref)


def bias_tables(geo, rel_table):
    shape = jax.ShapeDtypeStruct((geo.groups, geo.stack * geo.band, geo.slots), F32)
    return pl.pallas_call(
        functools.partial(bias_body, geo),
        out_shape=(shape, shape),
        in_specs=[pl.BlockSpec(memory_space=pltpu.SMEM)]
        + [pl.BlockSpec(memory_space=pltpu.VMEM)] * 2,
        out_specs=[pl.BlockSpec(memory_space=pltpu.VMEM)] * 2,
        name="bias_tables",
    )(rel_table, jnp.asarray(geo.offset), jnp.asarray(geo.mirror))


def qkv_body(x_ref, w_ref, vec_ref, bias_ref, o_ref):
    x = unmask(x_ref[...].astype(F32), vec_ref[0:1])
    unit, _ = norm_parts(x)
    normed = (unit * vec_ref[1:2] + vec_ref[2:3]).astype(BF16)
    o_ref[...] = (dot(normed, w_ref[...]) + bias_ref[0:1]).astype(BF16)


def qkv_call(x, w, vec, bias, tile):
    n, d = x.shape
    m = w.shape[1]
    return pl.pallas_call(
        qkv_body,
        out_shape=jax.ShapeDtypeStruct((n, m), BF16),
        grid=(n // tile,),
        in_specs=[
            pl.BlockSpec((tile, d), lambda i: (i, 0)),
            full((d, m)),
            full(vec.shape),
            full(bias.shape),
        ],
        out_specs=pl.BlockSpec((tile, m), lambda i: (i, 0)),
        compiler_params=params(40),
        cost_estimate=pl.CostEstimate(
            flops=2 * n * d * m, transcendentals=n, bytes_accessed=2 * (n * d + d * m + n * m)
        ),
        name="qkv",
    )(x, w, vec, bias)


def attend_body(
    geo, q_ref, k_ref, v_ref, hq_ref, hk_ref, hv_ref, bias_ref, ok_ref, hm_ref, hmf_ref,
    o_ref, lse_ref, cls_ref,
):
    g = pl.program_id(1)
    scale = BF16(1.0 / math.sqrt(geo.head))
    hm = hm_ref[...]
    q, k, v = q_ref[0], k_ref[0], v_ref[0]
    hk, hv = hk_ref[0], hv_ref[0]
    lane = lax.broadcasted_iota(jnp.int32, (geo.band, LANES), 1)

    @pl.when(g == 0)
    def _():
        lse_ref[...] = jnp.zeros_like(lse_ref)

    for b in range(geo.bands):
        rows = slice(b * geo.band, (b + 1) * geo.band)
        qs = geo.stacked(q[rows] * scale, hm)
        s = dot_t(qs, geo.block(k, hk, b)) + bias_ref[g] + ok_ref[b : b + 1]
        top = jnp.max(s, axis=-1, keepdims=True)
        e = jnp.exp(s - top)
        total = jnp.sum(e, axis=-1, keepdims=True)
        p = (e * (1.0 / total)).astype(BF16)
        o_ref[0, rows, :] = geo.unstacked(dot(p, geo.block(v, hv, b))).astype(BF16)
        lse = top + jnp.log(total)
        acc = lse_ref[0, rows, :]
        for h in range(geo.stack):
            acc = jnp.where(
                lane == g * geo.stack + h, lse[h * geo.band : (h + 1) * geo.band], acc
            )
        lse_ref[0, rows, :] = acc
    at = 2 * geo.edge + geo.side
    qc = jnp.broadcast_to(hq_ref[0, at : at + 1, :] * scale, (16, geo.lanes)) * hm
    s = dot_t(qc, k)
    top = jnp.max(s, axis=-1, keepdims=True)
    e = jnp.exp(s - top)
    total = jnp.sum(e, axis=-1, keepdims=True)
    hmf = hmf_ref[...]
    acc = sum(dot(part, v) for part in split3(e))
    cls_ref[0, 0:1, :] = jnp.sum(acc * hmf, axis=0, keepdims=True)
    cls_ref[0, 1:2, :] = jnp.sum(top * hmf, axis=0, keepdims=True)
    cls_ref[0, 2:3, :] = jnp.sum(total * hmf, axis=0, keepdims=True)
    cls_ref[0, 3:8, :] = jnp.zeros((5, geo.lanes), F32)


def lane_spec(rows, lanes, first):
    return pl.BlockSpec((1, rows, lanes), lambda p, g: (p, 0, first + g))


def attend_call(geo, own, halo, bias, ok, hm, hmf):
    G = geo.groups
    mm = 2 * geo.pages * G * geo.bands * 256 * 256 * 256
    return pl.pallas_call(
        functools.partial(attend_body, geo),
        out_shape=(
            jax.ShapeDtypeStruct((geo.pages, geo.own, geo.width), BF16),
            jax.ShapeDtypeStruct((geo.pages, geo.own, LANES), F32),
            jax.ShapeDtypeStruct((geo.pages, 8, geo.width), F32),
        ),
        grid=(geo.pages, G),
        in_specs=[lane_spec(geo.own, geo.lanes, i * G) for i in range(3)]
        + [lane_spec(geo.halo, geo.lanes, i * G) for i in range(3)]
        + [full(bias.shape), full(ok.shape), full(hm.shape), full(hmf.shape)],
        out_specs=[
            lane_spec(geo.own, geo.lanes, 0),
            pl.BlockSpec((1, geo.own, LANES), lambda p, g: (p, 0, 0)),
            lane_spec(8, geo.lanes, 0),
        ],
        compiler_params=params(40, 2),
        cost_estimate=pl.CostEstimate(
            flops=2 * mm, transcendentals=geo.pages * G * geo.bands * 65536, bytes_accessed=16 * MIB
        ),
        name="attend",
    )(own, own, own, halo, halo, halo, bias, ok, hm, hmf)


def mlp_body(
    tile, steps, att_ref, x_ref, og_ref, lse_ref, wout_ref, vec_ref, upb_ref, wup_ref, wdn_ref,
    toh_ref, out_ref, gmx_ref, gres_ref, dwup_ref, dwdn_ref, dwout_ref, vg_ref, dub_ref,
    n2, n2t, gm, branch, resid, mlp, dn2, act, dh,
):
    step = pl.program_id(0)
    n, d = n2.shape
    row = lambda i: vec_ref[i : i + 1]
    tiles = n // tile

    @pl.when(step == 0)
    def _():
        def one(t, carry):
            rows = pl.ds(pl.multiple_of(t * tile, tile), tile)
            br = dot(att_ref[rows, :], wout_ref[...]) + row(3)
            branch[rows, :] = br
            x = unmask(x_ref[rows, :].astype(F32), row(0))
            res = x + row(4) * br
            resid[rows, :] = res
            unit, _ = norm_parts(res)
            n2[rows, :] = (unit * row(5) + row(6)).astype(BF16)
            gm[rows, :] = (row(8) * og_ref[rows, :].astype(F32)).astype(BF16)
            mlp[rows, :] = jnp.zeros((tile, d), F32)
            dn2[rows, :] = jnp.zeros((tile, d), F32)
            return carry

        lax.fori_loop(0, tiles, one, 0)
        n2t[...] = n2[...].T
        vg_ref[...] = jnp.zeros_like(vg_ref)

    wup, wdn = wup_ref[...], wdn_ref[...]
    upb = upb_ref[0:1]

    def one(t, total):
        rows = pl.ds(pl.multiple_of(t * tile, tile), tile)
        h = dot(n2[rows, :], wup) + upb
        da = dot_t(gm[rows, :], wdn)
        cdf = 0.5 * (1.0 + lax.erf(h * math.sqrt(0.5)))
        pdf = jnp.exp(-0.5 * h * h) * (1.0 / math.sqrt(2.0 * math.pi))
        a = (h * cdf).astype(BF16)
        g = (da * (cdf + h * pdf)).astype(BF16)
        act[rows, :] = a
        dh[rows, :] = g
        mlp[rows, :] += dot(a, wdn)
        dn2[rows, :] += dot_t(g, wup)
        return total + jnp.sum(g.astype(F32), axis=0, keepdims=True)

    total = lax.fori_loop(0, tiles, one, jnp.zeros((1, wup.shape[1]), F32))
    dub_ref[...] = jnp.broadcast_to(total, dub_ref.shape)
    dwup_ref[...] = dot(n2t[...], dh[...]).astype(BF16)
    dwdn_ref[...] = dot_0(act[...], gm[...]).astype(BF16)

    @pl.when(step == steps - 1)
    def _():
        def one(t, carry):
            rows = pl.ds(pl.multiple_of(t * tile, tile), tile)
            add = lambda i, v: vg_ref.__setitem__(
                (slice(i, i + 1), slice(None)),
                vg_ref[i : i + 1] + jnp.sum(v, axis=0, keepdims=True),
            )
            res = resid[rows, :]
            og = og_ref[rows, :].astype(F32)
            mo = mlp[rows, :] + row(7)
            out_ref[rows, :] = (res + row(8) * mo).astype(BF16)
            add(0, og * mo)
            add(1, gm[rows, :].astype(F32))
            unit, inv = norm_parts(res)
            gn = dn2[rows, :]
            add(2, gn * unit)
            add(3, gn)
            gr = og + norm_pull(gn * row(5), unit, inv)
            gres_ref[rows, :] = gr
            add(4, gr * branch[rows, :])
            gb = (row(4) * gr).astype(BF16)
            add(5, gb.astype(F32))
            n2[rows, :] = gb
            mix = dot_t(gb, wout_ref[...]).astype(BF16)
            gmx_ref[rows, 0:d] = mix
            prod = mix.astype(F32) * att_ref[rows, :].astype(F32)
            toh = toh_ref[...]
            delta = sum(dot(part, toh) for part in split3(prod))
            packed = jnp.zeros((tile, LANES), F32)
            for i, part in enumerate(split3(lse_ref[rows, :]) + split3(delta)):
                part = part.astype(F32)
                packed += part if i == 0 else pltpu.roll(part, 16 * i, 1)
            gmx_ref[rows, d : d + LANES] = packed.astype(BF16)
            return carry

        lax.fori_loop(0, tiles, one, 0)
        dwout_ref[...] = dot_0(att_ref[...], n2[...]).astype(BF16)


def mlp_call(att, x, og, lse, w_out, vec, up_bias, w_up, w_down, to_head, chunk=256, tile=256):
    n, d = x.shape
    ff = w_up.shape[1]
    steps = ff // chunk
    hold = lambda shape: pl.BlockSpec(
        shape, lambda c: (0,) * len(shape), pipeline_mode=pl.Buffered(1)
    )
    return pl.pallas_call(
        functools.partial(mlp_body, tile, steps),
        out_shape=(
            jax.ShapeDtypeStruct((n, d), BF16),
            jax.ShapeDtypeStruct((n, d + LANES), BF16),
            jax.ShapeDtypeStruct((n, d), F32),
            jax.ShapeDtypeStruct((d, ff), BF16),
            jax.ShapeDtypeStruct((ff, d), BF16),
            jax.ShapeDtypeStruct((d, d), BF16),
            jax.ShapeDtypeStruct((8, d), F32),
            jax.ShapeDtypeStruct((8, ff), F32),
        ),
        grid=(steps,),
        in_specs=[
            hold((n, d)),
            hold((n, d)),
            hold((n, d)),
            hold((n, LANES)),
            hold((d, d)),
            hold(vec.shape),
            pl.BlockSpec((1, chunk), lambda c: (0, c)),
            pl.BlockSpec((d, chunk), lambda c: (0, c)),
            pl.BlockSpec((chunk, d), lambda c: (c, 0)),
            hold(to_head.shape),
        ],
        out_specs=[
            hold((n, d)),
            hold((n, d + LANES)),
            hold((n, d)),
            pl.BlockSpec((d, chunk), lambda c: (0, c)),
            pl.BlockSpec((chunk, d), lambda c: (c, 0)),
            hold((d, d)),
            hold((8, d)),
            pl.BlockSpec((8, chunk), lambda c: (0, c)),
        ],
        scratch_shapes=[
            pltpu.VMEM((n, d), BF16),
            pltpu.VMEM((d, n), BF16),
            pltpu.VMEM((n, d), BF16),
            pltpu.VMEM((n, d), F32),
            pltpu.VMEM((n, d), F32),
            pltpu.VMEM((n, d), F32),
            pltpu.VMEM((n, d), F32),
            pltpu.VMEM((n, chunk), BF16),
            pltpu.VMEM((n, chunk), BF16),
        ],
        compiler_params=params(56),
        cost_estimate=pl.CostEstimate(
            flops=2 * n * d * (6 * ff + 3 * d),
            transcendentals=2 * n * ff,
            bytes_accessed=2 * (8 * d * ff // 2 + 10 * n * d),
        ),
        name="mlp",
    )(att, x, og, lse, w_out, vec, up_bias, w_up, w_down, to_head)


def query_grad_body(
    geo, q_ref, k_ref, v_ref, hk_ref, hv_ref, gm_ref, st_ref, bias_ref, ok_ref, hm_ref, sm_ref,
    dq_ref, rel_ref,
):
    g, page = pl.program_id(0), pl.program_id(1)
    scale = 1.0 / math.sqrt(geo.head)
    hm = hm_ref[...]
    sm = sm_ref[g]
    q, k, v, gm, st = q_ref[0], k_ref[0], v_ref[0], gm_ref[0], st_ref[0]
    hk, hv = hk_ref[0], hv_ref[0]
    ones = jnp.ones((geo.slots, LANES), BF16)

    @pl.when(page == 0)
    def _():
        rel_ref[...] = jnp.zeros_like(rel_ref)

    for b in range(geo.bands):
        rows = slice(b * geo.band, (b + 1) * geo.band)
        kb = geo.block(k, hk, b)
        vb = geo.block(v, hv, b)
        qs = geo.stacked(q[rows] * BF16(scale), hm)
        gs = geo.stacked(gm[rows], hm)
        ql = geo.stacked(st[rows], sm[0:8])
        gl = geo.stacked(st[rows], sm[8:16])
        s = dot_t(qs, kb) + dot_t(ql, ones) + bias_ref[g] + ok_ref[b : b + 1]
        ds = jnp.exp(s) * (dot_t(gs, vb) + dot_t(gl, ones))
        rel_ref[0] += ds
        dl = (ds * scale).astype(BF16)
        dq_ref[0, rows, :] = geo.unstacked(dot(dl, kb)).astype(BF16)


def query_grad_call(geo, own, halo, gmx, bias, ok, hm, sm):
    G = geo.groups
    spec = lambda rows, first: pl.BlockSpec(
        (1, rows, geo.lanes), lambda g, p: (p, 0, first * G + g)
    )
    mm = 2 * geo.pages * G * geo.bands * 256 * 256 * 256
    return pl.pallas_call(
        functools.partial(query_grad_body, geo),
        out_shape=(
            jax.ShapeDtypeStruct((geo.pages, geo.own, geo.width), BF16),
            jax.ShapeDtypeStruct(bias.shape, F32),
        ),
        grid=(G, geo.pages),
        in_specs=[
            spec(geo.own, 0),
            spec(geo.own, 1),
            spec(geo.own, 2),
            spec(geo.halo, 1),
            spec(geo.halo, 2),
            spec(geo.own, 0),
            pl.BlockSpec((1, geo.own, LANES), lambda g, p: (p, 0, geo.width // LANES)),
            full(bias.shape),
            full(ok.shape),
            full(hm.shape),
            full(sm.shape),
        ],
        out_specs=[
            spec(geo.own, 0),
            pl.BlockSpec((1,) + bias.shape[1:], lambda g, p: (g, 0, 0)),
        ],
        compiler_params=params(40, 2),
        cost_estimate=pl.CostEstimate(
            flops=3 * mm, transcendentals=geo.pages * G * geo.bands * 65536, bytes_accessed=16 * MIB
        ),
        name="query_grad",
    )(own, own, own, halo, halo, gmx, gmx, bias, ok, hm, sm)


def key_grad_body(
    geo, q_ref, k_ref, v_ref, hq_ref, hk_ref, hv_ref, gm_ref, hgm_ref, st_ref, hst_ref, bias_ref,
    ok_ref, hm_ref, hmf_ref, sm_ref, ct_ref, dk_ref, dv_ref, cls_ref,
):
    g = pl.program_id(1)
    scale = 1.0 / math.sqrt(geo.head)
    hm = hm_ref[...]
    sm = sm_ref[g]
    q, k, v, gm, st = q_ref[0], k_ref[0], v_ref[0], gm_ref[0], st_ref[0]
    hq, hgm, hst = hq_ref[0], hgm_ref[0], hst_ref[0]
    spread = lambda m: jnp.concatenate(
        [jnp.broadcast_to(m[h : h + 1], (geo.band, LANES)) for h in range(geo.stack)], axis=0
    )
    kl, vl = spread(sm[0:8]), spread(sm[8:16])
    for b in range(geo.bands):
        rows = slice(b * geo.band, (b + 1) * geo.band)
        qb = geo.block(q, hq, b)
        gb = geo.block(gm, hgm, b)
        sb = geo.block(st, hst, b)
        ks = geo.stacked(k[rows] * BF16(scale), hm)
        vs = geo.stacked(v[rows], hm)
        s = dot_t(ks, qb) + dot_t(kl, sb) + bias_ref[g] + ok_ref[b : b + 1]
        p = jnp.exp(s)
        ds = p * (dot_t(vs, gb) + dot_t(vl, sb))
        dv_ref[0, rows, :] = geo.unstacked(dot(p.astype(BF16), gb)).astype(BF16)
        dk_ref[0, rows, :] = geo.unstacked(dot((ds * scale).astype(BF16), qb)).astype(BF16)
    at = 2 * geo.edge + geo.side
    kc = jnp.broadcast_to(hk_ref[0, at : at + 1, :] * BF16(scale), (16, geo.lanes)) * hm
    vc = jnp.broadcast_to(hv_ref[0, at : at + 1, :], (16, geo.lanes)) * hm
    zero = jnp.zeros((8, LANES), BF16)
    s = dot_t(kc, q) + dot_t(jnp.concatenate([sm[0:8], zero], 0), st) + ct_ref[g]
    p = jnp.exp(s)
    ds = p * (dot_t(vc, gm) + dot_t(jnp.concatenate([sm[8:16], zero], 0), st))
    hmf = hmf_ref[...]
    dkc = dot((ds * scale).astype(BF16), q)
    dvc = dot(p.astype(BF16), gm)
    cls_ref[0, 0:1, :] = jnp.sum(dkc * hmf, axis=0, keepdims=True)
    cls_ref[0, 1:2, :] = jnp.sum(dvc * hmf, axis=0, keepdims=True)
    cls_ref[0, 2:8, :] = jnp.zeros((6, geo.lanes), F32)


def key_grad_call(geo, own, halo, gmx, hgmx, bias, ok, hm, hmf, sm, ct):
    G = geo.groups
    stat = lambda rows: pl.BlockSpec((1, rows, LANES), lambda p, g: (p, 0, geo.width // LANES))
    mm = 2 * geo.pages * G * geo.bands * 256 * 256 * 256
    return pl.pallas_call(
        functools.partial(key_grad_body, geo),
        out_shape=(
            jax.ShapeDtypeStruct((geo.pages, geo.own, geo.width), BF16),
            jax.ShapeDtypeStruct((geo.pages, geo.own, geo.width), BF16),
            jax.ShapeDtypeStruct((geo.pages, 8, geo.width), F32),
        ),
        grid=(geo.pages, G),
        in_specs=[lane_spec(geo.own, geo.lanes, i * G) for i in range(3)]
        + [lane_spec(geo.halo, geo.lanes, i * G) for i in range(3)]
        + [
            lane_spec(geo.own, geo.lanes, 0),
            lane_spec(geo.halo, geo.lanes, 0),
            stat(geo.own),
            stat(geo.halo),
        ]
        + [full(a.shape) for a in (bias, ok, hm, hmf, sm, ct)],
        out_specs=[
            lane_spec(geo.own, geo.lanes, 0),
            lane_spec(geo.own, geo.lanes, 0),
            lane_spec(8, geo.lanes, 0),
        ],
        compiler_params=params(40, 2),
        cost_estimate=pl.CostEstimate(
            flops=4 * mm, transcendentals=geo.pages * G * geo.bands * 65536, bytes_accessed=20 * MIB
        ),
        name="key_grad",
    )(own, own, own, halo, halo, halo, gmx, hgmx, gmx, hgmx, bias, ok, hm, hmf, sm, ct)


def table_body(geo, acc_ref, fold_ref, o_ref):
    lane = lax.broadcasted_iota(jnp.int32, (geo.cols, geo.slots), 1)
    heads = []
    for g in range(geo.groups):
        for h in range(geo.stack):
            x = acc_ref[g, h * geo.band : (h + 1) * geo.band, :]
            parts = [x[i * geo.cols : (i + 1) * geo.cols] for i in range(BAND)]
            main, side, plain = parts[0], parts[0], parts[0]
            for i in range(1, BAND):
                main = main + pltpu.roll(parts[i], geo.slots - i * geo.cols, 1)
                side = side + pltpu.roll(parts[i], geo.slots - i * SIDE, 1)
                plain = plain + parts[i]
            z = jnp.where(lane < SPAN * geo.cols, main, jnp.where(lane < geo.cls_at, side, plain))
            heads.append(z)
    pad = [jnp.zeros((geo.cols, geo.slots), F32)] * (16 - geo.heads)
    z = jnp.stack(heads + pad, axis=0)
    total = jnp.zeros((16, LANES), F32)
    which = lax.broadcasted_iota(jnp.int32, (geo.slots, LANES), 1)
    for i in range(geo.cols):
        pick = jnp.where(fold_ref[:, i : i + 1] == which, 1.0, 0.0).astype(BF16)
        for part in split3(z[:, i, :]):
            total += dot(part, pick)
    o_ref[...] = total


def table_call(geo, acc):
    return pl.pallas_call(
        functools.partial(table_body, geo),
        out_shape=jax.ShapeDtypeStruct((16, LANES), F32),
        compiler_params=pltpu.CompilerParams(vmem_limit_bytes=40 * MIB),
        name="table_grad",
    )(acc, jnp.asarray(geo.fold))


def qkv_weight_body(
    tile, x_ref, dq_ref, dk_ref, dv_ref, c_ref, cg_ref, vec_ref, dw_ref, vg_ref, nt, ct
):
    which = pl.program_id(0)
    n, d = x_ref.shape

    @pl.when(which == 0)
    def _():
        def one(t, carry):
            rows = pl.ds(pl.multiple_of(t * tile, tile), tile)
            unit, _ = norm_parts(unmask(x_ref[rows, :].astype(F32), vec_ref[0:1]))
            nt[:, rows] = (unit * vec_ref[1:2] + vec_ref[2:3]).astype(BF16).T
            return carry

        lax.fori_loop(0, n // tile, one, 0, unroll=True)
        unit, _ = norm_parts(c_ref[...].astype(F32))
        ct[...] = unit * vec_ref[1:2] + vec_ref[2:3]
        vg_ref[...] = jnp.zeros_like(vg_ref)

    def go(ref, extra, bias_row):
        grad = ref[...]
        if extra is None:
            dw_ref[...] = dot(nt[...], grad).astype(BF16)
        else:
            dw_ref[...] = (dot(nt[...], grad) + dot_0(ct[...].astype(BF16), extra)).astype(BF16)
        if bias_row is not None:
            total = jnp.sum(grad.astype(F32), axis=0, keepdims=True)
            if extra is not None:
                total = total + jnp.sum(extra.astype(F32), axis=0, keepdims=True)
            vg_ref[bias_row : bias_row + 1] = total

    @pl.when(which == 0)
    def _():
        go(dq_ref, None, 0)

    @pl.when(which == 1)
    def _():
        go(dk_ref, cg_ref[:, 0:d], None)

    @pl.when(which == 2)
    def _():
        go(dv_ref, cg_ref[:, d : 2 * d], 1)


def qkv_weight_call(x, dq, dk, dv, cls_rows, cls_grad, vec, tile=256):
    n, d = x.shape
    return pl.pallas_call(
        functools.partial(qkv_weight_body, tile),
        out_shape=(
            jax.ShapeDtypeStruct((d, 3 * d), BF16),
            jax.ShapeDtypeStruct((8, d), F32),
        ),
        grid=(3,),
        in_specs=[full(a.shape) for a in (x, dq, dk, dv, cls_rows, cls_grad, vec)],
        out_specs=[pl.BlockSpec((d, d), lambda i: (0, i)), full((8, d))],
        scratch_shapes=[pltpu.VMEM((d, n), BF16), pltpu.VMEM((16, d), F32)],
        compiler_params=params(48),
        cost_estimate=pl.CostEstimate(
            flops=2 * n * d * 3 * d, transcendentals=n, bytes_accessed=2 * (4 * n * d + 3 * d * d)
        ),
        name="qkv_weight",
    )(x, dq, dk, dv, cls_rows, cls_grad, vec)


def token_grad_body(
    x_ref, dq_ref, dk_ref, dv_ref, gres_ref, w_ref, c_ref, cg_ref, vec_ref, dt_ref, dc_ref, vg_ref
):
    d = x_ref.shape[1]
    wq, wk, wv = w_ref[:, 0:d], w_ref[:, d : 2 * d], w_ref[:, 2 * d : 3 * d]
    gain = vec_ref[1:2]

    @pl.when(pl.program_id(0) == 0)
    def _():
        unit, inv = norm_parts(c_ref[...].astype(F32))
        gn = dot_t(cg_ref[:, 0:d], wk) + dot_t(cg_ref[:, d : 2 * d], wv)
        dc_ref[...] = norm_pull(gn * gain, unit, inv)
        vg_ref[...] = jnp.zeros_like(vg_ref)
        vg_ref[1:2] = jnp.sum(gn * unit, axis=0, keepdims=True)
        vg_ref[2:3] = jnp.sum(gn, axis=0, keepdims=True)

    raw = x_ref[...].astype(F32)
    masked = raw > FLAG / 2
    unit, inv = norm_parts(jnp.where(masked, vec_ref[0:1], raw))
    gn = dot_t(dq_ref[...], wq) + dot_t(dk_ref[...], wk) + dot_t(dv_ref[...], wv)
    gs = gres_ref[...] + norm_pull(gn * gain, unit, inv)
    dt_ref[...] = jnp.where(masked, 0.0, gs)
    vg_ref[0:1] += jnp.sum(jnp.where(masked, gs, 0.0), axis=0, keepdims=True)
    vg_ref[1:2] += jnp.sum(gn * unit, axis=0, keepdims=True)
    vg_ref[2:3] += jnp.sum(gn, axis=0, keepdims=True)


def token_grad_call(x, dq, dk, dv, gres, w_qkv, cls_rows, cls_grad, vec, tile=256):
    n, d = x.shape
    rows = pl.BlockSpec((tile, d), lambda i: (i, 0))
    return pl.pallas_call(
        token_grad_body,
        out_shape=(
            jax.ShapeDtypeStruct((n, d), F32),
            jax.ShapeDtypeStruct((16, d), F32),
            jax.ShapeDtypeStruct((8, d), F32),
        ),
        grid=(n // tile,),
        in_specs=[rows] * 5 + [full(a.shape) for a in (w_qkv, cls_rows, cls_grad, vec)],
        out_specs=[rows, full((16, d)), full((8, d))],
        compiler_params=params(48),
        cost_estimate=pl.CostEstimate(
            flops=2 * n * d * 3 * d, transcendentals=n, bytes_accessed=2 * (8 * n * d + 3 * d * d)
        ),
        name="token_grad",
    )(x, dq, dk, dv, gres, w_qkv, cls_rows, cls_grad, vec)


def passed_along(value, axis, steps):
    count = lax.axis_size(axis)
    first, last = max(0, -steps), min(count, count - steps)
    return lax.ppermute(value, axis, [(i, i + steps) for i in range(first, last)])


def halo_of(x, rows, cols):
    pages, width = x.shape[0], x.shape[-1]
    tile = x.reshape(pages, rows, cols, width)
    top = passed_along(tile[:, rows - REACH :], "row", 1)
    bottom = passed_along(tile[:, :REACH], "row", -1)
    tall = lambda cut: jnp.concatenate([cut(top), cut(tile), cut(bottom)], axis=1)
    left = passed_along(tall(lambda a: a[:, :, cols - REACH :]), "col", 1)
    right = passed_along(tall(lambda a: a[:, :, :REACH]), "col", -1)
    gap = jnp.zeros((pages, rows + 2 * REACH, SIDE - 2 * REACH, width), x.dtype)
    side = jnp.concatenate([left, right, gap], axis=2)
    flat = lambda a: a.reshape(pages, -1, width)
    return [flat(top), flat(bottom), flat(side)]


def summed(value, axis):
    count, step = lax.axis_size(axis), 1
    while step < count:
        value = value + lax.ppermute(value, axis, [(i, i ^ step) for i in range(count)])
        step *= 2
    return value


def shards(
    tokens, cls_token, patch_mask, loss_mask, mask_emb, ln1_gain, ln1_bias, w_qkv, q_bias, v_bias,
    rel_table, w_out, out_bias, scale_attn, ln2_gain, ln2_bias, w_up, up_bias, w_down, down_bias,
    scale_mlp, out_grad,
):
    pages, rows, cols, width = tokens.shape
    heads = rel_table.shape[0]
    geo = Geometry(pages, rows, cols, width, heads)
    count = pages * rows * cols
    grid_rows, grid_cols = rows * lax.axis_size("row"), cols * lax.axis_size("col")

    vec = jnp.concatenate(
        [
            a[None]
            for a in (
                mask_emb, ln1_gain, ln1_bias, out_bias, scale_attn, ln2_gain, ln2_bias, down_bias,
                scale_mlp,
            )
        ]
        + [jnp.zeros((7, width), F32)],
        axis=0,
    )
    qkv_bias = jnp.concatenate([q_bias, jnp.zeros((width,), F32), v_bias])[None]
    qkv_bias = jnp.broadcast_to(qkv_bias, (8, 3 * width))
    hm = jnp.asarray(geo.head_mask, BF16)
    hmf = jnp.asarray(geo.head_mask, F32)
    sm = jnp.asarray(geo.stat_mask, BF16)
    to_head = jnp.asarray(geo.to_head, BF16)
    class_bias = jnp.zeros((geo.groups, 16), F32)
    class_bias = class_bias.at[:, : geo.stack].set(
        rel_table[:, SPAN * SPAN].reshape(geo.groups, geo.stack)
    )
    class_bias = jnp.broadcast_to(class_bias[:, :, None], (geo.groups, 16, geo.own))

    first_row = lax.axis_index("row") * rows - REACH
    first_col = lax.axis_index("col") * cols
    at_row = first_row + BAND * np.arange(8)[:, None] + geo.slot_row[None, :]
    at_col = first_col + geo.slot_col[None, :]
    inside = (at_row >= 0) & (at_row < grid_rows) & (at_col >= 0) & (at_col < grid_cols)
    inside = inside | (np.arange(geo.slots) >= geo.cls_at)[None, :]
    ok = jnp.where(inside, 0.0, NEG).astype(F32)

    flag = jnp.asarray(FLAG, BF16)
    masked = (patch_mask == 1)[..., None]
    marked = jnp.where(masked, flag, tokens)
    counted = (patch_mask * loss_mask == 1)[..., None]
    out_g = jnp.where(counted, out_grad, jnp.zeros((), BF16)).reshape(count, width)
    x = marked.reshape(count, width)

    bias_a, bias_b = bias_tables(geo, rel_table)
    own = qkv_call(x, w_qkv, vec, qkv_bias, geo.own).reshape(pages, geo.own, 3 * width)
    cls_block = jnp.concatenate(
        [cls_token[:, None], jnp.zeros((pages, 15, width), BF16)], axis=1
    )
    halo_x = jnp.concatenate(halo_of(marked, rows, cols) + [cls_block], axis=1)
    halo = qkv_call(
        halo_x.reshape(pages * geo.halo, width), w_qkv, vec, qkv_bias, geo.halo
    ).reshape(pages, geo.halo, 3 * width)

    att, lse, cls_part = attend_call(geo, own, halo, bias_a, ok, hm, hmf)
    att = att.reshape(count, width)
    out, gmx, gres, d_up, d_down, d_wout, vg_mlp, d_upb = mlp_call(
        att, x, out_g, lse.reshape(count, LANES), w_out, vec, up_bias[None], w_up, w_down, to_head
    )
    gmx = gmx.reshape(pages, geo.own, width + LANES)
    dq, rel_acc = query_grad_call(geo, own, halo, gmx, bias_a, ok, hm, sm)
    halo_g = jnp.concatenate(
        halo_of(gmx, rows, cols) + [jnp.zeros((pages, 16, width + LANES), BF16)], axis=1
    )
    dk, dv, cls_grad = key_grad_call(
        geo, own, halo, gmx, halo_g, bias_b, ok, hm, hmf, sm, class_bias
    )
    d_table = table_call(geo, rel_acc)
    dq, dk, dv = (a.reshape(count, width) for a in (dq, dk, dv))
    cls_rows = jnp.concatenate([cls_token, jnp.zeros((16 - pages, width), BF16)], axis=0)
    cls_low = jnp.concatenate([cls_grad[:, 0], cls_grad[:, 1]], axis=-1).astype(BF16)
    cls_low = jnp.concatenate([cls_low, jnp.zeros((16 - pages, 2 * width), BF16)], axis=0)
    d_qkv, vg_qkv = qkv_weight_call(x, dq, dk, dv, cls_rows, cls_low, vec)
    d_tok, d_cls, vg_tok = token_grad_call(x, dq, dk, dv, gres, w_qkv, cls_rows, cls_low, vec)

    tile_axes = ("row", "col")

    def scattered(grad):
        part = lax.psum_scatter(grad, tile_axes, scatter_dimension=0, tiled=True)
        return lax.psum_scatter(part, "dp", scatter_dimension=1, tiled=True).astype(F32)

    weight_grads = [scattered(g) for g in (d_qkv, d_wout, d_up, d_down)]

    slots = lax.axis_size("row") * lax.axis_size("col")
    mine = lax.axis_index("row") * lax.axis_size("col") + lax.axis_index("col")
    here = (jnp.arange(slots) == mine)[:, None, None, None]
    everyone = lax.psum(jnp.where(here, cls_part[None, :, :3], 0.0), tile_axes)
    cls_in = cls_token.astype(F32)
    cls_qkv = halo[:, 2 * geo.edge + geo.side].astype(F32)
    cq, ck, cv = jnp.split(cls_qkv, 3, axis=-1)
    own_score = jnp.sum((cq * ck).reshape(pages, heads, geo.head), axis=-1) / math.sqrt(geo.head)
    own_score = jnp.repeat(own_score, geo.head, axis=-1)
    tops = everyone[:, :, 1]
    top = jnp.maximum(jnp.max(tops, axis=0), own_score)
    weight = jnp.exp(tops - top)
    own_weight = jnp.exp(own_score - top)
    total = jnp.sum(everyone[:, :, 2] * weight, axis=0) + own_weight
    mixed = (jnp.sum(everyone[:, :, 0] * weight, axis=0) + own_weight * cv) / total
    cls_branch = dot(mixed.astype(BF16), w_out) + out_bias
    cls_res = cls_in + scale_attn * cls_branch
    cls_unit, _ = norm_parts(cls_res)
    cls_two = (cls_unit * ln2_gain + ln2_bias).astype(BF16)
    cls_act = jax.nn.gelu(dot(cls_two, w_up) + up_bias, approximate=False).astype(BF16)
    out_cls = (cls_res + scale_mlp * (dot(cls_act, w_down) + down_bias)).astype(BF16)

    table_rows = jnp.pad(d_table[:heads].reshape(-1), (0, 2 * width - heads * LANES)).reshape(2, width)
    vectors = jnp.concatenate(
        [
            d_cls[:pages],
            vg_tok[0:3],
            vg_qkv[0:2],
            vg_mlp[0:6],
            d_upb[0].reshape(-1, width),
            table_rows,
        ],
        axis=0,
    )
    vectors = summed(summed(vectors, "row"), "col")
    d_cls = vectors[:pages]
    v = summed(vectors[pages:], "dp")
    ups = w_up.shape[1] // width
    d_rel = v[11 + ups :].reshape(-1)[: heads * LANES].reshape(heads, LANES)[:, : SPAN * SPAN + 1]
    return (
        out.reshape(tokens.shape),
        out_cls,
        d_tok.reshape(tokens.shape),
        d_cls,
        *weight_grads,
        v[0],
        v[1],
        v[2],
        v[3],
        v[4],
        d_rel,
        v[10],
        v[9],
        v[7],
        v[8],
        v[11 : 11 + ups].reshape(-1),
        v[6],
        v[5],
    )


def solution(mesh):
    tile = P("dp", "row", "col", None)
    flat = P("dp", "row", "col")
    weights = P(("row", "col"), "dp")
    return jax.shard_map(
        shards,
        mesh=mesh,
        in_specs=(tile, P("dp", None), flat, flat) + (P(),) * 17 + (tile,),
        out_specs=(tile, P("dp", None), tile, P("dp", None)) + (weights,) * 4 + (P(),) * 13,
        check_vma=False,
    )
```

```python
import functools
import math

import jax
import jax.numpy as jnp
import numpy as np
from jax import lax
from jax.experimental import pallas as pl
from jax.experimental.pallas import tpu as pltpu
from jax.sharding import PartitionSpec as P

F32 = jnp.float32
BF16 = jnp.bfloat16
NEG = -1e30
REACH = 3
SPAN = 7
BAND = 4
SIDE = 8
LANES = 128
FLAG = 1024.0
ROOM = 56
EPS = 1e-06
MIB = 1 << 20


def dot(a, b):
    return jnp.dot(a, b, preferred_element_type=F32)


def dot_t(a, b):
    return lax.dot_general(a, b, (((1,), (1,)), ((), ())), preferred_element_type=F32)


def dot_0(a, b):
    return lax.dot_general(a, b, (((0,), (0,)), ((), ())), preferred_element_type=F32)


def split3(x):
    hi = x.astype(BF16)
    rest = x - hi.astype(F32)
    mid = rest.astype(BF16)
    low = (rest - mid.astype(F32)).astype(BF16)
    return hi, mid, low


def norm_parts(x):
    c = x - jnp.mean(x, axis=-1, keepdims=True)
    inv = lax.rsqrt(jnp.mean(c * c, axis=-1, keepdims=True) + EPS)
    return c * inv, inv


def norm_pull(e, unit, inv):
    return inv * (
        e
        - jnp.mean(e, axis=-1, keepdims=True)
        - unit * jnp.mean(e * unit, axis=-1, keepdims=True)
    )


def unmask(x, emb):
    return jnp.where(x > FLAG / 2, emb, x)


class Geometry:
    def __init__(self, pages, rows, cols, width, heads):
        self.pages, self.rows, self.cols = pages, rows, cols
        self.width, self.heads = width, heads
        self.head = width // heads
        self.lanes = 256
        self.stack = self.lanes // self.head
        self.groups = width // self.lanes
        self.own = rows * cols
        self.edge = REACH * cols
        self.side = (rows + 2 * REACH) * SIDE
        self.halo = 2 * self.edge + self.side + 16
        self.bands = rows // BAND
        self.band = BAND * cols
        self.main = (BAND + 2 * REACH) * cols
        self.flank = (BAND + 2 * REACH) * SIDE
        self.slots = self.main + self.flank + 16
        self.cls_at = self.main + self.flank
        slot = np.arange(self.slots)
        r = np.where(slot < self.main, slot // cols, (slot - self.main) // SIDE)
        s = (slot - self.main) % SIDE
        c = np.where(
            slot < self.main,
            slot % cols,
            np.where(s < REACH, s - REACH, np.where(s < 2 * REACH, cols + s - REACH, -1000)),
        )
        is_cls = slot >= self.cls_at
        r = np.where(is_cls, -1000, r)
        c = np.where(is_cls, -1000, c)
        self.slot_row, self.slot_col = r, c
        q = np.arange(self.band)
        a = r[None, :] - (q // cols)[:, None]
        b = c[None, :] - (q % cols)[:, None] + REACH
        ok = (a >= 0) & (a < SPAN) & (b >= 0) & (b < SPAN)
        offset = np.where(ok, a * SPAN + b, -1)
        mirror = np.where(ok, SPAN * SPAN - 1 - offset, -1)
        offset[:, self.cls_at] = SPAN * SPAN
        self.offset = offset.astype(np.int32)
        self.mirror = mirror.astype(np.int32)
        fold = np.full((cols, self.slots), -1, np.int32)
        for i in range(cols):
            for lane in range(SPAN * cols):
                d = lane % cols - i + REACH
                if 0 <= d < SPAN:
                    fold[i, lane] = lane // cols * SPAN + d
            for lane in range(SPAN * SIDE):
                s1 = lane % SIDE
                if s1 < 2 * REACH:
                    col = s1 - REACH if s1 < REACH else cols + s1 - REACH
                    d = col - i + REACH
                    if 0 <= d < SPAN:
                        fold[i, self.main + lane] = lane // SIDE * SPAN + d
            fold[i, self.cls_at] = SPAN * SPAN
        self.fold = fold.T.copy()
        lane = np.arange(self.lanes) // self.head
        self.head_mask = (np.arange(16)[:, None] == lane[None, :]).astype(np.float32)
        stat = np.zeros((self.groups, 8, LANES), np.float32)
        every = np.zeros((32, LANES), np.float32)
        for h in range(heads):
            g, k = divmod(h, self.stack)
            for part in range(3):
                stat[g, k, 48 + 16 * part + h] = -1.0
                every[h, 16 * part + h] = -1.0
                every[16 + h, 48 + 16 * part + h] = -1.0
        self.stat_mask = stat
        self.stat_all = every
        self.to_head = (np.arange(width)[:, None] // self.head == np.arange(LANES)[None, :]).astype(
            np.float32
        )
        self.head_rows = self.to_head.T[:16].copy()
        base = np.full((2, cols, self.slots), -1, np.int32)
        for i in range(cols):
            for lane in range(self.slots):
                o = fold[i, lane]
                base[0, i, lane] = o
                base[1, i, lane] = SPAN * SPAN - 1 - o if 0 <= o < SPAN * SPAN else -1
        self.base = base
        tall = rows + 2 * REACH
        self.strip = -(-REACH * tall // 8) * 8
        near = np.zeros((2, self.strip, tall * cols), np.float32)
        flank = np.zeros((2, self.side, self.strip), np.float32)
        for r in range(tall):
            for i in range(REACH):
                near[0, r * REACH + i, r * cols + cols - REACH + i] = 1.0
                near[1, r * REACH + i, r * cols + i] = 1.0
                flank[0, r * SIDE + i, r * REACH + i] = 1.0
                flank[1, r * SIDE + REACH + i, r * REACH + i] = 1.0
        e, o = self.edge, self.own
        self.cut_above, self.cut_own, self.cut_below = (
            near[:, :, :e],
            near[:, :, e : e + o],
            near[:, :, e + o :],
        )
        self.flank_of = flank

    def block(self, own, halo, b):
        lo, hi = b * self.band, b * self.band + self.main
        e, o = self.edge, self.own
        parts = []
        if lo < e:
            parts.append(halo[lo : min(hi, e)])
        parts.append(own[max(lo - e, 0) : min(hi - e, o)])
        if hi > e + o:
            parts.append(halo[e + max(lo - e - o, 0) : e + hi - e - o])
        at = 2 * e + b * BAND * SIDE
        parts.append(halo[at : at + self.flank])
        parts.append(halo[2 * e + self.side : 2 * e + self.side + 16])
        return jnp.concatenate(parts, axis=0)

    def around(self, top, bottom, left, right, flank, last):
        side = dot(flank[0], left) + dot(flank[1], right)
        return jnp.concatenate([top, bottom, side.astype(BF16), last], axis=0)

    def stacked(self, x, mask):
        return jnp.concatenate([x * mask[h : h + 1] for h in range(self.stack)], axis=0)

    def unstacked(self, r):
        rows = r.shape[0] // self.stack
        lane = lax.broadcasted_iota(jnp.int32, (rows, self.lanes), 1) // self.head
        out = r[(self.stack - 1) * rows :]
        for h in range(self.stack - 1):
            out = jnp.where(lane == h, r[h * rows : (h + 1) * rows], out)
        return out


def full(shape):
    return pl.BlockSpec(shape, lambda *_: (0,) * len(shape))


def hold(shape):
    return pl.BlockSpec(shape, lambda *_: (0,) * len(shape), pipeline_mode=pl.Buffered(1))


def params(limit, sem=1):
    return pltpu.CompilerParams(
        dimension_semantics=("arbitrary",) * sem, vmem_limit_bytes=limit * MIB
    )


def bias_body(geo, table, index_ref, out_ref):
    lane = lax.broadcasted_iota(jnp.int32, (geo.cols, geo.slots), 1)
    low = jnp.full((geo.cols, geo.slots), NEG, F32)
    index = index_ref[...]
    pair = 2

    def head(i, carry):
        acc = [low] * (2 * pair)
        for o in range(SPAN * SPAN + 1):
            hit = index == o
            for j in range(pair):
                at = 2 * j + o % 2
                acc[at] = jnp.where(hit, table[i * pair + j, o], acc[at])
        for j in range(pair):
            both = jnp.maximum(acc[2 * j], acc[2 * j + 1])
            main = jnp.where(lane < geo.main, both, low)
            side = jnp.where((lane >= geo.main) & (lane < geo.cls_at), both, low)
            last = jnp.where(lane >= geo.cls_at, both, low)
            h = i * pair + j
            for r in range(BAND):
                if r:
                    both = jnp.maximum(
                        pltpu.roll(main, r * geo.cols, 1), pltpu.roll(side, r * SIDE, 1)
                    )
                else:
                    both = jnp.maximum(main, side)
                at = pl.multiple_of(h % geo.stack * geo.band + r * geo.cols, 8)
                out_ref[h // geo.stack, pl.ds(at, geo.cols), :] = jnp.maximum(both, last)
        return carry

    lax.fori_loop(0, geo.heads // pair, head, 0)


def bias_table(geo, rel_table, which):
    return pl.pallas_call(
        functools.partial(bias_body, geo),
        out_shape=jax.ShapeDtypeStruct((geo.groups, geo.stack * geo.band, geo.slots), F32),
        in_specs=[
            pl.BlockSpec(memory_space=pltpu.SMEM),
            pl.BlockSpec(memory_space=pltpu.VMEM),
        ],
        out_specs=pl.BlockSpec(memory_space=pltpu.VMEM),
        compiler_params=pltpu.CompilerParams(vmem_limit_bytes=ROOM * MIB),
        name="bias_table",
    )(rel_table, jnp.asarray(geo.base[which]))


def qkv_rows(raw, w_ref, vec_ref, o_ref, span=1):
    unit, _ = norm_parts(unmask(raw.astype(F32), vec_ref[0:1]))
    normed = (unit * vec_ref[1:2] + vec_ref[2:3]).astype(BF16)
    n, d = raw.shape
    for i in range(3):
        cols = slice(i * d, (i + 1) * d)
        rows = (dot(normed, w_ref[:, cols]) + vec_ref[9 + i : 10 + i]).astype(BF16)
        for k in range(span):
            o_ref[k, :, cols] = rows[k * (n // span) : (k + 1) * (n // span)]


def qkv_own_body(x_ref, w_ref, vec_ref, o_ref):
    span = x_ref.shape[0]
    raw = jnp.concatenate([x_ref[k] for k in range(span)], axis=0)
    qkv_rows(raw, w_ref, vec_ref, o_ref, span)


def qkv_halo_body(geo, top_ref, bottom_ref, left_ref, right_ref, last_ref, flank_ref, w_ref, vec_ref, o_ref):
    span = top_ref.shape[0]
    raw = [
        geo.around(
            top_ref[k], bottom_ref[k], left_ref[k], right_ref[k], flank_ref[...], last_ref[k]
        )
        for k in range(span)
    ]
    qkv_rows(jnp.concatenate(raw, axis=0), w_ref, vec_ref, o_ref, span)


def by_page(a, span=1):
    return pl.BlockSpec((span,) + a.shape[1:], lambda p: (p,) + (0,) * (len(a.shape) - 1))


def qkv_call(body, rows, paged, whole, name):
    pages, _, d = paged[0].shape
    span = 2 if pages % 2 == 0 else 1
    n = pages * rows
    return pl.pallas_call(
        body,
        out_shape=jax.ShapeDtypeStruct((pages, rows, 3 * d), BF16),
        grid=(pages // span,),
        in_specs=[by_page(a, span) for a in paged] + [hold(a.shape) for a in whole],
        out_specs=pl.BlockSpec((span, rows, 3 * d), lambda p: (p, 0, 0)),
        compiler_params=params(ROOM),
        cost_estimate=pl.CostEstimate(
            flops=6 * n * d * d, transcendentals=n, bytes_accessed=2 * (4 * n * d + 3 * d * d)
        ),
        name=name,
    )(*paged, *whole)


def strips_body(geo, x_ref, top_ref, bottom_ref, above_ref, own_ref, below_ref, right_ref, left_ref):
    d = top_ref.shape[2]
    for p in range(geo.pages):
        for i, out in enumerate((right_ref, left_ref)):
            strip = dot(own_ref[i], x_ref[p]) + dot(above_ref[i], top_ref[p])
            out[p] = (strip + dot(below_ref[i], bottom_ref[p])).astype(BF16)


def strips_call(geo, x, top, bottom):
    cuts = [jnp.asarray(a, BF16) for a in (geo.cut_above, geo.cut_own, geo.cut_below)]
    shape = jax.ShapeDtypeStruct((geo.pages, geo.strip, x.shape[2]), BF16)
    return pl.pallas_call(
        functools.partial(strips_body, geo),
        out_shape=(shape, shape),
        compiler_params=pltpu.CompilerParams(vmem_limit_bytes=ROOM * MIB),
        name="strips",
    )(x, top, bottom, *cuts)


def attend_body(geo, own_ref, halo_ref, bias_ref, ok_ref, hm_ref, o_ref, lse_ref, p_ref):
    scale = BF16(1.0 / math.sqrt(geo.head))
    hm = hm_ref[...]
    lane = lax.broadcasted_iota(jnp.int32, (geo.band, LANES), 1)
    bands = range(geo.bands)
    at = [slice(b * geo.band, (b + 1) * geo.band) for b in bands]
    lses = [jnp.zeros((geo.band, LANES), F32) for _ in bands]

    def part(ref, which, g):
        lo = which * geo.width + g * geo.lanes
        return ref[0, :, lo : lo + geo.lanes]

    def score(g):
        q, k, hk = part(own_ref, 0, g), part(own_ref, 1, g), part(halo_ref, 1, g)
        return [
            dot_t(geo.stacked(q[at[b]] * scale, hm), geo.block(k, hk, b))
            + bias_ref[g]
            + ok_ref[b : b + 1]
            for b in bands
        ]

    def soften(g, scores):
        probs = []
        for b in bands:
            top = jnp.max(scores[b], axis=-1, keepdims=True)
            e = jnp.exp(scores[b] - top)
            total = jnp.sum(e, axis=-1, keepdims=True)
            lse = top + jnp.log(total)
            for h in range(geo.stack):
                rows = slice(h * geo.band, (h + 1) * geo.band)
                lses[b] = jnp.where(lane == g * geo.stack + h, lse[rows], lses[b])
            p = (e * (1.0 / total)).astype(BF16)
            p_ref[0, g, b] = p
            probs.append(p)
        return probs

    def mix(g, probs):
        v, hv = part(own_ref, 2, g), part(halo_ref, 2, g)
        for b in bands:
            rows = geo.unstacked(dot(probs[b], geo.block(v, hv, b)))
            o_ref[0, at[b], g * geo.lanes : (g + 1) * geo.lanes] = rows.astype(BF16)

    scores = score(0)
    for g in range(geo.groups):
        probs = soften(g, scores)
        if g + 1 < geo.groups:
            scores = score(g + 1)
        mix(g, probs)
    for b in bands:
        lse_ref[0, at[b], :] = lses[b]


def attend_call(geo, own, halo, bias, ok, hm):
    G = geo.groups
    mm = 2 * geo.pages * G * geo.bands * 256 * 256 * 256
    outs = (
        jax.ShapeDtypeStruct((geo.pages, geo.own, geo.width), BF16),
        jax.ShapeDtypeStruct((geo.pages, geo.own, LANES), F32),
        jax.ShapeDtypeStruct((geo.pages, G, geo.bands, geo.lanes, geo.slots), BF16),
    )
    return pl.pallas_call(
        functools.partial(attend_body, geo),
        out_shape=outs,
        grid=(geo.pages,),
        in_specs=[by_page(own), by_page(halo)] + [hold(a.shape) for a in (bias, ok, hm)],
        out_specs=[by_page(a) for a in outs],
        compiler_params=params(ROOM),
        cost_estimate=pl.CostEstimate(
            flops=2 * mm, transcendentals=geo.pages * G * geo.bands * 65536, bytes_accessed=16 * MIB
        ),
        name="attend",
    )(own, halo, bias, ok, hm)


def hidden_body(
    tile, steps, att_ref, x_ref, og_ref, wout_ref, vec_ref, wup_ref, wdn_ref,
    act_ref, dh_ref, dw_ref, dub_ref, n2, n2t, gm, up_buf, dn_buf, sems,
):
    step = pl.program_id(0)
    n, d = n2.shape
    row = lambda i: vec_ref[i : i + 1]
    tiles = n // tile
    dests, rows_up, _ = up_buf.shape
    few, rows_dn, _ = dn_buf.shape

    @pl.when(step == 0)
    def _():
        def one(t, carry):
            rows = pl.ds(pl.multiple_of(t * tile, tile), tile)
            x = unmask(x_ref[rows, :].astype(F32), row(0))
            unit, _ = norm_parts(x + row(4) * (dot(att_ref[rows, :], wout_ref[...]) + row(3)))
            n2[rows, :] = (unit * row(5) + row(6)).astype(BF16)
            gm[rows, :] = (row(8) * og_ref[rows, :].astype(F32)).astype(BF16)
            return carry

        lax.fori_loop(0, tiles, one, 0)
        n2t[...] = n2[...].T

    wup, wdn = wup_ref[...], wdn_ref[...]
    upb = vec_ref[pl.ds(12 + step, 1), :]

    def one(t, total):
        rows = pl.ds(pl.multiple_of(t * tile, tile), tile)
        h = dot(n2[rows, :], wup) + upb
        da = dot_t(gm[rows, :], wdn)
        cdf = 0.5 * (1.0 + lax.erf(h * math.sqrt(0.5)))
        pdf = jnp.exp(-0.5 * h * h) * (1.0 / math.sqrt(2.0 * math.pi))
        act_ref[rows, :] = (h * cdf).astype(BF16)
        g = (da * (cdf + h * pdf)).astype(BF16)
        dh_ref[rows, :] = g
        return total + jnp.sum(g.astype(F32), axis=0, keepdims=True)

    total = lax.fori_loop(0, tiles, one, jnp.zeros((1, wup.shape[1]), F32))
    dub_ref[...] = jnp.broadcast_to(total, dub_ref.shape)

    def copies(c):
        at = pl.multiple_of(c * rows_up, 8)
        return (
            pltpu.make_async_copy(up_buf, dw_ref.at[:, pl.ds(at, rows_up), :], sems.at[0]),
            pltpu.make_async_copy(
                dn_buf,
                dw_ref.at[pl.ds(c * few, few), steps * rows_up : steps * rows_up + rows_dn, :],
                sems.at[1],
            ),
        )

    @pl.when(step > 0)
    def _():
        for copy in copies(step - 1):
            copy.wait()

    up_buf[...] = dot(n2t[...], dh_ref[...]).astype(BF16).reshape(up_buf.shape)
    dn_buf[...] = dot_0(act_ref[...], gm[...]).astype(BF16).reshape(dn_buf.shape)
    for copy in copies(step):
        copy.start()

    @pl.when(step == steps - 1)
    def _():
        for copy in copies(step):
            copy.wait()


def hidden_call(att, x, og, w_out, vec, w_up, w_down, dests, tile=512):
    n, d = x.shape
    ff = w_up.shape[1]
    steps = ff // d
    rows_up, rows_dn = d // dests, ff // dests
    return pl.pallas_call(
        functools.partial(hidden_body, tile, steps),
        out_shape=(
            jax.ShapeDtypeStruct((n, ff), BF16),
            jax.ShapeDtypeStruct((n, ff), BF16),
            jax.ShapeDtypeStruct((dests, steps * rows_up + rows_dn, d), BF16),
            jax.ShapeDtypeStruct((8, ff), F32),
        ),
        grid=(steps,),
        in_specs=[hold((n, d))] * 3
        + [
            hold((d, d)),
            hold(vec.shape),
            pl.BlockSpec((d, d), lambda c: (0, c)),
            pl.BlockSpec((d, d), lambda c: (c, 0)),
        ],
        out_specs=[
            pl.BlockSpec((n, d), lambda c: (0, c)),
            pl.BlockSpec((n, d), lambda c: (0, c)),
            pl.BlockSpec(memory_space=pl.ANY),
            pl.BlockSpec((8, d), lambda c: (0, c)),
        ],
        scratch_shapes=[
            pltpu.VMEM((n, d), BF16),
            pltpu.VMEM((d, n), BF16),
            pltpu.VMEM((n, d), BF16),
            pltpu.VMEM((dests, rows_up, d), BF16),
            pltpu.VMEM((dests // steps, rows_dn, d), BF16),
            pltpu.SemaphoreType.DMA((2,)),
        ],
        compiler_params=params(ROOM),
        cost_estimate=pl.CostEstimate(
            flops=2 * n * d * (4 * ff + d),
            transcendentals=2 * n * ff,
            bytes_accessed=2 * (4 * d * ff + 2 * n * ff + 3 * n * d),
        ),
        name="hidden",
    )(att, x, og, w_out, vec, w_up, w_down)


def close_body(
    att_ref, x_ref, og_ref, lse_ref, act_ref, dh_ref, wout_ref, vec_ref, wup_ref, wdn_ref, toh_ref,
    out_ref, gmx_ref, gres_ref, gb_ref, vg_ref,
):
    step = pl.program_id(0)
    d = x_ref.shape[1]
    row = lambda i: vec_ref[i : i + 1]

    @pl.when(step == 0)
    def _():
        vg_ref[...] = jnp.zeros_like(vg_ref)

    def add(i, v):
        vg_ref[i : i + 1] += jnp.sum(v, axis=0, keepdims=True)

    att = att_ref[...]
    br = dot(att, wout_ref[...]) + row(3)
    res = unmask(x_ref[...].astype(F32), row(0)) + row(4) * br
    og = og_ref[...].astype(F32)
    mo = dot(act_ref[...], wdn_ref[...]) + row(7)
    out_ref[...] = (res + row(8) * mo).astype(BF16)
    add(0, og * mo)
    add(1, (row(8) * og).astype(BF16).astype(F32))
    unit, inv = norm_parts(res)
    gn = dot_t(dh_ref[...], wup_ref[...])
    add(2, gn * unit)
    add(3, gn)
    gr = og + norm_pull(gn * row(5), unit, inv)
    gres_ref[...] = gr
    add(4, gr * br)
    gb = (row(4) * gr).astype(BF16)
    add(5, gb.astype(F32))
    gb_ref[...] = gb
    mix = dot_t(gb, wout_ref[...]).astype(BF16)
    gmx_ref[:, 0:d] = mix
    prod = mix.astype(F32) * att.astype(F32)
    toh = toh_ref[...]
    delta = sum(dot(part, toh) for part in split3(prod))
    packed = jnp.zeros(delta.shape, F32)
    for i, part in enumerate(split3(lse_ref[...]) + split3(delta)):
        part = part.astype(F32)
        packed += part if i == 0 else pltpu.roll(part, 16 * i, 1)
    gmx_ref[:, d : d + LANES] = packed.astype(BF16)


def close_call(att, x, og, lse, act, dh, w_out, vec, w_up, w_down, to_head, tile=256):
    n, d = x.shape
    ff = w_up.shape[1]
    rows = lambda width: pl.BlockSpec((tile, width), lambda i: (i, 0))
    return pl.pallas_call(
        close_body,
        out_shape=(
            jax.ShapeDtypeStruct((n, d), BF16),
            jax.ShapeDtypeStruct((n, d + LANES), BF16),
            jax.ShapeDtypeStruct((n, d), F32),
            jax.ShapeDtypeStruct((n, d), BF16),
            jax.ShapeDtypeStruct((8, d), F32),
        ),
        grid=(n // tile,),
        in_specs=[rows(d), rows(d), rows(d), rows(LANES), rows(ff), rows(ff)]
        + [hold(a.shape) for a in (w_out, vec, w_up, w_down, to_head)],
        out_specs=[rows(d), rows(d + LANES), rows(d), rows(d), hold((8, d))],
        compiler_params=params(ROOM),
        cost_estimate=pl.CostEstimate(
            flops=2 * n * d * (2 * ff + 3 * d),
            transcendentals=n,
            bytes_accessed=2 * (2 * d * ff + 2 * n * ff + 8 * n * d),
        ),
        name="close",
    )(att, x, og, lse, act, dh, w_out, vec, w_up, w_down, to_head)


def query_grad_body(geo, p_ref, own_ref, halo_ref, gm_ref, hm_ref, sm_ref, dq_ref, rel_ref):
    scale = 1.0 / math.sqrt(geo.head)
    hm = hm_ref[...]
    bands = range(geo.bands)
    at = [slice(b * geo.band, (b + 1) * geo.band) for b in bands]
    ones = jnp.ones((geo.slots, LANES), BF16)
    join = lambda a, b: jnp.concatenate([a, b], axis=1)
    st = gm_ref[0, :, geo.width :]

    @pl.when(pl.program_id(0) == 0)
    def _():
        rel_ref[...] = jnp.zeros_like(rel_ref)

    def part(ref, which, g):
        lo = which * geo.width + g * geo.lanes
        return ref[0, :, lo : lo + geo.lanes]

    def pull(g):
        gm, v, hv = part(gm_ref, 0, g), part(own_ref, 2, g), part(halo_ref, 2, g)
        sm = sm_ref[g]
        return [
            dot_t(
                join(geo.stacked(gm[at[b]], hm), geo.stacked(st[at[b]], sm)),
                join(geo.block(v, hv, b), ones),
            )
            for b in bands
        ]

    dp = pull(0)
    for g in range(geo.groups):
        ds = [p_ref[0, g, b].astype(F32) * dp[b] for b in bands]
        if g + 1 < geo.groups:
            dp = pull(g + 1)
        total = ds[0]
        for d in ds[1:]:
            total = total + d
        rel_ref[g] += total
        k, hk = part(own_ref, 1, g), part(halo_ref, 1, g)
        for b in bands:
            rows = geo.unstacked(dot((ds[b] * scale).astype(BF16), geo.block(k, hk, b)))
            dq_ref[0, at[b], g * geo.lanes : (g + 1) * geo.lanes] = rows.astype(BF16)


def query_grad_call(geo, probs, own, halo, gmx, hm, sm):
    G = geo.groups
    mm = 2 * geo.pages * G * geo.bands * 256 * 256 * 256
    dq = jax.ShapeDtypeStruct((geo.pages, geo.own, geo.width), BF16)
    table = jax.ShapeDtypeStruct((geo.groups, geo.stack * geo.band, geo.slots), F32)
    return pl.pallas_call(
        functools.partial(query_grad_body, geo),
        out_shape=(dq, table),
        grid=(geo.pages,),
        in_specs=[by_page(a) for a in (probs, own, halo, gmx)]
        + [hold(a.shape) for a in (hm, sm)],
        out_specs=[by_page(dq), hold(table.shape)],
        compiler_params=params(ROOM),
        cost_estimate=pl.CostEstimate(
            flops=2 * mm, transcendentals=0, bytes_accessed=20 * MIB
        ),
        name="query_grad",
    )(probs, own, halo, gmx, hm, sm)


def key_grad_body(
    geo, own_ref, halo_ref, gm_ref, top_ref, bottom_ref, left_ref, right_ref,
    bias_ref, ok_ref, hm_ref, sa_ref, flank_ref, dk_ref, dv_ref, hgm, rowstat,
):
    scale = 1.0 / math.sqrt(geo.head)
    hm = hm_ref[...]
    bands = range(geo.bands)
    at = [slice(b * geo.band, (b + 1) * geo.band) for b in bands]
    last = jnp.zeros((16, gm_ref.shape[2]), BF16)
    hgm[...] = geo.around(
        top_ref[0], bottom_ref[0], left_ref[0], right_ref[0], flank_ref[...], last
    )
    stats, own = hgm[:, geo.width :], gm_ref[0, :, geo.width :]
    row = lax.broadcasted_iota(jnp.int32, (32, geo.slots), 0)
    for b in bands:
        r = dot_t(sa_ref[...], geo.block(own, stats, b))
        rowstat[b] = r + jnp.where(row < 16, ok_ref[b : b + 1], 0.0)

    def part(ref, which, g):
        lo = which * geo.width + g * geo.lanes
        return ref[0, :, lo : lo + geo.lanes]

    def spread(g, b, first):
        at = first + g * geo.stack
        return jnp.concatenate(
            [
                jnp.broadcast_to(rowstat[b, at + h : at + h + 1, :], (geo.band, geo.slots))
                for h in range(geo.stack)
            ],
            axis=0,
        )

    def first(g):
        q, k, v = (part(own_ref, i, g) for i in range(3))
        hq, gm = part(halo_ref, 0, g), part(gm_ref, 0, g)
        hg = hgm[:, g * geo.lanes : (g + 1) * geo.lanes]
        qb = [geo.block(q, hq, b) for b in bands]
        gb = [geo.block(gm, hg, b) for b in bands]
        s = [dot_t(geo.stacked(k[at[b]] * BF16(scale), hm), qb[b]) for b in bands]
        dp = [dot_t(geo.stacked(v[at[b]], hm), gb[b]) for b in bands]
        return qb, gb, s, dp

    now = first(0)
    for g in range(geo.groups):
        qb, gb, s, dp = now
        p = [jnp.exp(s[b] + bias_ref[g] + spread(g, b, 0)) for b in bands]
        ds = [(p[b] * (dp[b] + spread(g, b, 16)) * scale).astype(BF16) for b in bands]
        if g + 1 < geo.groups:
            now = first(g + 1)
        lanes = slice(g * geo.lanes, (g + 1) * geo.lanes)
        for b in bands:
            dv_ref[0, at[b], lanes] = geo.unstacked(dot(p[b].astype(BF16), gb[b])).astype(BF16)
            dk_ref[0, at[b], lanes] = geo.unstacked(dot(ds[b], qb[b])).astype(BF16)


def key_grad_call(geo, own, halo, gmx, pieces, bias, ok, hm, sa, flank):
    G = geo.groups
    mm = 2 * geo.pages * G * geo.bands * 256 * 256 * 256
    out = jax.ShapeDtypeStruct((geo.pages, geo.own, geo.width), BF16)
    return pl.pallas_call(
        functools.partial(key_grad_body, geo),
        out_shape=(out, out),
        grid=(geo.pages,),
        in_specs=[by_page(a) for a in (own, halo, gmx) + pieces]
        + [hold(a.shape) for a in (bias, ok, hm, sa, flank)],
        out_specs=[by_page(out)] * 2,
        scratch_shapes=[
            pltpu.VMEM((geo.halo, geo.width + LANES), BF16),
            pltpu.VMEM((geo.bands, 32, geo.slots), F32),
        ],
        compiler_params=params(ROOM),
        cost_estimate=pl.CostEstimate(
            flops=4 * mm, transcendentals=geo.pages * G * geo.bands * 65536, bytes_accessed=20 * MIB
        ),
        name="key_grad",
    )(own, halo, gmx, *pieces, bias, ok, hm, sa, flank)


def class_attend_body(geo, q_ref, k_ref, v_ref, hr_ref, hrf_ref, o_ref):
    scale = BF16(1.0 / math.sqrt(geo.head))
    hr, hrf = hr_ref[...], hrf_ref[...]
    for p in range(geo.pages):
        k, v = k_ref[p], v_ref[p]
        qc = jnp.broadcast_to(q_ref[p, 0:1, :] * scale, (16, geo.width)) * hr
        s = dot_t(qc, k)
        top = jnp.max(s, axis=-1, keepdims=True)
        e = jnp.exp(s - top)
        total = jnp.sum(e, axis=-1, keepdims=True)
        acc = sum(dot(part, v) for part in split3(e))
        for i, value in enumerate((acc, top, total)):
            at = i * geo.pages + p
            o_ref[at : at + 1, :] = jnp.sum(value * hrf, axis=0, keepdims=True)
    o_ref[3 * geo.pages :, :] = jnp.zeros((16 - 3 * geo.pages, geo.width), F32)


def part_spec(geo, i):
    return pl.BlockSpec((geo.pages, geo.own, geo.width), lambda t: (0, 0, i))


def cls_spec(geo, i):
    return pl.BlockSpec((geo.pages, 16, geo.width), lambda t: (0, geo.halo // 16 - 1, i))


def class_attend_call(geo, own, halo, hr, hrf):
    return pl.pallas_call(
        functools.partial(class_attend_body, geo),
        out_shape=jax.ShapeDtypeStruct((16, geo.width), F32),
        grid=(1,),
        in_specs=[
            cls_spec(geo, 0),
            part_spec(geo, 1),
            part_spec(geo, 2),
            full(hr.shape),
            full(hrf.shape),
        ],
        out_specs=full((16, geo.width)),
        compiler_params=params(ROOM),
        cost_estimate=pl.CostEstimate(
            flops=2 * MIB * 256, transcendentals=16384, bytes_accessed=4 * MIB
        ),
        name="class_attend",
    )(halo, own, own, hr, hrf)


def class_grad_body(
    geo, q_ref, ck_ref, cv_ref, gm_ref, st_ref, hr_ref, hrf_ref, sa_ref, cb_ref, o_ref
):
    scale = 1.0 / math.sqrt(geo.head)
    hr, hrf, sa = hr_ref[...], hrf_ref[...], sa_ref[...]
    d = geo.width
    for p in range(geo.pages):
        q, gm, st = q_ref[p], gm_ref[p], st_ref[p]
        kc = jnp.broadcast_to(ck_ref[p, 0:1, :] * BF16(scale), (16, d)) * hr
        vc = jnp.broadcast_to(cv_ref[p, 0:1, :], (16, d)) * hr
        prob = jnp.exp(dot_t(kc, q) + dot_t(sa[0:16], st) + cb_ref[...])
        ds = prob * (dot_t(vc, gm) + dot_t(sa[16:32], st))
        dk = dot((ds * scale).astype(BF16), q)
        dv = dot(prob.astype(BF16), gm)
        o_ref[p : p + 1, 0:d] = jnp.sum(dk * hrf, axis=0, keepdims=True)
        o_ref[p : p + 1, d : 2 * d] = jnp.sum(dv * hrf, axis=0, keepdims=True)
    o_ref[geo.pages :, :] = jnp.zeros((16 - geo.pages, 2 * d), F32)


def class_grad_call(geo, own, halo, gmx, hr, hrf, sa, class_bias):
    return pl.pallas_call(
        functools.partial(class_grad_body, geo),
        out_shape=jax.ShapeDtypeStruct((16, 2 * geo.width), F32),
        grid=(1,),
        in_specs=[
            part_spec(geo, 0),
            cls_spec(geo, 1),
            cls_spec(geo, 2),
            part_spec(geo, 0),
            pl.BlockSpec((geo.pages, geo.own, LANES), lambda t: (0, 0, geo.width // LANES)),
        ]
        + [full(a.shape) for a in (hr, hrf, sa, class_bias)],
        out_specs=full((16, 2 * geo.width)),
        compiler_params=params(ROOM),
        cost_estimate=pl.CostEstimate(
            flops=4 * MIB * 256, transcendentals=16384, bytes_accessed=4 * MIB
        ),
        name="class_grad",
    )(own, halo, halo, gmx, gmx, hr, hrf, sa, class_bias)


def class_close_body(
    geo, mine_ref, parts_ref, cls_ref, x_ref, toh_ref, wout_ref, vec_ref, wup_ref, wdn_ref,
    out_ref, res, n2, acc,
):
    step = pl.program_id(0)
    d, pages = geo.width, geo.pages
    row = lambda i: vec_ref[i : i + 1]
    places = parts_ref.shape[0]

    @pl.when(step == 0)
    def _():
        mine = mine_ref[0]
        q = jnp.concatenate([cls_ref[p, 0:1, 0:d] for p in range(pages)], axis=0).astype(F32)
        k = jnp.concatenate([cls_ref[p, 0:1, d : 2 * d] for p in range(pages)], axis=0).astype(F32)
        v = jnp.concatenate([cls_ref[p, 0:1, 2 * d :] for p in range(pages)], axis=0).astype(F32)
        toh = toh_ref[...]
        own = sum(dot(part, toh) for part in split3(q * k)) * (1.0 / math.sqrt(geo.head))
        own = sum(dot_t(part, toh) for part in split3(own))
        top = own
        for code in range(places):
            top = jnp.maximum(top, parts_ref[code ^ mine, pages : 2 * pages, :])
        weight = jnp.exp(own - top)
        total, mixed = weight, weight * v
        for code in range(places):
            part = parts_ref.at[code ^ mine]
            weight = jnp.exp(part[pages : 2 * pages, :] - top)
            mixed = mixed + weight * part[0:pages, :]
            total = total + weight * part[2 * pages : 3 * pages, :]
        mixed = (mixed / total).astype(BF16)
        mixed = jnp.concatenate([mixed, jnp.zeros((16 - pages, d), BF16)], axis=0)
        r = x_ref[...].astype(F32) + row(4) * (dot(mixed, wout_ref[...]) + row(3))
        res[...] = r
        unit, _ = norm_parts(r)
        n2[...] = (unit * row(5) + row(6)).astype(BF16)
        acc[...] = jnp.zeros_like(acc)

    h = dot(n2[...], wup_ref[...]) + vec_ref[pl.ds(12 + step, 1), :]
    a = (h * 0.5 * (1.0 + lax.erf(h * math.sqrt(0.5)))).astype(BF16)
    acc[...] += dot(a, wdn_ref[...])

    @pl.when(step == pl.num_programs(0) - 1)
    def _():
        out_ref[...] = (res[...] + row(8) * (acc[...] + row(7))).astype(BF16)


def class_close_call(geo, mine, parts, halo, x, to_head, w_out, vec, w_up, w_down):
    d = geo.width
    ff = w_up.shape[1]
    return pl.pallas_call(
        functools.partial(class_close_body, geo),
        out_shape=jax.ShapeDtypeStruct((16, d), BF16),
        grid=(ff // d,),
        in_specs=[pl.BlockSpec(memory_space=pltpu.SMEM)]
        + [
            full(parts.shape),
            pl.BlockSpec((geo.pages, 16, 3 * d), lambda c: (0, geo.halo // 16 - 1, 0)),
        ]
        + [full(a.shape) for a in (x, to_head, w_out, vec)]
        + [
            pl.BlockSpec((d, d), lambda c: (0, c)),
            pl.BlockSpec((d, d), lambda c: (c, 0)),
        ],
        out_specs=full((16, d)),
        scratch_shapes=[
            pltpu.VMEM((16, d), F32),
            pltpu.VMEM((16, d), BF16),
            pltpu.VMEM((16, d), F32),
        ],
        compiler_params=params(ROOM),
        cost_estimate=pl.CostEstimate(
            flops=64 * d * (2 * ff + d), transcendentals=16 * ff, bytes_accessed=12 * MIB
        ),
        name="class_close",
    )(mine, parts, halo, x, to_head, w_out, vec, w_up, w_down)


def table_body(geo, acc_ref, fold_ref, o_ref):
    lane = lax.broadcasted_iota(jnp.int32, (geo.cols, geo.slots), 1)
    heads = []
    for g in range(geo.groups):
        for h in range(geo.stack):
            x = acc_ref[g, h * geo.band : (h + 1) * geo.band, :]
            parts = [x[i * geo.cols : (i + 1) * geo.cols] for i in range(BAND)]
            main, side, plain = parts[0], parts[0], parts[0]
            for i in range(1, BAND):
                main = main + pltpu.roll(parts[i], geo.slots - i * geo.cols, 1)
                side = side + pltpu.roll(parts[i], geo.slots - i * SIDE, 1)
                plain = plain + parts[i]
            z = jnp.where(lane < SPAN * geo.cols, main, jnp.where(lane < geo.cls_at, side, plain))
            heads.append(z)
    pad = [jnp.zeros((geo.cols, geo.slots), F32)] * (16 - geo.heads)
    z = jnp.stack(heads + pad, axis=0)
    total = jnp.zeros((16, LANES), F32)
    which = lax.broadcasted_iota(jnp.int32, (geo.slots, LANES), 1)
    for i in range(geo.cols):
        pick = jnp.where(fold_ref[:, i : i + 1] == which, 1.0, 0.0).astype(BF16)
        for part in split3(z[:, i, :]):
            total += dot(part, pick)
    o_ref[...] = total


def table_call(geo, acc):
    return pl.pallas_call(
        functools.partial(table_body, geo),
        out_shape=jax.ShapeDtypeStruct((16, LANES), F32),
        compiler_params=pltpu.CompilerParams(vmem_limit_bytes=ROOM * MIB),
        name="table_grad",
    )(acc, jnp.asarray(geo.fold))


def qkv_weight_body(
    tile, cols, at_ref, x_ref, dq_ref, dk_ref, dv_ref, c_ref, cg_ref, vec_ref, att_ref, gb_ref,
    dw_ref, vg_ref, nt, ct
):
    step = pl.program_id(0)
    n, d = x_ref.shape
    width = cg_ref.shape[1] // 2
    core, half, column = at_ref[0], at_ref[1], at_ref[2]

    @pl.when(step == 0)
    def _():
        def one(t, carry):
            rows = pl.ds(pl.multiple_of(t * tile, tile), tile)
            unit, _ = norm_parts(unmask(x_ref[rows, :].astype(F32), vec_ref[0:1]))
            nt[:, rows] = (unit * vec_ref[1:2] + vec_ref[2:3]).astype(BF16).T
            return carry

        lax.fori_loop(0, n // tile, one, 0, unroll=True)
        unit, _ = norm_parts(c_ref[...].astype(F32))
        ct[...] = (unit * vec_ref[1:2] + vec_ref[2:3]).astype(BF16)

    def go(ref, extra):
        grad = ref[...]
        total = jnp.sum(grad.astype(F32), axis=0, keepdims=True)
        dw = dot(nt[...], grad)
        if extra is not None:
            dw = dw + dot_0(ct[...], extra)
            total = total + jnp.sum(extra.astype(F32), axis=0, keepdims=True)
        vg_ref[...] = jnp.broadcast_to(total, vg_ref.shape)
        dw = dw.astype(BF16)
        slab = dw_ref.shape[3]
        for dest in range(4 * cols):
            y, b, c = dest // (2 * cols), dest // cols % 2, dest % cols
            place = (y ^ half) * cols + (c ^ column)
            dw_ref[b ^ core, 0, place] = dw[dest * slab : (dest + 1) * slab]

    @pl.when(step < 2)
    def _():
        go(dq_ref, None)

    @pl.when((step >= 2) & (step < 4))
    def _():
        go(dk_ref, cg_ref[...])

    @pl.when((step >= 4) & (step < 6))
    def _():
        go(dv_ref, cg_ref[...])

    @pl.when(step >= 6)
    def _():
        @pl.when(step == 6)
        def _():
            nt[...] = att_ref[...].T

        go(gb_ref, None)


def qkv_weight_call(where, cols, x, dq, dk, dv, cls_rows, cls_grad, vec, att, gb, tile=256):
    n, d = x.shape
    w = d // 2
    slab = d // (4 * cols)
    at = lambda first: lambda i, p: (0, jnp.clip(i - first, 0, 1))

    def place(i, p):
        half = jnp.where(i < 6, i // 3, i - 6)
        return (0, half ^ p[3], 0, 0, jnp.where(i < 6, i % 3, 3))

    spec = pltpu.PrefetchScalarGridSpec(
        num_scalar_prefetch=1,
        grid=(8,),
        in_specs=[
            full((n, d)),
            pl.BlockSpec((n, w), at(0)),
            pl.BlockSpec((n, w), at(2)),
            pl.BlockSpec((n, w), at(4)),
            full(cls_rows.shape),
            pl.BlockSpec((16, w), lambda i, p: (0, jnp.clip(i - 2, 0, 3))),
            full(vec.shape),
            hold((n, d)),
            pl.BlockSpec((n, w), at(6)),
        ],
        out_specs=[
            pl.BlockSpec((2, 1, 2 * cols, slab, w), place),
            pl.BlockSpec((8, w), lambda i, p: (0, i)),
        ],
        scratch_shapes=[pltpu.VMEM((d, n), BF16), pltpu.VMEM((16, d), BF16)],
    )
    return pl.pallas_call(
        functools.partial(qkv_weight_body, tile, cols),
        out_shape=(
            jax.ShapeDtypeStruct((2, 2, 2 * cols, slab, 4 * w), BF16),
            jax.ShapeDtypeStruct((8, 4 * d), F32),
        ),
        grid_spec=spec,
        compiler_params=params(ROOM),
        cost_estimate=pl.CostEstimate(
            flops=2 * n * d * 3 * d, transcendentals=n, bytes_accessed=2 * (4 * n * d + 3 * d * d)
        ),
        name="qkv_weight",
    )(where, x, dq, dk, dv, cls_rows, cls_grad, vec, att, gb)


def token_grad_body(
    x_ref, dq_ref, dk_ref, dv_ref, gres_ref, w_ref, c_ref, cg_ref, vec_ref, dt_ref, dc_ref, vg_ref
):
    d = x_ref.shape[1]
    wq, wk, wv = w_ref[:, 0:d], w_ref[:, d : 2 * d], w_ref[:, 2 * d : 3 * d]
    gain = vec_ref[1:2]

    @pl.when(pl.program_id(0) == 0)
    def _():
        unit, inv = norm_parts(c_ref[...].astype(F32))
        gn = dot_t(cg_ref[:, 0:d], wk) + dot_t(cg_ref[:, d : 2 * d], wv)
        dc_ref[...] = norm_pull(gn * gain, unit, inv)
        vg_ref[...] = jnp.zeros_like(vg_ref)
        vg_ref[1:2] = jnp.sum(gn * unit, axis=0, keepdims=True)
        vg_ref[2:3] = jnp.sum(gn, axis=0, keepdims=True)

    raw = x_ref[...].astype(F32)
    masked = raw > FLAG / 2
    unit, inv = norm_parts(jnp.where(masked, vec_ref[0:1], raw))
    gn = dot_t(dq_ref[...], wq) + dot_t(dk_ref[...], wk) + dot_t(dv_ref[...], wv)
    gs = gres_ref[...] + norm_pull(gn * gain, unit, inv)
    dt_ref[...] = jnp.where(masked, 0.0, gs)
    vg_ref[0:1] += jnp.sum(jnp.where(masked, gs, 0.0), axis=0, keepdims=True)
    vg_ref[1:2] += jnp.sum(gn * unit, axis=0, keepdims=True)
    vg_ref[2:3] += jnp.sum(gn, axis=0, keepdims=True)


def token_grad_call(x, dq, dk, dv, gres, w_qkv, cls_rows, cls_grad, vec, tile=256):
    n, d = x.shape
    rows = pl.BlockSpec((tile, d), lambda i: (i, 0))
    return pl.pallas_call(
        token_grad_body,
        out_shape=(
            jax.ShapeDtypeStruct((n, d), F32),
            jax.ShapeDtypeStruct((16, d), F32),
            jax.ShapeDtypeStruct((8, d), F32),
        ),
        grid=(n // tile,),
        in_specs=[rows] * 5 + [full(a.shape) for a in (w_qkv, cls_rows, cls_grad, vec)],
        out_specs=[rows, full((16, d)), full((8, d))],
        compiler_params=params(ROOM),
        cost_estimate=pl.CostEstimate(
            flops=2 * n * d * 3 * d, transcendentals=n, bytes_accessed=2 * (8 * n * d + 3 * d * d)
        ),
        name="token_grad",
    )(x, dq, dk, dv, gres, w_qkv, cls_rows, cls_grad, vec)


def passed_along(value, axis, steps):
    count = lax.axis_size(axis)
    first, last = max(0, -steps), min(count, count - steps)
    return lax.ppermute(value, axis, [(i, i + steps) for i in range(first, last)])


def swap(value, axis, bit):
    return lax.ppermute(value, axis, [(i, i ^ bit) for i in range(lax.axis_size(axis))])


def halo_pieces(geo, x):
    top = passed_along(x[:, geo.own - geo.edge :], "row", 1)
    bottom = passed_along(x[:, : geo.edge], "row", -1)
    to_right, to_left = strips_call(geo, x, top, bottom)
    return top, bottom, passed_along(to_right, "col", 1), passed_along(to_left, "col", -1)


def page_sum(part, by):
    return lax.psum_scatter(part, "dp", scatter_dimension=by, tiled=True)


def spread_sum(grad):
    part = lax.psum_scatter(grad, ("row", "col"), scatter_dimension=0, tiled=True)
    return page_sum(part, 1).astype(F32)


def join(values):
    return lax.optimization_barrier(values)


def shards(
    tokens, cls_token, patch_mask, loss_mask, mask_emb, ln1_gain, ln1_bias, w_qkv, q_bias, v_bias,
    rel_table, w_out, out_bias, scale_attn, ln2_gain, ln2_bias, w_up, up_bias, w_down, down_bias,
    scale_mlp, out_grad,
):
    pages, rows, cols, width = tokens.shape
    heads = rel_table.shape[0]
    geo = Geometry(pages, rows, cols, width, heads)
    count = pages * rows * cols
    row_peers, col_peers = lax.axis_size("row"), lax.axis_size("col")
    grid_rows, grid_cols = rows * row_peers, cols * col_peers
    row_at, col_at, page_at = (lax.axis_index(a) for a in ("row", "col", "dp"))

    ups = w_up.shape[1] // width
    vec = jnp.concatenate(
        [
            mask_emb, ln1_gain, ln1_bias, out_bias, scale_attn, ln2_gain, ln2_bias, down_bias,
            scale_mlp, q_bias, jnp.zeros((width,), F32), v_bias, up_bias,
        ]
    ).reshape(12 + ups, width)
    hm = jnp.asarray(geo.head_mask, BF16)
    hr, hrf = jnp.asarray(geo.head_rows, BF16), jnp.asarray(geo.head_rows, F32)
    sm, sa = jnp.asarray(geo.stat_mask, BF16), jnp.asarray(geo.stat_all, BF16)
    to_head, flank = jnp.asarray(geo.to_head, BF16), jnp.asarray(geo.flank_of, BF16)

    at_row = row_at * rows + BAND * np.arange(8)[:, None] - REACH + geo.slot_row[None, :]
    at_col = col_at * cols + geo.slot_col[None, :]
    inside = (at_row >= 0) & (at_row < grid_rows) & (at_col >= 0) & (at_col < grid_cols)
    inside = inside | (np.arange(geo.slots) >= geo.cls_at)[None, :]
    ok = jnp.where(inside, 0.0, NEG).astype(F32)

    masked = (patch_mask == 1)[..., None]
    x = jnp.where(masked, jnp.asarray(FLAG, BF16), tokens).reshape(pages, geo.own, width)
    pieces = halo_pieces(geo, x)
    bias_a = bias_table(geo, rel_table, 0)
    own = qkv_call(qkv_own_body, geo.own, (x,), (w_qkv, vec), "qkv_own")
    first = np.arange(16)[:, None] == 0
    cls_block = jnp.where(first, cls_token[:, None, :], jnp.zeros((), BF16))
    halo = qkv_call(
        functools.partial(qkv_halo_body, geo), geo.halo, pieces + (cls_block,),
        (flank, w_qkv, vec), "qkv_halo",
    )
    att, lse, probs = attend_call(geo, own, halo, bias_a, ok, hm)
    att, lse, x = att.reshape(count, width), lse.reshape(count, LANES), x.reshape(count, width)
    counted = (patch_mask * loss_mask == 1)[..., None]
    out_g = jnp.where(counted, out_grad, jnp.zeros((), BF16)).reshape(count, width)
    act, dh, d_mlp, d_upb = hidden_call(
        att, x, out_g, w_out, vec, w_up, w_down, row_peers * col_peers
    )
    d_mlp = lax.psum_scatter(d_mlp, ("row", "col"), scatter_dimension=0, tiled=True)[0]
    out, gmx, gres, gb, vg_mlp = close_call(
        att, x, out_g, lse, act, dh, w_out, vec, w_up, w_down, to_head
    )
    gmx = gmx.reshape(pages, geo.own, width + LANES)
    pieces = halo_pieces(geo, gmx)
    bias_b = bias_table(geo, rel_table, 1)
    dq, rel_acc = query_grad_call(geo, probs, own, halo, gmx, hm, sm)
    cls_part = class_attend_call(geo, own, halo, hr, hrf)
    class_bias = jnp.concatenate([rel_table[:, SPAN * SPAN], jnp.zeros((16 - heads,), F32)])
    class_bias = jnp.broadcast_to(class_bias[:, None], (16, geo.own))
    cls_low = class_grad_call(geo, own, halo, gmx, hr, hrf, sa, class_bias).astype(BF16)
    d_table = table_call(geo, rel_acc)
    dk, dv = key_grad_call(geo, own, halo, gmx, pieces, bias_b, ok, hm, sa, flank)
    dq, dk, dv = (a.reshape(count, width) for a in (dq, dk, dv))
    cls_rows = jnp.concatenate([cls_token, jnp.zeros((16 - pages, width), BF16)], axis=0)
    direct = (lax.axis_size("dp"), row_peers, col_peers) == (2, 4, 4)
    if direct:
        where = jnp.stack([row_at % 2, row_at // 2, col_at, page_at]).astype(jnp.int32)
    else:
        where = jnp.zeros((4,), jnp.int32)
    d_late, vg_qkv = qkv_weight_call(
        where, col_peers, x, dq, dk, dv, cls_rows, cls_low, vec, att, gb
    )
    half = 3 * width // 2
    wide = lambda a: a.astype(F32)
    if direct:
        mine = (wide(d_late[0]) + wide(swap(d_late[1], "row", 1))).astype(BF16)
        mine, dq = join((mine, dq))
        near_x = swap(mine[1, :col_peers], "dp", 1)
        near_y = swap(mine[0, col_peers:], "row", 2)
        far = lax.ppermute(
            mine[1, col_peers:],
            ("dp", "row"),
            [(4 * i + j, 4 * (i ^ 1) + (j ^ 2)) for i in range(2) for j in range(4)],
        )
    d_tok, d_cls, vg_tok = token_grad_call(x, dq, dk, dv, gres, w_qkv, cls_rows, cls_low, vec)
    slab = width // (row_peers * col_peers)
    if direct:
        near_x, near_y, far, d_cls, vg_tok, d_mlp = join((near_x, near_y, far, d_cls, vg_tok, d_mlp))
        late = (wide(mine[0, :col_peers]) + wide(near_x) + wide(near_y) + wide(far)).astype(BF16)
        beside = [swap(late[step], "col", step) for step in range(1, col_peers)]
        up, down = d_mlp[: ups * slab], d_mlp[ups * slab :]
        cut_up, cut_down = ups * slab // 2, width // 2

        def halves(place):
            return jnp.concatenate(
                [
                    lax.dynamic_slice_in_dim(up, place * cut_up, cut_up, 0),
                    lax.dynamic_slice_in_dim(down, place * cut_down, cut_down, 1).reshape(
                        -1, width
                    ),
                ],
                axis=0,
            )

        other = swap(halves(1 - page_at), "dp", 1)

    table_rows = jnp.pad(d_table[:heads].reshape(-1), (0, 2 * width - heads * LANES))
    vectors = jnp.concatenate(
        [
            d_cls[:pages],
            vg_tok[0:3],
            vg_qkv[0:1, :width],
            vg_qkv[0:1, 2 * width : 3 * width],
            vg_mlp[0:6],
            d_upb[0].reshape(-1, width),
            table_rows.reshape(2, width),
        ],
        axis=0,
    )
    parts = cls_part
    mine, place = jnp.zeros((), jnp.int32), 1
    for axis in ("col", "row"):
        bit = lax.axis_size(axis) // 2
        while bit:
            both = swap(jnp.concatenate([parts, vectors], axis=0), axis, bit)
            vectors = vectors + both[parts.shape[0] :]
            parts = jnp.concatenate([parts, both[: parts.shape[0]]], axis=0)
            mine = mine + place * (lax.axis_index(axis) // bit % 2).astype(jnp.int32)
            place, bit = 2 * place, bit // 2
    d_cls, v = vectors[:pages], vectors[pages:]
    bit = 1
    while bit < lax.axis_size("dp"):
        v, bit = v + swap(v, "dp", bit), 2 * bit
    out_cls = class_close_call(
        geo, mine[None], parts.reshape(-1, 16, width), halo, cls_rows, to_head, w_out, vec, w_up,
        w_down,
    )[:pages]

    half = 3 * width // 2
    if direct:
        beside, other, v, out_cls = join((beside, other, v, out_cls))
        late = wide(late[0])
        for part in beside:
            late = late + wide(part)
        d_qkv, d_wout = late[:, :half], late[:, half:]
        both = wide(halves(page_at)) + wide(other)
        d_up = jnp.transpose(both[:cut_up].reshape(-1, slab, width), (1, 0, 2)).reshape(slab, -1)
        d_down = both[cut_up:].reshape(-1, cut_down)
    else:
        d_late = jnp.transpose(
            d_late.reshape(2, 2, 2, col_peers, -1, 4 * width // 2), (2, 0, 3, 4, 1, 5)
        ).reshape(width, 2, 2 * width)
        d_qkv = spread_sum(d_late[:, :, :half].reshape(width, 2 * half))
        d_wout = spread_sum(d_late[:, :, half:].reshape(width, width))
        d_up = jnp.transpose(d_mlp[: ups * slab].reshape(ups, slab, width), (1, 0, 2))
        d_up = page_sum(d_up.reshape(slab, ups * width), 1).astype(F32)
        d_down = page_sum(d_mlp[ups * slab :], 1).astype(F32)

    d_rel = v[11 + ups :].reshape(-1)[: heads * LANES].reshape(heads, LANES)[:, : SPAN * SPAN + 1]
    return (
        out.reshape(tokens.shape),
        out_cls,
        d_tok.reshape(tokens.shape),
        d_cls,
        d_qkv,
        d_wout,
        d_up,
        d_down,
        v[0],
        v[1],
        v[2],
        v[3],
        v[4],
        d_rel,
        v[10],
        v[9],
        v[7],
        v[8],
        v[11 : 11 + ups].reshape(-1),
        v[6],
        v[5],
    )


def solution(mesh):
    tile = P("dp", "row", "col", None)
    flat = P("dp", "row", "col")
    weights = P(("row", "col"), "dp")
    return jax.shard_map(
        shards,
        mesh=mesh,
        in_specs=(tile, P("dp", None), flat, flat) + (P(),) * 17 + (tile,),
        out_specs=(tile, P("dp", None), tile, P("dp", None)) + (weights,) * 4 + (P(),) * 13,
        check_vma=False,
    )
```

```python
import functools
import math

import jax
import jax.numpy as jnp
import numpy as np
from jax import lax
from jax.experimental import pallas as pl
from jax.experimental.pallas import tpu as pltpu
from jax.sharding import PartitionSpec as P

F32 = jnp.float32
BF16 = jnp.bfloat16
NEG = -1e30
REACH = 3
SPAN = 7
BAND = 4
SIDE = 8
LANES = 128
FLAG = 1024.0
ROOM, LESS = 56, 28
EPS = 1e-06
MIB = 1 << 20


def dot(a, b):
    return jnp.dot(a, b, preferred_element_type=F32)


def dot_t(a, b):
    return lax.dot_general(a, b, (((1,), (1,)), ((), ())), preferred_element_type=F32)


def dot_0(a, b):
    return lax.dot_general(a, b, (((0,), (0,)), ((), ())), preferred_element_type=F32)


def split3(x):
    hi = x.astype(BF16)
    rest = x - hi.astype(F32)
    mid = rest.astype(BF16)
    low = (rest - mid.astype(F32)).astype(BF16)
    return hi, mid, low


def norm_parts(x):
    c = x - jnp.mean(x, axis=-1, keepdims=True)
    inv = lax.rsqrt(jnp.mean(c * c, axis=-1, keepdims=True) + EPS)
    return c * inv, inv


def norm_pull(e, unit, inv):
    return inv * (
        e
        - jnp.mean(e, axis=-1, keepdims=True)
        - unit * jnp.mean(e * unit, axis=-1, keepdims=True)
    )


def unmask(x, emb):
    return jnp.where(x > FLAG / 2, emb, x)


class Geometry:
    def __init__(self, pages, rows, cols, width, heads):
        self.pages, self.rows, self.cols = pages, rows, cols
        self.width, self.heads = width, heads
        self.head = width // heads
        self.lanes = 256
        self.stack = self.lanes // self.head
        self.groups = width // self.lanes
        self.own = rows * cols
        self.edge = REACH * cols
        self.side = (rows + 2 * REACH) * SIDE
        self.halo = 2 * self.edge + self.side + 16
        self.bands = rows // BAND
        self.band = BAND * cols
        self.main = (BAND + 2 * REACH) * cols
        self.flank = (BAND + 2 * REACH) * SIDE
        self.slots = self.main + self.flank + 16
        self.cls_at = self.main + self.flank
        slot = np.arange(self.slots)
        r = np.where(slot < self.main, slot // cols, (slot - self.main) // SIDE)
        s = (slot - self.main) % SIDE
        c = np.where(
            slot < self.main,
            slot % cols,
            np.where(s < REACH, s - REACH, np.where(s < 2 * REACH, cols + s - REACH, -1000)),
        )
        is_cls = slot >= self.cls_at
        r = np.where(is_cls, -1000, r)
        c = np.where(is_cls, -1000, c)
        self.slot_row, self.slot_col = r, c
        q = np.arange(self.band)
        a = r[None, :] - (q // cols)[:, None]
        b = c[None, :] - (q % cols)[:, None] + REACH
        ok = (a >= 0) & (a < SPAN) & (b >= 0) & (b < SPAN)
        offset = np.where(ok, a * SPAN + b, -1)
        mirror = np.where(ok, SPAN * SPAN - 1 - offset, -1)
        offset[:, self.cls_at] = SPAN * SPAN
        self.offset = offset.astype(np.int32)
        self.mirror = mirror.astype(np.int32)
        fold = np.full((cols, self.slots), -1, np.int32)
        for i in range(cols):
            for lane in range(SPAN * cols):
                d = lane % cols - i + REACH
                if 0 <= d < SPAN:
                    fold[i, lane] = lane // cols * SPAN + d
            for lane in range(SPAN * SIDE):
                s1 = lane % SIDE
                if s1 < 2 * REACH:
                    col = s1 - REACH if s1 < REACH else cols + s1 - REACH
                    d = col - i + REACH
                    if 0 <= d < SPAN:
                        fold[i, self.main + lane] = lane // SIDE * SPAN + d
            fold[i, self.cls_at] = SPAN * SPAN
        self.fold = fold.T.copy()
        lane = np.arange(self.lanes) // self.head
        self.head_mask = (np.arange(16)[:, None] == lane[None, :]).astype(np.float32)
        stat = np.zeros((self.groups, 8, LANES), np.float32)
        every = np.zeros((32, LANES), np.float32)
        for h in range(heads):
            g, k = divmod(h, self.stack)
            for part in range(3):
                stat[g, k, 48 + 16 * part + h] = -1.0
                every[h, 16 * part + h] = -1.0
                every[16 + h, 48 + 16 * part + h] = -1.0
        self.stat_mask = stat
        self.stat_all = every
        self.to_head = (np.arange(width)[:, None] // self.head == np.arange(LANES)[None, :]).astype(
            np.float32
        )
        self.head_rows = self.to_head.T[:16].copy()
        base = np.full((2, cols, self.slots), -1, np.int32)
        for i in range(cols):
            for lane in range(self.slots):
                o = fold[i, lane]
                base[0, i, lane] = o
                base[1, i, lane] = SPAN * SPAN - 1 - o if 0 <= o < SPAN * SPAN else -1
        self.base = base
        tall = rows + 2 * REACH
        self.strip = -(-REACH * tall // 8) * 8
        flank = np.zeros((2, self.side, self.strip), np.float32)
        for r in range(tall):
            for i in range(REACH):
                flank[0, r * SIDE + i, r * REACH + i] = 1.0
                flank[1, r * SIDE + REACH + i, r * REACH + i] = 1.0
        self.flank_of = flank

    def block(self, own, halo, b):
        lo, hi = b * self.band, b * self.band + self.main
        e, o = self.edge, self.own
        parts = []
        if lo < e:
            parts.append(halo[lo : min(hi, e)])
        parts.append(own[max(lo - e, 0) : min(hi - e, o)])
        if hi > e + o:
            parts.append(halo[e + max(lo - e - o, 0) : e + hi - e - o])
        at = 2 * e + b * BAND * SIDE
        parts.append(halo[at : at + self.flank])
        parts.append(halo[2 * e + self.side : 2 * e + self.side + 16])
        return jnp.concatenate(parts, axis=0)

    def around(self, top, bottom, left, right, flank, last):
        side = dot(flank[0], left) + dot(flank[1], right)
        return jnp.concatenate([top, bottom, side.astype(BF16), last], axis=0)

    def stacked(self, x, mask):
        return jnp.concatenate([x * mask[h : h + 1] for h in range(self.stack)], axis=0)

    def unstacked(self, r):
        rows = r.shape[0] // self.stack
        lane = lax.broadcasted_iota(jnp.int32, (rows, self.lanes), 1) // self.head
        out = r[(self.stack - 1) * rows :]
        for h in range(self.stack - 1):
            out = jnp.where(lane == h, r[h * rows : (h + 1) * rows], out)
        return out


def full(shape):
    return pl.BlockSpec(shape, lambda *_: (0,) * len(shape))


def hold(shape):
    return pl.BlockSpec(shape, lambda *_: (0,) * len(shape), pipeline_mode=pl.Buffered(1))


def params(limit, sem=1):
    return pltpu.CompilerParams(
        dimension_semantics=("arbitrary",) * sem, vmem_limit_bytes=limit * MIB
    )


def bias_body(geo, table, index_ref, out_ref):
    lane = lax.broadcasted_iota(jnp.int32, (geo.cols, geo.slots), 1)
    low = jnp.full((geo.cols, geo.slots), NEG, F32)
    index = index_ref[...]
    pair = 2

    def head(i, carry):
        acc = [low] * (2 * pair)
        for o in range(SPAN * SPAN + 1):
            hit = index == o
            for j in range(pair):
                at = 2 * j + o % 2
                acc[at] = jnp.where(hit, table[i * pair + j, o], acc[at])
        for j in range(pair):
            both = jnp.maximum(acc[2 * j], acc[2 * j + 1])
            main = jnp.where(lane < geo.main, both, low)
            side = jnp.where((lane >= geo.main) & (lane < geo.cls_at), both, low)
            last = jnp.where(lane >= geo.cls_at, both, low)
            h = i * pair + j
            for r in range(BAND):
                if r:
                    both = jnp.maximum(
                        pltpu.roll(main, r * geo.cols, 1), pltpu.roll(side, r * SIDE, 1)
                    )
                else:
                    both = jnp.maximum(main, side)
                at = pl.multiple_of(h % geo.stack * geo.band + r * geo.cols, 8)
                out_ref[h // geo.stack, pl.ds(at, geo.cols), :] = jnp.maximum(both, last)
        return carry

    lax.fori_loop(0, geo.heads // pair, head, 0)


def bias_table(geo, rel_table, which):
    return pl.pallas_call(
        functools.partial(bias_body, geo),
        out_shape=jax.ShapeDtypeStruct((geo.groups, geo.stack * geo.band, geo.slots), F32),
        in_specs=[
            pl.BlockSpec(memory_space=pltpu.SMEM),
            pl.BlockSpec(memory_space=pltpu.VMEM),
        ],
        out_specs=pl.BlockSpec(memory_space=pltpu.VMEM),
        compiler_params=pltpu.CompilerParams(vmem_limit_bytes=ROOM * MIB),
        name="bias_table",
    )(rel_table, jnp.asarray(geo.base[which]))


def qkv_rows(pages, w_ref, vec_ref, o_ref):
    d = pages[0].shape[1]

    def normed(raw):
        unit, _ = norm_parts(unmask(raw.astype(F32), vec_ref[0:1]))
        return (unit * vec_ref[1:2] + vec_ref[2:3]).astype(BF16)

    now = normed(pages[0])
    for k in range(len(pages)):
        rows = dot(now, w_ref[...])
        if k + 1 < len(pages):
            now = normed(pages[k + 1])
        for i in range(3):
            cols = slice(i * d, (i + 1) * d)
            o_ref[k, :, cols] = (rows[:, cols] + vec_ref[9 + i : 10 + i]).astype(BF16)


def qkv_own_body(x_ref, w_ref, vec_ref, o_ref):
    span = x_ref.shape[0]
    qkv_rows([x_ref[k] for k in range(span)], w_ref, vec_ref, o_ref)


def qkv_halo_body(geo, top_ref, bottom_ref, left_ref, right_ref, last_ref, flank_ref, w_ref, vec_ref, o_ref):
    span = top_ref.shape[0]
    raw = [
        geo.around(
            top_ref[k], bottom_ref[k], left_ref[k], right_ref[k], flank_ref[...], last_ref[k]
        )
        for k in range(span)
    ]
    qkv_rows(raw, w_ref, vec_ref, o_ref)


def by_page(a, span=1):
    return pl.BlockSpec((span,) + a.shape[1:], lambda p: (p,) + (0,) * (len(a.shape) - 1))


def qkv_call(body, rows, paged, whole, name):
    pages, _, d = paged[0].shape
    span = 2 if pages % 2 == 0 else 1
    n = pages * rows
    return pl.pallas_call(
        body,
        out_shape=jax.ShapeDtypeStruct((pages, rows, 3 * d), BF16),
        grid=(pages // span,),
        in_specs=[by_page(a, span) for a in paged] + [hold(a.shape) for a in whole],
        out_specs=pl.BlockSpec((span, rows, 3 * d), lambda p: (p, 0, 0)),
        compiler_params=params(ROOM),
        cost_estimate=pl.CostEstimate(
            flops=6 * n * d * d, transcendentals=n, bytes_accessed=2 * (4 * n * d + 3 * d * d)
        ),
        name=name,
    )(*paged, *whole)


def strips_body(geo, x_ref, top_ref, bottom_ref, right_ref, left_ref, tall, near):
    e, o = geo.edge, geo.own
    near[...] = jnp.zeros_like(near)

    def page(p, carry):
        tall[0:e, :] = top_ref[p].astype(F32)
        tall[e : e + o, :] = x_ref[p].astype(F32)
        tall[e + o :, :] = bottom_ref[p].astype(F32)
        for r in range(geo.rows + 2 * REACH):
            to, at = r * REACH, r * geo.cols
            near[0, to : to + REACH, :] = tall[at + geo.cols - REACH : at + geo.cols, :]
            near[1, to : to + REACH, :] = tall[at : at + REACH, :]
        right_ref[p] = near[0].astype(BF16)
        left_ref[p] = near[1].astype(BF16)
        return carry

    lax.fori_loop(0, geo.pages, page, 0)


def strips_call(geo, x, top, bottom):
    width = x.shape[2]
    shape = jax.ShapeDtypeStruct((geo.pages, geo.strip, width), BF16)
    return pl.pallas_call(
        functools.partial(strips_body, geo),
        out_shape=(shape, shape),
        scratch_shapes=[
            pltpu.VMEM((2 * geo.edge + geo.own, width), F32),
            pltpu.VMEM((2, geo.strip, width), F32),
        ],
        compiler_params=pltpu.CompilerParams(vmem_limit_bytes=ROOM * MIB),
        name="strips",
    )(x, top, bottom)


def class_part(geo, own_ref, halo_ref, hr_ref, hrf_ref, o_ref):
    page, d, at = pl.program_id(0), geo.width, geo.halo - 16

    @pl.when(page == 0)
    def _():
        o_ref[...] = jnp.zeros_like(o_ref)

    scale = BF16(1.0 / math.sqrt(geo.head))
    hr, hrf = hr_ref[...], hrf_ref[...]
    qc = jnp.broadcast_to(halo_ref[0, at : at + 1, 0:d] * scale, (16, d)) * hr
    s = dot_t(qc, own_ref[0, :, d : 2 * d])
    top = jnp.max(s, axis=-1, keepdims=True)
    e = jnp.exp(s - top)
    total = jnp.sum(e, axis=-1, keepdims=True)
    acc = dot(jnp.concatenate(split3(e), axis=0), own_ref[0, :, 2 * d : 3 * d])
    acc = acc[0:16] + acc[16:32] + acc[32:48]
    o_ref[pl.ds(page, 1), :] = jnp.sum(acc * hrf, axis=0, keepdims=True)
    row = lax.broadcasted_iota(jnp.int32, (16, LANES), 0)
    diag = row == lax.broadcasted_iota(jnp.int32, (16, LANES), 1)
    stats = [jnp.sum(jnp.where(diag, a, 0.0), axis=0, keepdims=True) for a in (top, total)]
    stats.append(jnp.zeros((1, d - 2 * LANES), F32))
    o_ref[pl.ds(geo.pages + page, 1), :] = jnp.concatenate(stats, axis=1)


def attend_body(
    geo, own_ref, halo_ref, bias_ref, ok_ref, hm_ref, hr_ref, hrf_ref, o_ref, lse_ref, p_ref, c_ref
):
    scale = BF16(1.0 / math.sqrt(geo.head))
    hm = hm_ref[...]
    lane = lax.broadcasted_iota(jnp.int32, (geo.band, LANES), 1)
    bands = range(geo.bands)
    at = [slice(b * geo.band, (b + 1) * geo.band) for b in bands]
    lses = [jnp.zeros((geo.band, LANES), F32) for _ in bands]

    def part(ref, which, g):
        lo = which * geo.width + g * geo.lanes
        return ref[0, :, lo : lo + geo.lanes]

    def score(g):
        q, k, hk = part(own_ref, 0, g), part(own_ref, 1, g), part(halo_ref, 1, g)
        return [
            dot_t(geo.stacked(q[at[b]] * scale, hm), geo.block(k, hk, b))
            + bias_ref[g]
            + ok_ref[b : b + 1]
            for b in bands
        ]

    def soften(g, scores):
        probs = []
        for b in bands:
            top = jnp.max(scores[b], axis=-1, keepdims=True)
            e = jnp.exp(scores[b] - top)
            total = jnp.sum(e, axis=-1, keepdims=True)
            lse = top + jnp.log(total)
            for h in range(geo.stack):
                rows = slice(h * geo.band, (h + 1) * geo.band)
                lses[b] = jnp.where(lane == g * geo.stack + h, lse[rows], lses[b])
            p = (e * (1.0 / total)).astype(BF16)
            p_ref[0, g, b] = p
            probs.append(p)
        return probs

    def mix(g, probs):
        v, hv = part(own_ref, 2, g), part(halo_ref, 2, g)
        for b in bands:
            rows = geo.unstacked(dot(probs[b], geo.block(v, hv, b)))
            o_ref[0, at[b], g * geo.lanes : (g + 1) * geo.lanes] = rows.astype(BF16)

    class_part(geo, own_ref, halo_ref, hr_ref, hrf_ref, c_ref)
    scores = score(0)
    for g in range(geo.groups):
        probs = soften(g, scores)
        if g + 1 < geo.groups:
            scores = score(g + 1)
        mix(g, probs)
    for b in bands:
        lse_ref[0, at[b], :] = lses[b]


def attend_call(geo, own, halo, bias, ok, hm, hr, hrf):
    G = geo.groups
    mm = 2 * geo.pages * G * geo.bands * 256 * 256 * 256
    outs = (
        jax.ShapeDtypeStruct((geo.pages, geo.own, geo.width), BF16),
        jax.ShapeDtypeStruct((geo.pages, geo.own, LANES), F32),
        jax.ShapeDtypeStruct((geo.pages, G, geo.bands, geo.lanes, geo.slots), BF16),
        jax.ShapeDtypeStruct((2 * geo.pages, geo.width), F32),
    )
    return pl.pallas_call(
        functools.partial(attend_body, geo),
        out_shape=outs,
        grid=(geo.pages,),
        in_specs=[by_page(own), by_page(halo)] + [hold(a.shape) for a in (bias, ok, hm, hr, hrf)],
        out_specs=[by_page(a) for a in outs[:3]] + [hold((2 * geo.pages, geo.width))],
        compiler_params=params(ROOM),
        cost_estimate=pl.CostEstimate(
            flops=2 * mm, transcendentals=geo.pages * G * geo.bands * 65536, bytes_accessed=16 * MIB
        ),
        name="attend",
    )(own, halo, bias, ok, hm, hr, hrf)


def mlp_body(
    tile, steps, att_ref, x_ref, og_ref, lse_ref, wout_ref, vec_ref, toh_ref, wup_ref, wdn_ref,
    out_ref, gmx_ref, gres_ref, gb_ref, dw_ref, vg_ref, dub_ref,
    n2, n2t, gm, res, branch, mlp, gn, act, dh, up_buf, dn_buf, out_buf, gmx_buf, gres_buf, gb_buf,
    sems, out_sems,
):
    step = pl.program_id(0)
    n, d = n2.shape
    row = lambda i: vec_ref[i : i + 1]
    tiles, few, rows_dn = n // tile, dn_buf.shape[0], dn_buf.shape[1]
    rows_up = up_buf.shape[1]
    span = lambda t: pl.ds(pl.multiple_of(t * tile, tile), tile)

    @pl.when(step == 0)
    def _():
        def one(t, carry):
            rows = span(t)
            x = unmask(x_ref[rows, :].astype(F32), row(0))
            br = dot(att_ref[rows, :], wout_ref[...]) + row(3)
            r = x + row(4) * br
            branch[rows, :] = br
            res[rows, :] = r
            unit, _ = norm_parts(r)
            n2[rows, :] = (unit * row(5) + row(6)).astype(BF16)
            gm[rows, :] = (row(8) * og_ref[rows, :].astype(F32)).astype(BF16)
            mlp[rows, :] = jnp.zeros((tile, d), F32)
            gn[rows, :] = jnp.zeros((tile, d), F32)
            return carry

        lax.fori_loop(0, tiles, one, 0)
        n2t[...] = n2[...].T
        vg_ref[...] = jnp.zeros_like(vg_ref)

    wup, wdn = wup_ref[...], wdn_ref[...]
    upb = vec_ref[pl.ds(12 + step, 1), :]
    dub_ref[...] = jnp.zeros_like(dub_ref)

    def one(t, carry):
        rows = pl.ds(pl.multiple_of(t * 2 * tile, 2 * tile), 2 * tile)
        h = dot(n2[rows, :], wup) + upb
        da = dot_t(gm[rows, :], wdn)
        cdf = 0.5 * (1.0 + lax.erf(h * math.sqrt(0.5)))
        pdf = jnp.exp(-0.5 * h * h) * (1.0 / math.sqrt(2.0 * math.pi))
        a = (h * cdf).astype(BF16)
        g = (da * (cdf + h * pdf)).astype(BF16)
        act[rows, :] = a
        dh[rows, :] = g
        mlp[rows, :] += dot(a, wdn)
        gn[rows, :] += dot_t(g, wup)
        dub_ref[0:1] += jnp.sum(g.astype(F32), axis=0, keepdims=True)
        return carry

    lax.fori_loop(0, tiles // 2, one, 0)

    def copies(c):
        at = pl.multiple_of(c * rows_up, 8)
        return (
            pltpu.make_async_copy(up_buf, dw_ref.at[:, pl.ds(at, rows_up), :], sems.at[0]),
            pltpu.make_async_copy(
                dn_buf,
                dw_ref.at[pl.ds(c * few, few), steps * rows_up : steps * rows_up + rows_dn, :],
                sems.at[1],
            ),
        )

    @pl.when(step > 0)
    def _():
        for copy in copies(step - 1):
            copy.wait()

    up_buf[...] = dot(n2t[...], dh[...]).astype(BF16).reshape(up_buf.shape)
    dn_buf[...] = dot_0(act[...], gm[...]).astype(BF16).reshape(dn_buf.shape)
    for copy in copies(step):
        copy.start()

    @pl.when(step == steps - 1)
    def _():
        outs = ((out_buf, out_ref), (gmx_buf, gmx_ref), (gres_buf, gres_ref), (gb_buf, gb_ref))

        def sends(t, slot):
            return [
                pltpu.make_async_copy(buf.at[slot], ref.at[span(t), :], out_sems.at[slot, i])
                for i, (buf, ref) in enumerate(outs)
            ]

        def add(i, v):
            vg_ref[i : i + 1] += jnp.sum(v, axis=0, keepdims=True)

        def one(t, carry):
            rows, slot = span(t), lax.rem(t, 2)

            @pl.when(t >= 2)
            def _():
                for copy in sends(t - 2, slot):
                    copy.wait()

            r, br, att = res[rows, :], branch[rows, :], att_ref[rows, :]
            og = og_ref[rows, :].astype(F32)
            mo = mlp[rows, :] + row(7)
            out_buf[slot] = (r + row(8) * mo).astype(BF16)
            add(0, og * mo)
            add(1, gm[rows, :].astype(F32))
            unit, inv = norm_parts(r)
            grad = gn[rows, :]
            add(2, grad * unit)
            add(3, grad)
            gr = og + norm_pull(grad * row(5), unit, inv)
            gres_buf[slot] = gr
            add(4, gr * br)
            gb = (row(4) * gr).astype(BF16)
            add(5, gb.astype(F32))
            gb_buf[slot] = gb
            mix = dot_t(gb, wout_ref[...]).astype(BF16)
            prod = mix.astype(F32) * att.astype(F32)
            delta = sum(dot(part, toh_ref[...]) for part in split3(prod))
            packed = jnp.zeros(delta.shape, F32)
            for i, part in enumerate(split3(lse_ref[rows, :]) + split3(delta)):
                part = part.astype(F32)
                packed += part if i == 0 else pltpu.roll(part, 16 * i, 1)
            gmx_buf[slot, :, 0:d] = mix
            gmx_buf[slot, :, d : d + LANES] = packed.astype(BF16)
            for copy in sends(t, slot):
                copy.start()
            return carry

        lax.fori_loop(0, tiles, one, 0)
        for t in (tiles - 2, tiles - 1):
            for copy in sends(t, t % 2):
                copy.wait()
        for copy in copies(step):
            copy.wait()


def mlp_call(att, x, og, lse, w_out, vec, to_head, w_up, w_down, dests, tile=256):
    n, d = x.shape
    ff = w_up.shape[1]
    steps = ff // d
    rows_up, rows_dn = d // dests, ff // dests
    anywhere = pl.BlockSpec(memory_space=pl.ANY)
    return pl.pallas_call(
        functools.partial(mlp_body, tile, steps),
        out_shape=(
            jax.ShapeDtypeStruct((n, d), BF16),
            jax.ShapeDtypeStruct((n, d + LANES), BF16),
            jax.ShapeDtypeStruct((n, d), F32),
            jax.ShapeDtypeStruct((n, d), BF16),
            jax.ShapeDtypeStruct((dests, steps * rows_up + rows_dn, d), BF16),
            jax.ShapeDtypeStruct((8, d), F32),
            jax.ShapeDtypeStruct((8, ff), F32),
        ),
        grid=(steps,),
        in_specs=[hold(a.shape) for a in (att, x, og, lse, w_out, vec, to_head)]
        + [pl.BlockSpec((d, d), lambda c: (0, c)), pl.BlockSpec((d, d), lambda c: (c, 0))],
        out_specs=[anywhere] * 5 + [hold((8, d)), pl.BlockSpec((8, d), lambda c: (0, c))],
        scratch_shapes=[
            pltpu.VMEM((n, d), BF16),
            pltpu.VMEM((d, n), BF16),
            pltpu.VMEM((n, d), BF16),
            pltpu.VMEM((n, d), F32),
            pltpu.VMEM((n, d), F32),
            pltpu.VMEM((n, d), F32),
            pltpu.VMEM((n, d), F32),
            pltpu.VMEM((n, d), BF16),
            pltpu.VMEM((n, d), BF16),
            pltpu.VMEM((dests, rows_up, d), BF16),
            pltpu.VMEM((dests // steps, rows_dn, d), BF16),
            pltpu.VMEM((2, tile, d), BF16),
            pltpu.VMEM((2, tile, d + LANES), BF16),
            pltpu.VMEM((2, tile, d), F32),
            pltpu.VMEM((2, tile, d), BF16),
            pltpu.SemaphoreType.DMA((2,)),
            pltpu.SemaphoreType.DMA((2, 4)),
        ],
        compiler_params=params(ROOM),
        cost_estimate=pl.CostEstimate(
            flops=2 * n * d * (6 * ff + 2 * d),
            transcendentals=2 * n * ff,
            bytes_accessed=2 * (4 * d * ff + 8 * n * d),
        ),
        name="mlp",
    )(att, x, og, lse, w_out, vec, to_head, w_up, w_down)


def table_sums(geo, acc_ref, fold_ref, o_ref):
    lane = lax.broadcasted_iota(jnp.int32, (geo.cols, geo.slots), 1)
    heads = []
    for g in range(geo.groups):
        for h in range(geo.stack):
            x = acc_ref[g, h * geo.band : (h + 1) * geo.band, :]
            parts = [x[i * geo.cols : (i + 1) * geo.cols] for i in range(BAND)]
            main, side, plain = parts[0], parts[0], parts[0]
            for i in range(1, BAND):
                main = main + pltpu.roll(parts[i], geo.slots - i * geo.cols, 1)
                side = side + pltpu.roll(parts[i], geo.slots - i * SIDE, 1)
                plain = plain + parts[i]
            z = jnp.where(lane < SPAN * geo.cols, main, jnp.where(lane < geo.cls_at, side, plain))
            heads.append(z)
    pad = [jnp.zeros((geo.cols, geo.slots), F32)] * (16 - geo.heads)
    z = jnp.stack(heads + pad, axis=0)
    total = jnp.zeros((16, LANES), F32)
    which = lax.broadcasted_iota(jnp.int32, (geo.slots, LANES), 1)
    for i in range(geo.cols):
        pick = jnp.where(fold_ref[:, i : i + 1] == which, 1.0, 0.0).astype(BF16)
        for part in split3(z[:, i, :]):
            total += dot(part, pick)
    o_ref[...] = total


def query_grad_body(
    geo, p_ref, own_ref, halo_ref, gm_ref, hm_ref, sm_ref, fold_ref, dq_ref, table_ref, rel_ref
):
    scale = 1.0 / math.sqrt(geo.head)
    hm = hm_ref[...]
    bands = range(geo.bands)
    at = [slice(b * geo.band, (b + 1) * geo.band) for b in bands]
    ones = jnp.ones((geo.slots, LANES), BF16)
    join = lambda a, b: jnp.concatenate([a, b], axis=1)
    st = gm_ref[0, :, geo.width :]

    @pl.when(pl.program_id(0) == 0)
    def _():
        rel_ref[...] = jnp.zeros_like(rel_ref)

    def part(ref, which, g):
        lo = which * geo.width + g * geo.lanes
        return ref[0, :, lo : lo + geo.lanes]

    def pull(g):
        gm, v, hv = part(gm_ref, 0, g), part(own_ref, 2, g), part(halo_ref, 2, g)
        sm = sm_ref[g]
        return [
            dot_t(
                join(geo.stacked(gm[at[b]], hm), geo.stacked(st[at[b]], sm)),
                join(geo.block(v, hv, b), ones),
            )
            for b in bands
        ]

    dp = pull(0)
    for g in range(geo.groups):
        ds = [p_ref[0, g, b].astype(F32) * dp[b] for b in bands]
        if g + 1 < geo.groups:
            dp = pull(g + 1)
        total = ds[0]
        for d in ds[1:]:
            total = total + d
        rel_ref[g] += total
        k, hk = part(own_ref, 1, g), part(halo_ref, 1, g)
        for b in bands:
            rows = geo.unstacked(dot((ds[b] * scale).astype(BF16), geo.block(k, hk, b)))
            dq_ref[0, at[b], g * geo.lanes : (g + 1) * geo.lanes] = rows.astype(BF16)

    @pl.when(pl.program_id(0) == geo.pages - 1)
    def _():
        table_sums(geo, rel_ref, fold_ref, table_ref)


def query_grad_call(geo, probs, own, halo, gmx, hm, sm):
    G = geo.groups
    mm = 2 * geo.pages * G * geo.bands * 256 * 256 * 256
    dq = jax.ShapeDtypeStruct((geo.pages, geo.own, geo.width), BF16)
    table = jax.ShapeDtypeStruct((16, LANES), F32)
    fold = jnp.asarray(geo.fold)
    return pl.pallas_call(
        functools.partial(query_grad_body, geo),
        out_shape=(dq, table),
        grid=(geo.pages,),
        in_specs=[by_page(a) for a in (probs, own, halo, gmx)]
        + [hold(a.shape) for a in (hm, sm, fold)],
        out_specs=[by_page(dq), hold(table.shape)],
        scratch_shapes=[pltpu.VMEM((geo.groups, geo.stack * geo.band, geo.slots), F32)],
        compiler_params=params(ROOM),
        cost_estimate=pl.CostEstimate(
            flops=2 * mm, transcendentals=0, bytes_accessed=20 * MIB
        ),
        name="query_grad",
    )(probs, own, halo, gmx, hm, sm, fold)


def class_grad(geo, own_ref, halo_ref, gm_ref, hr_ref, hrf_ref, sa_ref, cb_ref, o_ref, acc):
    page, d, at = pl.program_id(0), geo.width, geo.halo - 16

    @pl.when(page == 0)
    def _():
        acc[...] = jnp.zeros_like(acc)

    scale = 1.0 / math.sqrt(geo.head)
    hr, hrf, sa = hr_ref[...], hrf_ref[...], sa_ref[...]
    q, gm, st = own_ref[0, :, 0:d], gm_ref[0, :, 0:d], gm_ref[0, :, d:]
    kc = jnp.broadcast_to(halo_ref[0, at : at + 1, d : 2 * d] * BF16(scale), (16, d)) * hr
    vc = jnp.broadcast_to(halo_ref[0, at : at + 1, 2 * d : 3 * d], (16, d)) * hr
    prob = jnp.exp(dot_t(kc, q) + dot_t(sa[0:16], st) + cb_ref[...])
    ds = prob * (dot_t(vc, gm) + dot_t(sa[16:32], st))
    row = pl.ds(page, 1)
    dk = dot((ds * scale).astype(BF16), q)
    dv = dot(prob.astype(BF16), gm)
    acc[row, 0:d] = jnp.sum(dk * hrf, axis=0, keepdims=True)
    acc[row, d : 2 * d] = jnp.sum(dv * hrf, axis=0, keepdims=True)

    @pl.when(page == geo.pages - 1)
    def _():
        o_ref[...] = acc[...].astype(BF16)


def key_grad_body(
    geo, own_ref, halo_ref, gm_ref, top_ref, bottom_ref, left_ref, right_ref,
    bias_ref, ok_ref, hm_ref, sa_ref, flank_ref, hr_ref, hrf_ref, cb_ref, dk_ref, dv_ref, c_ref,
    hgm, rowstat, acc,
):
    scale = 1.0 / math.sqrt(geo.head)
    hm = hm_ref[...]
    bands = range(geo.bands)
    at = [slice(b * geo.band, (b + 1) * geo.band) for b in bands]
    last = jnp.zeros((16, gm_ref.shape[2]), BF16)
    hgm[...] = geo.around(
        top_ref[0], bottom_ref[0], left_ref[0], right_ref[0], flank_ref[...], last
    )
    stats, own = hgm[:, geo.width :], gm_ref[0, :, geo.width :]
    row = lax.broadcasted_iota(jnp.int32, (32, geo.slots), 0)
    for b in bands:
        r = dot_t(sa_ref[...], geo.block(own, stats, b))
        rowstat[b] = r + jnp.where(row < 16, ok_ref[b : b + 1], 0.0)

    def part(ref, which, g):
        lo = which * geo.width + g * geo.lanes
        return ref[0, :, lo : lo + geo.lanes]

    def spread(g, b, first):
        at = first + g * geo.stack
        return jnp.concatenate(
            [
                jnp.broadcast_to(rowstat[b, at + h : at + h + 1, :], (geo.band, geo.slots))
                for h in range(geo.stack)
            ],
            axis=0,
        )

    def first(g):
        q, k, v = (part(own_ref, i, g) for i in range(3))
        hq, gm = part(halo_ref, 0, g), part(gm_ref, 0, g)
        hg = hgm[:, g * geo.lanes : (g + 1) * geo.lanes]
        qb = [geo.block(q, hq, b) for b in bands]
        gb = [geo.block(gm, hg, b) for b in bands]
        s = [dot_t(geo.stacked(k[at[b]] * BF16(scale), hm), qb[b]) for b in bands]
        dp = [dot_t(geo.stacked(v[at[b]], hm), gb[b]) for b in bands]
        return qb, gb, s, dp

    class_grad(geo, own_ref, halo_ref, gm_ref, hr_ref, hrf_ref, sa_ref, cb_ref, c_ref, acc)
    now = first(0)
    for g in range(geo.groups):
        qb, gb, s, dp = now
        p = [jnp.exp(s[b] + bias_ref[g] + spread(g, b, 0)) for b in bands]
        ds = [(p[b] * (dp[b] + spread(g, b, 16)) * scale).astype(BF16) for b in bands]
        if g + 1 < geo.groups:
            now = first(g + 1)
        lanes = slice(g * geo.lanes, (g + 1) * geo.lanes)
        for b in bands:
            dv_ref[0, at[b], lanes] = geo.unstacked(dot(p[b].astype(BF16), gb[b])).astype(BF16)
            dk_ref[0, at[b], lanes] = geo.unstacked(dot(ds[b], qb[b])).astype(BF16)


def key_grad_call(geo, own, halo, gmx, pieces, *whole):
    G = geo.groups
    mm = 2 * geo.pages * G * geo.bands * 256 * 256 * 256
    out = jax.ShapeDtypeStruct((geo.pages, geo.own, geo.width), BF16)
    return pl.pallas_call(
        functools.partial(key_grad_body, geo),
        out_shape=(out, out, jax.ShapeDtypeStruct((16, 2 * geo.width), BF16)),
        grid=(geo.pages,),
        in_specs=[by_page(a) for a in (own, halo, gmx) + pieces]
        + [hold(a.shape) for a in whole],
        out_specs=[by_page(out)] * 2 + [hold((16, 2 * geo.width))],
        scratch_shapes=[
            pltpu.VMEM((geo.halo, geo.width + LANES), BF16),
            pltpu.VMEM((geo.bands, 32, geo.slots), F32),
            pltpu.VMEM((16, 2 * geo.width), F32),
        ],
        compiler_params=params(ROOM),
        cost_estimate=pl.CostEstimate(
            flops=4 * mm, transcendentals=geo.pages * G * geo.bands * 65536, bytes_accessed=20 * MIB
        ),
        name="key_grad",
    )(own, halo, gmx, *pieces, *whole)


def class_close_body(
    geo, mine_ref, parts_ref, cls_ref, x_ref, toh_ref, wout_ref, vec_ref, wup_ref, wdn_ref,
    out_ref, res, n2, acc,
):
    step = pl.program_id(0)
    d, pages = geo.width, geo.pages
    row = lambda i: vec_ref[i : i + 1]
    places = parts_ref.shape[0]

    @pl.when(step == 0)
    def _():
        mine = mine_ref[0]
        q = jnp.concatenate([cls_ref[p, 0:1, 0:d] for p in range(pages)], axis=0).astype(F32)
        k = jnp.concatenate([cls_ref[p, 0:1, d : 2 * d] for p in range(pages)], axis=0).astype(F32)
        v = jnp.concatenate([cls_ref[p, 0:1, 2 * d :] for p in range(pages)], axis=0).astype(F32)
        toh = toh_ref[...]
        own = sum(dot(part, toh) for part in split3(q * k)) * (1.0 / math.sqrt(geo.head))
        tops = [parts_ref[code ^ mine, pages:, 0:LANES] for code in range(places)]
        top = own
        for value in tops:
            top = jnp.maximum(top, value)
        weights = [jnp.exp(value - top) for value in tops] + [jnp.exp(own - top)]
        total = weights[-1]
        for code in range(places):
            total = total + weights[code] * parts_ref[code ^ mine, pages:, LANES : 2 * LANES]
        spread = jnp.concatenate([w / total for w in weights], axis=0)
        spread = sum(dot_t(part, toh) for part in split3(spread))
        mixed = spread[places * pages :] * v
        for code in range(places):
            rows = spread[code * pages : (code + 1) * pages]
            mixed = mixed + rows * parts_ref[code ^ mine, 0:pages, :]
        mixed = mixed.astype(BF16)
        mixed = jnp.concatenate([mixed, jnp.zeros((16 - pages, d), BF16)], axis=0)
        r = x_ref[...].astype(F32) + row(4) * (dot(mixed, wout_ref[...]) + row(3))
        res[...] = r
        unit, _ = norm_parts(r)
        n2[...] = (unit * row(5) + row(6)).astype(BF16)
        acc[...] = jnp.zeros_like(acc)

    h = dot(n2[...], wup_ref[...]) + vec_ref[pl.ds(12 + step, 1), :]
    a = (h * 0.5 * (1.0 + lax.erf(h * math.sqrt(0.5)))).astype(BF16)
    acc[...] += dot(a, wdn_ref[...])

    @pl.when(step == pl.num_programs(0) - 1)
    def _():
        out_ref[...] = (res[...] + row(8) * (acc[...] + row(7))).astype(BF16)


def class_close_call(geo, mine, parts, halo, x, to_head, w_out, vec, w_up, w_down):
    d = geo.width
    ff = w_up.shape[1]
    return pl.pallas_call(
        functools.partial(class_close_body, geo),
        out_shape=jax.ShapeDtypeStruct((16, d), BF16),
        grid=(ff // d,),
        in_specs=[pl.BlockSpec(memory_space=pltpu.SMEM)]
        + [
            full(parts.shape),
            pl.BlockSpec((geo.pages, 16, 3 * d), lambda c: (0, geo.halo // 16 - 1, 0)),
        ]
        + [full(a.shape) for a in (x, to_head, w_out, vec)]
        + [
            pl.BlockSpec((d, d), lambda c: (0, c)),
            pl.BlockSpec((d, d), lambda c: (c, 0)),
        ],
        out_specs=full((16, d)),
        scratch_shapes=[
            pltpu.VMEM((16, d), F32),
            pltpu.VMEM((16, d), BF16),
            pltpu.VMEM((16, d), F32),
        ],
        compiler_params=params(ROOM),
        cost_estimate=pl.CostEstimate(
            flops=64 * d * (2 * ff + d), transcendentals=16 * ff, bytes_accessed=12 * MIB
        ),
        name="class_close",
    )(mine, parts, halo, x, to_head, w_out, vec, w_up, w_down)


def by_place(dw, cols, core, half, column, keep_ref, send_ref):
    slab = dw.shape[0] // (4 * cols)
    for mine in range(2):

        @pl.when(core == mine)
        def _():
            for dest in range(4 * cols):
                y, b, c = dest // (2 * cols), dest // cols % 2, dest % cols
                place = (y ^ half) * cols + (c ^ column)
                ref = keep_ref if b == mine else send_ref
                ref[place] = dw[dest * slab : (dest + 1) * slab]


def early_weight_body(
    tile, cols, at_ref, x_ref, att_ref, dq_ref, gb_ref, vec_ref, keep_ref, send_ref, nt_ref, sum_ref,
    left, grad,
):
    step = pl.program_id(0)
    n, d = x_ref.shape

    @pl.when(step == 0)
    def _():
        def one(t, carry):
            rows = pl.ds(pl.multiple_of(t * tile, tile), tile)
            unit, _ = norm_parts(unmask(x_ref[rows, :].astype(F32), vec_ref[0:1]))
            grad[rows, :] = (unit * vec_ref[1:2] + vec_ref[2:3]).astype(BF16)
            return carry

        lax.fori_loop(0, n // tile, one, 0)
        left[...] = grad[...].T
        nt_ref[...] = left[...]
        grad[...] = dq_ref[...]
        total = jnp.sum(dq_ref[...].astype(F32), axis=0, keepdims=True)
        sum_ref[...] = jnp.broadcast_to(total, sum_ref.shape)

    @pl.when(step == 1)
    def _():
        left[...] = att_ref[...].T
        grad[...] = gb_ref[...]

    dw = dot(left[...], grad[...]).astype(BF16)
    by_place(dw, cols, at_ref[0], at_ref[1], at_ref[2], keep_ref, send_ref)


def late_weight_body(
    cols, at_ref, nt_ref, dk_ref, dv_ref, c_ref, cg_ref, vec_ref, keep_ref, send_ref, sum_ref, grad
):
    step = pl.program_id(0)
    extra = cg_ref[...]

    @pl.when(step == 0)
    def _():
        grad[...] = dk_ref[...]

    @pl.when(step == 1)
    def _():
        grad[...] = dv_ref[...]
        total = jnp.sum(dv_ref[...].astype(F32), axis=0, keepdims=True)
        total = total + jnp.sum(extra.astype(F32), axis=0, keepdims=True)
        sum_ref[...] = jnp.broadcast_to(total, sum_ref.shape)

    unit, _ = norm_parts(c_ref[...].astype(F32))
    left = (unit * vec_ref[1:2] + vec_ref[2:3]).astype(BF16)
    dw = (dot(nt_ref[...], grad[...]) + dot_0(left, extra)).astype(BF16)
    by_place(dw, cols, at_ref[0], at_ref[1], at_ref[2], keep_ref, send_ref)


def weight_call(body, where, cols, ins, in_specs, n, d, more, more_specs, scratch, name):
    slab = d // (4 * cols)
    out = jax.ShapeDtypeStruct((2 * cols, slab, 2 * d), BF16)
    block = pl.BlockSpec((2 * cols, slab, d), lambda i, p: (0, 0, i))
    return pl.pallas_call(
        body,
        out_shape=(out, out) + more,
        grid_spec=pltpu.PrefetchScalarGridSpec(
            num_scalar_prefetch=1,
            grid=(2,),
            in_specs=in_specs,
            out_specs=[block, block] + more_specs,
            scratch_shapes=scratch,
        ),
        compiler_params=params(ROOM),
        cost_estimate=pl.CostEstimate(
            flops=4 * n * d * d, transcendentals=n, bytes_accessed=2 * (5 * n * d + 2 * d * d)
        ),
        name=name,
    )(where, *ins)


def early_weight_call(where, cols, x, att, dq, gb, vec, tile=256):
    n, d = x.shape
    return weight_call(
        functools.partial(early_weight_body, tile, cols), where, cols, (x, att, dq, gb, vec),
        [hold(a.shape) for a in (x, att, dq, gb, vec)], n, d,
        (jax.ShapeDtypeStruct((d, n), BF16), jax.ShapeDtypeStruct((8, d), F32)),
        [hold((d, n)), hold((8, d))],
        [pltpu.VMEM((d, n), BF16), pltpu.VMEM((n, d), BF16)],
        "early_weight",
    )


def late_weight_call(where, cols, nt, dk, dv, cls_rows, cls_grad, vec):
    n, d = dk.shape
    ins = (nt, dk, dv, cls_rows)
    return weight_call(
        functools.partial(late_weight_body, cols), where, cols, ins + (cls_grad, vec),
        [hold(a.shape) for a in ins]
        + [pl.BlockSpec((16, d), lambda i, p: (0, i)), hold(vec.shape)],
        n, d, (jax.ShapeDtypeStruct((8, d), F32),), [hold((8, d))],
        [pltpu.VMEM((n, d), BF16)],
        "late_weight",
    )


def fold_body(cols, at_ref, k1_ref, r1_ref, k2_ref, r2_ref, own_ref, x_ref, y_ref, far_ref):
    d = k1_ref.shape[2] // 2
    add = lambda a, b, lo, hi: (a[:, :, lo:hi].astype(F32) + b[:, :, lo:hi].astype(F32)).astype(BF16)
    one = lambda lo, hi: add(k1_ref, r1_ref, lo, hi)
    two = lambda lo, hi: add(k2_ref, r2_ref, lo, hi)
    h = d // 2
    for page in range(2):

        @pl.when(at_ref[3] == page)
        def _():
            for near, far, half in ((own_ref, y_ref, page), (x_ref, far_ref, 1 - page)):
                if half == 0:
                    parts = ((one(0, d), 0), (two(0, h), d), (one(d, d + h), d + h))
                else:
                    parts = ((two(h, 2 * d), 0), (one(d + h, 2 * d), d + h))
                for value, lo in parts:
                    hi = lo + value.shape[2]
                    near[:, :, lo:hi] = value[:cols]
                    far[:, :, lo:hi] = value[cols:]


def fold_call(where, cols, keep1, got1, keep2, got2):
    _, slab, d2 = keep1.shape
    out = jax.ShapeDtypeStruct((cols, slab, d2), BF16)
    rows = slab // 3
    spec = lambda k: pl.BlockSpec((k, rows, d2), lambda i, p: (0, i, 0))
    return pl.pallas_call(
        functools.partial(fold_body, cols),
        out_shape=(out,) * 4,
        grid_spec=pltpu.PrefetchScalarGridSpec(
            num_scalar_prefetch=1,
            grid=(3,),
            in_specs=[spec(2 * cols)] * 4,
            out_specs=[spec(cols)] * 4,
        ),
        compiler_params=params(LESS),
        name="fold",
    )(where, keep1, got1, keep2, got2)


def token_grad_body(
    pages, heads, x_ref, dq_ref, dk_ref, dv_ref, gres_ref, w_ref, c_ref, cg_ref, vec_ref, part_ref,
    mlp_ref, up_ref, table_ref, sq_ref, sv_ref, dt_ref, o_ref,
):
    d = x_ref.shape[1]
    wq, wk, wv = w_ref[:, 0:d], w_ref[:, d : 2 * d], w_ref[:, 2 * d : 3 * d]
    gain = vec_ref[1:2]
    lead = 2 * pages
    at = lead + pages

    @pl.when(pl.program_id(0) == 0)
    def _():
        o_ref[...] = jnp.zeros_like(o_ref)
        unit, inv = norm_parts(c_ref[...].astype(F32))
        gn = dot_t(cg_ref[:, 0:d], wk) + dot_t(cg_ref[:, d : 2 * d], wv)
        o_ref[0:lead] = part_ref[...]
        o_ref[lead:at] = norm_pull(gn * gain, unit, inv)[0:pages]
        o_ref[at + 1 : at + 2] = jnp.sum(gn * unit, axis=0, keepdims=True)
        o_ref[at + 2 : at + 3] = jnp.sum(gn, axis=0, keepdims=True)
        o_ref[at + 3 : at + 4] = sq_ref[0:1]
        o_ref[at + 4 : at + 5] = sv_ref[0:1]
        o_ref[at + 5 : at + 11] = mlp_ref[0:6]
        ups = up_ref.shape[1] // d
        for i in range(ups):
            o_ref[at + 11 + i : at + 12 + i] = up_ref[0:1, i * d : (i + 1) * d]
        for h in range(heads):
            r, c = divmod(h * LANES, d)
            o_ref[at + 11 + ups + r : at + 12 + ups + r, c : c + LANES] = table_ref[h : h + 1]

    raw = x_ref[...].astype(F32)
    masked = raw > FLAG / 2
    unit, inv = norm_parts(jnp.where(masked, vec_ref[0:1], raw))
    gn = dot_t(dq_ref[...], wq) + dot_t(dk_ref[...], wk) + dot_t(dv_ref[...], wv)
    gs = gres_ref[...] + norm_pull(gn * gain, unit, inv)
    dt_ref[...] = jnp.where(masked, 0.0, gs)
    o_ref[at : at + 1] += jnp.sum(jnp.where(masked, gs, 0.0), axis=0, keepdims=True)
    o_ref[at + 1 : at + 2] += jnp.sum(gn * unit, axis=0, keepdims=True)
    o_ref[at + 2 : at + 3] += jnp.sum(gn, axis=0, keepdims=True)


def token_grad_call(pages, heads, rows_in, whole, tile=256):
    n, d = rows_in[0].shape
    up = whole[6]
    count = 3 * pages + 11 + up.shape[1] // d - (-heads * LANES // d)
    height = -(-count // 8) * 8
    rows = pl.BlockSpec((tile, d), lambda i: (i, 0))
    return pl.pallas_call(
        functools.partial(token_grad_body, pages, heads),
        out_shape=(jax.ShapeDtypeStruct((n, d), F32), jax.ShapeDtypeStruct((height, d), F32)),
        grid=(n // tile,),
        in_specs=[rows] * 5 + [hold(a.shape) for a in whole],
        out_specs=[rows, hold((height, d))],
        compiler_params=params(ROOM),
        cost_estimate=pl.CostEstimate(
            flops=2 * n * d * 3 * d, transcendentals=n, bytes_accessed=2 * (8 * n * d + 3 * d * d)
        ),
        name="token_grad",
    )(*rows_in, *whole)


def passed_along(value, axis, steps):
    count = lax.axis_size(axis)
    first, last = max(0, -steps), min(count, count - steps)
    return lax.ppermute(value, axis, [(i, i + steps) for i in range(first, last)])


def swap(value, axis, bit):
    return lax.ppermute(value, axis, [(i, i ^ bit) for i in range(lax.axis_size(axis))])


def halo_pieces(geo, x):
    top = passed_along(x[:, geo.own - geo.edge :], "row", 1)
    bottom = passed_along(x[:, : geo.edge], "row", -1)
    to_right, to_left = strips_call(geo, x, top, bottom)
    return top, bottom, passed_along(to_right, "col", 1), passed_along(to_left, "col", -1)


def page_sum(part, by):
    return lax.psum_scatter(part, "dp", scatter_dimension=by, tiled=True)


def spread_sum(grad):
    part = lax.psum_scatter(grad, ("row", "col"), scatter_dimension=0, tiled=True)
    return page_sum(part, 1).astype(F32)


def join(values):
    return lax.optimization_barrier(values)


def shards(
    tokens, cls_token, patch_mask, loss_mask, mask_emb, ln1_gain, ln1_bias, w_qkv, q_bias, v_bias,
    rel_table, w_out, out_bias, scale_attn, ln2_gain, ln2_bias, w_up, up_bias, w_down, down_bias,
    scale_mlp, out_grad,
):
    pages, rows, cols, width = tokens.shape
    heads = rel_table.shape[0]
    geo = Geometry(pages, rows, cols, width, heads)
    count = pages * rows * cols
    row_peers, col_peers = lax.axis_size("row"), lax.axis_size("col")
    grid_rows, grid_cols = rows * row_peers, cols * col_peers
    row_at, col_at, page_at = (lax.axis_index(a) for a in ("row", "col", "dp"))

    ups = w_up.shape[1] // width
    vec = jnp.concatenate(
        [
            mask_emb, ln1_gain, ln1_bias, out_bias, scale_attn, ln2_gain, ln2_bias, down_bias,
            scale_mlp, q_bias, jnp.zeros((width,), F32), v_bias, up_bias,
        ]
    ).reshape(12 + ups, width)
    hm = jnp.asarray(geo.head_mask, BF16)
    hr, hrf = jnp.asarray(geo.head_rows, BF16), jnp.asarray(geo.head_rows, F32)
    sm, sa = jnp.asarray(geo.stat_mask, BF16), jnp.asarray(geo.stat_all, BF16)
    to_head, flank = jnp.asarray(geo.to_head, BF16), jnp.asarray(geo.flank_of, BF16)

    at_row = row_at * rows + BAND * np.arange(8)[:, None] - REACH + geo.slot_row[None, :]
    at_col = col_at * cols + geo.slot_col[None, :]
    inside = (at_row >= 0) & (at_row < grid_rows) & (at_col >= 0) & (at_col < grid_cols)
    inside = inside | (np.arange(geo.slots) >= geo.cls_at)[None, :]
    ok = jnp.where(inside, 0.0, NEG).astype(F32)

    masked = (patch_mask == 1)[..., None]
    x = jnp.where(masked, jnp.asarray(FLAG, BF16), tokens).reshape(pages, geo.own, width)
    pieces = halo_pieces(geo, x)
    bias_a = bias_table(geo, rel_table, 0)
    own = qkv_call(qkv_own_body, geo.own, (x,), (w_qkv, vec), "qkv_own")
    first = np.arange(16)[:, None] == 0
    cls_block = jnp.where(first, cls_token[:, None, :], jnp.zeros((), BF16))
    halo = qkv_call(
        functools.partial(qkv_halo_body, geo), geo.halo, pieces + (cls_block,),
        (flank, w_qkv, vec), "qkv_halo",
    )
    att, lse, probs, cls_part = attend_call(geo, own, halo, bias_a, ok, hm, hr, hrf)
    att, lse, x = att.reshape(count, width), lse.reshape(count, LANES), x.reshape(count, width)
    counted = (patch_mask * loss_mask == 1)[..., None]
    out_g = jnp.where(counted, out_grad, jnp.zeros((), BF16)).reshape(count, width)
    out, gmx, gres, gb, d_mlp, vg_mlp, d_upb = mlp_call(
        att, x, out_g, lse, w_out, vec, to_head, w_up, w_down, row_peers * col_peers
    )
    d_mlp = lax.psum_scatter(d_mlp, ("row", "col"), scatter_dimension=0, tiled=True)[0]
    gmx = gmx.reshape(pages, geo.own, width + LANES)
    pieces = halo_pieces(geo, gmx)
    bias_b = bias_table(geo, rel_table, 1)
    dq, d_table = query_grad_call(geo, probs, own, halo, gmx, hm, sm)
    class_bias = jnp.concatenate([rel_table[:, SPAN * SPAN], jnp.zeros((16 - heads,), F32)])
    class_bias = jnp.broadcast_to(class_bias[:, None], (16, geo.own))
    cls_rows = jnp.concatenate([cls_token, jnp.zeros((16 - pages, width), BF16)], axis=0)
    direct = (lax.axis_size("dp"), row_peers, col_peers) == (2, 4, 4)
    if direct:
        where = jnp.stack([row_at % 2, row_at // 2, col_at, page_at]).astype(jnp.int32)
    else:
        where = jnp.zeros((4,), jnp.int32)
    dq = dq.reshape(count, width)
    keep1, send1, nt, sum_q = early_weight_call(where, col_peers, x, att, dq, gb, vec)
    pieces, bias_b, nt = join((pieces, bias_b, nt))
    if direct:
        got1 = swap(send1, "row", 1)
    dk, dv, cls_low = key_grad_call(
        geo, own, halo, gmx, pieces, bias_b, ok, hm, sa, flank, hr, hrf, class_bias
    )
    dk, dv = dk.reshape(count, width), dv.reshape(count, width)
    keep2, send2, sum_v = late_weight_call(where, col_peers, nt, dk, dv, cls_rows, cls_low, vec)
    wide = lambda a: a.astype(F32)
    if direct:
        got2 = swap(send2, "row", 1)
        mine, to_x, to_y, to_far = fold_call(where, col_peers, keep1, got1, keep2, got2)
        mine, dq = join((mine, dq))
        near_x = swap(to_x, "dp", 1)
        near_y = swap(to_y, "row", 2)
        far = lax.ppermute(
            to_far,
            ("dp", "row"),
            [(4 * i + j, 4 * (i ^ 1) + (j ^ 2)) for i in range(2) for j in range(4)],
        )
    d_tok, block = token_grad_call(
        pages, heads, (x, dq, dk, dv, gres),
        (w_qkv, cls_rows, cls_low, vec, cls_part, vg_mlp, d_upb, d_table, sum_q, sum_v),
    )
    slab = width // (row_peers * col_peers)
    if direct:
        near_x, near_y, far, block = join((near_x, near_y, far, block))
        late = (wide(mine) + wide(near_x) + wide(near_y) + wide(far)).astype(BF16)
        beside = [swap(late[step], "col", step) for step in range(1, col_peers)]
        up, down = d_mlp[: ups * slab], d_mlp[ups * slab :]
        cut_up, cut_down = ups * slab // 2, width // 2

        def halves(place):
            return jnp.concatenate(
                [
                    lax.dynamic_slice_in_dim(up, place * cut_up, cut_up, 0),
                    lax.dynamic_slice_in_dim(down, place * cut_down, cut_down, 1).reshape(
                        -1, width
                    ),
                ],
                axis=0,
            )

        other = swap(halves(1 - page_at), "dp", 1)

    lead = 2 * pages
    vectors = block[lead:]
    parts, mine_at, place = block[:lead], jnp.zeros((), jnp.int32), 1
    sent = block
    for axis in ("col", "row"):
        peers, rows_in = lax.axis_size(axis), parts.shape[0]
        got = [swap(sent, axis, bit) for bit in range(1, peers)]
        level = [vectors] + [g[rows_in:] for g in got]
        while len(level) > 1:
            level = [a + b for a, b in zip(level[0::2], level[1::2])]
        vectors = level[0]
        parts = jnp.concatenate([parts] + [g[:rows_in] for g in got], axis=0)
        mine_at = mine_at + place * lax.axis_index(axis).astype(jnp.int32)
        place = place * peers
        sent = jnp.concatenate([parts, vectors], axis=0)

    d_cls, v = vectors[:pages], vectors[pages:]
    bit = 1
    while bit < lax.axis_size("dp"):
        v, bit = v + swap(v, "dp", bit), 2 * bit
    out_cls = class_close_call(
        geo, mine_at[None], parts.reshape(-1, 2 * pages, width), halo, cls_rows, to_head, w_out, vec, w_up,
        w_down,
    )[:pages]

    half = 3 * width // 2
    if direct:
        beside, other, v, out_cls = join((beside, other, v, out_cls))
        late = wide(late[0])
        for part in beside:
            late = late + wide(part)
        d_qkv, d_wout = late[:, :half], late[:, half:]
        both = wide(halves(page_at)) + wide(other)
        d_up = jnp.transpose(both[:cut_up].reshape(-1, slab, width), (1, 0, 2)).reshape(slab, -1)
        d_down = both[cut_up:].reshape(-1, cut_down)
    else:
        def whole(keep, send):
            both = jnp.stack([keep, send]).reshape(2, 2, col_peers, slab, 2 * width)
            return jnp.transpose(both, (1, 0, 2, 3, 4)).reshape(width, 2 * width)

        early, late = whole(keep1, send1), whole(keep2, send2)
        d_qkv = spread_sum(jnp.concatenate([early[:, :width], late], axis=1))
        d_wout = spread_sum(early[:, width:])
        d_up = jnp.transpose(d_mlp[: ups * slab].reshape(ups, slab, width), (1, 0, 2))
        d_up = page_sum(d_up.reshape(slab, ups * width), 1).astype(F32)
        d_down = page_sum(d_mlp[ups * slab :], 1).astype(F32)

    d_rel = v[11 + ups : 13 + ups].reshape(-1)[: heads * LANES].reshape(heads, LANES)[:, : SPAN * SPAN + 1]
    return (
        out.reshape(tokens.shape),
        out_cls,
        d_tok.reshape(tokens.shape),
        d_cls,
        d_qkv,
        d_wout,
        d_up,
        d_down,
        v[0],
        v[1],
        v[2],
        v[3],
        v[4],
        d_rel,
        v[10],
        v[9],
        v[7],
        v[8],
        v[11 : 11 + ups].reshape(-1),
        v[6],
        v[5],
    )


def solution(mesh):
    tile = P("dp", "row", "col", None)
    flat = P("dp", "row", "col")
    weights = P(("row", "col"), "dp")
    return jax.shard_map(
        shards,
        mesh=mesh,
        in_specs=(tile, P("dp", None), flat, flat) + (P(),) * 17 + (tile,),
        out_specs=(tile, P("dp", None), tile, P("dp", None)) + (weights,) * 4 + (P(),) * 13,
        check_vma=False,
    )
```

```python
import functools
import math

import jax
import jax.numpy as jnp
import numpy as np
from jax import lax
from jax.experimental import pallas as pl
from jax.experimental.pallas import tpu as pltpu
from jax.sharding import PartitionSpec as P

F32 = jnp.float32
BF16 = jnp.bfloat16
NEG = -1e30
REACH = 3
SPAN = 7
BAND = 4
SIDE = 8
LANES = 128
FLAG = 1024.0
ROOM, LESS = 56, 28
EPS = 1e-06
MIB = 1 << 20
ANYWHERE = pl.BlockSpec(memory_space=pl.ANY)


def dot(a, b):
    return jnp.dot(a, b, preferred_element_type=F32)


def dot_t(a, b):
    return lax.dot_general(a, b, (((1,), (1,)), ((), ())), preferred_element_type=F32)


def dot_0(a, b):
    return lax.dot_general(a, b, (((0,), (0,)), ((), ())), preferred_element_type=F32)


def split3(x):
    hi = x.astype(BF16)
    rest = x - hi.astype(F32)
    mid = rest.astype(BF16)
    low = (rest - mid.astype(F32)).astype(BF16)
    return hi, mid, low


def norm_parts(x):
    c = x - jnp.mean(x, axis=-1, keepdims=True)
    inv = lax.rsqrt(jnp.mean(c * c, axis=-1, keepdims=True) + EPS)
    return c * inv, inv


def norm_pull(e, unit, inv):
    return inv * (
        e
        - jnp.mean(e, axis=-1, keepdims=True)
        - unit * jnp.mean(e * unit, axis=-1, keepdims=True)
    )


def unmask(x, emb):
    return jnp.where(x > FLAG / 2, emb, x)


class Geometry:
    def __init__(self, pages, rows, cols, width, heads):
        self.pages, self.rows, self.cols = pages, rows, cols
        self.width, self.heads = width, heads
        self.head = width // heads
        self.lanes = 256
        self.stack = self.lanes // self.head
        self.groups = width // self.lanes
        self.own = rows * cols
        self.edge = REACH * cols
        self.side = (rows + 2 * REACH) * SIDE
        self.halo = 2 * self.edge + self.side + 16
        self.bands = rows // BAND
        self.band = BAND * cols
        self.main = (BAND + 2 * REACH) * cols
        self.flank = (BAND + 2 * REACH) * SIDE
        self.slots = self.main + self.flank + 16
        self.cls_at = self.main + self.flank
        slot = np.arange(self.slots)
        r = np.where(slot < self.main, slot // cols, (slot - self.main) // SIDE)
        s = (slot - self.main) % SIDE
        c = np.where(
            slot < self.main,
            slot % cols,
            np.where(s < REACH, s - REACH, np.where(s < 2 * REACH, cols + s - REACH, -1000)),
        )
        is_cls = slot >= self.cls_at
        r = np.where(is_cls, -1000, r)
        c = np.where(is_cls, -1000, c)
        self.slot_row, self.slot_col = r, c
        q = np.arange(self.band)
        a = r[None, :] - (q // cols)[:, None]
        b = c[None, :] - (q % cols)[:, None] + REACH
        ok = (a >= 0) & (a < SPAN) & (b >= 0) & (b < SPAN)
        offset = np.where(ok, a * SPAN + b, -1)
        mirror = np.where(ok, SPAN * SPAN - 1 - offset, -1)
        offset[:, self.cls_at] = SPAN * SPAN
        self.offset = offset.astype(np.int32)
        self.mirror = mirror.astype(np.int32)
        fold = np.full((cols, self.slots), -1, np.int32)
        for i in range(cols):
            for lane in range(SPAN * cols):
                d = lane % cols - i + REACH
                if 0 <= d < SPAN:
                    fold[i, lane] = lane // cols * SPAN + d
            for lane in range(SPAN * SIDE):
                s1 = lane % SIDE
                if s1 < 2 * REACH:
                    col = s1 - REACH if s1 < REACH else cols + s1 - REACH
                    d = col - i + REACH
                    if 0 <= d < SPAN:
                        fold[i, self.main + lane] = lane // SIDE * SPAN + d
            fold[i, self.cls_at] = SPAN * SPAN
        self.fold = fold.T.copy()
        lane = np.arange(self.lanes) // self.head
        self.head_mask = (np.arange(16)[:, None] == lane[None, :]).astype(np.float32)
        stat = np.zeros((self.groups, 8, LANES), np.float32)
        every = np.zeros((32, LANES), np.float32)
        for h in range(heads):
            g, k = divmod(h, self.stack)
            for part in range(3):
                stat[g, k, 48 + 16 * part + h] = -1.0
                every[h, 16 * part + h] = -1.0
                every[16 + h, 48 + 16 * part + h] = -1.0
        self.stat_mask = stat
        self.stat_all = every
        self.to_head = (np.arange(width)[:, None] // self.head == np.arange(LANES)[None, :]).astype(
            np.float32
        )
        self.head_rows = self.to_head.T[:16].copy()
        base = np.full((2, cols, self.slots), -1, np.int32)
        for i in range(cols):
            for lane in range(self.slots):
                o = fold[i, lane]
                base[0, i, lane] = o
                base[1, i, lane] = SPAN * SPAN - 1 - o if 0 <= o < SPAN * SPAN else -1
        self.base = base
        tall = rows + 2 * REACH
        self.strip = -(-REACH * tall // 8) * 8
        flank = np.zeros((2, self.side, self.strip), np.float32)
        for r in range(tall):
            for i in range(REACH):
                flank[0, r * SIDE + i, r * REACH + i] = 1.0
                flank[1, r * SIDE + REACH + i, r * REACH + i] = 1.0
        self.flank_of = flank

    def block(self, own, halo, b):
        lo, hi = b * self.band, b * self.band + self.main
        e, o = self.edge, self.own
        parts = []
        if lo < e:
            parts.append(halo[lo : min(hi, e)])
        parts.append(own[max(lo - e, 0) : min(hi - e, o)])
        if hi > e + o:
            parts.append(halo[e + max(lo - e - o, 0) : e + hi - e - o])
        at = 2 * e + b * BAND * SIDE
        parts.append(halo[at : at + self.flank])
        parts.append(halo[2 * e + self.side : 2 * e + self.side + 16])
        return jnp.concatenate(parts, axis=0)

    def around(self, top, bottom, left, right, flank, last):
        side = dot(flank[0], left) + dot(flank[1], right)
        return jnp.concatenate([top, bottom, side.astype(BF16), last], axis=0)

    def stacked(self, x, mask):
        return jnp.concatenate([x * mask[h : h + 1] for h in range(self.stack)], axis=0)

    def unstacked(self, r):
        rows = r.shape[0] // self.stack
        lane = lax.broadcasted_iota(jnp.int32, (rows, self.lanes), 1) // self.head
        out = r[(self.stack - 1) * rows :]
        for h in range(self.stack - 1):
            out = jnp.where(lane == h, r[h * rows : (h + 1) * rows], out)
        return out


def full(shape):
    return pl.BlockSpec(shape, lambda *_: (0,) * len(shape))


def hold(shape):
    return pl.BlockSpec(shape, lambda *_: (0,) * len(shape), pipeline_mode=pl.Buffered(1))


def params(limit, sem=1):
    return pltpu.CompilerParams(
        dimension_semantics=("arbitrary",) * sem, vmem_limit_bytes=limit * MIB
    )


def bias_body(geo, table, index_ref, out_ref):
    lane = lax.broadcasted_iota(jnp.int32, (geo.cols, geo.slots), 1)
    low = jnp.full((geo.cols, geo.slots), NEG, F32)
    index = index_ref[...]
    pair = 2

    def head(i, carry):
        acc = [low] * (2 * pair)
        for o in range(SPAN * SPAN + 1):
            hit = index == o
            for j in range(pair):
                at = 2 * j + o % 2
                acc[at] = jnp.where(hit, table[i * pair + j, o], acc[at])
        for j in range(pair):
            both = jnp.maximum(acc[2 * j], acc[2 * j + 1])
            main = jnp.where(lane < geo.main, both, low)
            side = jnp.where((lane >= geo.main) & (lane < geo.cls_at), both, low)
            last = jnp.where(lane >= geo.cls_at, both, low)
            h = i * pair + j
            for r in range(BAND):
                if r:
                    both = jnp.maximum(
                        pltpu.roll(main, r * geo.cols, 1), pltpu.roll(side, r * SIDE, 1)
                    )
                else:
                    both = jnp.maximum(main, side)
                at = pl.multiple_of(h % geo.stack * geo.band + r * geo.cols, 8)
                out_ref[h // geo.stack, pl.ds(at, geo.cols), :] = jnp.maximum(both, last)
        return carry

    lax.fori_loop(0, geo.heads // pair, head, 0)


def bias_table(geo, rel_table, which):
    return pl.pallas_call(
        functools.partial(bias_body, geo),
        out_shape=jax.ShapeDtypeStruct((geo.groups, geo.stack * geo.band, geo.slots), F32),
        in_specs=[
            pl.BlockSpec(memory_space=pltpu.SMEM),
            pl.BlockSpec(memory_space=pltpu.VMEM),
        ],
        out_specs=pl.BlockSpec(memory_space=pltpu.VMEM),
        compiler_params=pltpu.CompilerParams(vmem_limit_bytes=ROOM * MIB),
        name="bias_table",
    )(rel_table, jnp.asarray(geo.base[which]))


def qkv_rows(pages, w_ref, vec_ref, o_ref):
    d = pages[0].shape[1]

    def normed(raw):
        unit, _ = norm_parts(unmask(raw.astype(F32), vec_ref[0:1]))
        return (unit * vec_ref[1:2] + vec_ref[2:3]).astype(BF16)

    now = normed(pages[0])
    for k in range(len(pages)):
        rows = dot(now, w_ref[...])
        if k + 1 < len(pages):
            now = normed(pages[k + 1])
        for i in range(3):
            cols = slice(i * d, (i + 1) * d)
            o_ref[k, :, cols] = (rows[:, cols] + vec_ref[9 + i : 10 + i]).astype(BF16)


def qkv_own_body(x_ref, w_ref, vec_ref, o_ref):
    span = x_ref.shape[0]
    qkv_rows([x_ref[k] for k in range(span)], w_ref, vec_ref, o_ref)


def qkv_halo_body(geo, top_ref, bottom_ref, left_ref, right_ref, last_ref, flank_ref, w_ref, vec_ref, o_ref):
    span = top_ref.shape[0]
    raw = [
        geo.around(
            top_ref[k], bottom_ref[k], left_ref[k], right_ref[k], flank_ref[...], last_ref[k]
        )
        for k in range(span)
    ]
    qkv_rows(raw, w_ref, vec_ref, o_ref)


def part_of(a, i, d, rows=None):
    rows = rows or a.shape[1]
    return pl.BlockSpec((1, rows, d), lambda p: (p, a.shape[1] // rows - 1, i))


def by_page(a, span=1):
    return pl.BlockSpec((span,) + a.shape[1:], lambda p: (p,) + (0,) * (len(a.shape) - 1))


def qkv_call(body, rows, paged, whole, name):
    pages, _, d = paged[0].shape
    span = 2 if pages % 2 == 0 else 1
    n = pages * rows
    return pl.pallas_call(
        body,
        out_shape=jax.ShapeDtypeStruct((pages, rows, 3 * d), BF16),
        grid=(pages // span,),
        in_specs=[by_page(a, span) for a in paged] + [hold(a.shape) for a in whole],
        out_specs=pl.BlockSpec((span, rows, 3 * d), lambda p: (p, 0, 0)),
        compiler_params=params(ROOM),
        cost_estimate=pl.CostEstimate(
            flops=6 * n * d * d, transcendentals=n, bytes_accessed=2 * (4 * n * d + 3 * d * d)
        ),
        name=name,
    )(*paged, *whole)


def strips_body(geo, x_ref, top_ref, bottom_ref, right_ref, left_ref, tall, near):
    e, o = geo.edge, geo.own
    near[...] = jnp.zeros_like(near)

    def page(p, carry):
        tall[0:e, :] = top_ref[p].astype(F32)
        tall[e : e + o, :] = x_ref[p].astype(F32)
        tall[e + o :, :] = bottom_ref[p].astype(F32)
        for r in range(geo.rows + 2 * REACH):
            to, at = r * REACH, r * geo.cols
            near[0, to : to + REACH, :] = tall[at + geo.cols - REACH : at + geo.cols, :]
            near[1, to : to + REACH, :] = tall[at : at + REACH, :]
        right_ref[p] = near[0].astype(BF16)
        left_ref[p] = near[1].astype(BF16)
        return carry

    lax.fori_loop(0, geo.pages, page, 0)


def strips_call(geo, x, top, bottom):
    width = x.shape[2]
    shape = jax.ShapeDtypeStruct((geo.pages, geo.strip, width), BF16)
    return pl.pallas_call(
        functools.partial(strips_body, geo),
        out_shape=(shape, shape),
        scratch_shapes=[
            pltpu.VMEM((2 * geo.edge + geo.own, width), F32),
            pltpu.VMEM((2, geo.strip, width), F32),
        ],
        compiler_params=pltpu.CompilerParams(vmem_limit_bytes=ROOM * MIB),
        name="strips",
    )(x, top, bottom)


def class_part(geo, own_ref, cq_ref, hr_ref, hrf_ref, o_ref):
    page, d = pl.program_id(0), geo.width

    @pl.when(page == 0)
    def _():
        o_ref[...] = jnp.zeros_like(o_ref)

    scale = BF16(1.0 / math.sqrt(geo.head))
    hr, hrf = hr_ref[...], hrf_ref[...]
    qc = jnp.broadcast_to(cq_ref[0, 0:1, :] * scale, (16, d)) * hr
    s = dot_t(qc, own_ref[0, :, d : 2 * d])
    top = jnp.max(s, axis=-1, keepdims=True)
    e = jnp.exp(s - top)
    total = jnp.sum(e, axis=-1, keepdims=True)
    acc = dot(jnp.concatenate(split3(e), axis=0), own_ref[0, :, 2 * d : 3 * d])
    acc = acc[0:16] + acc[16:32] + acc[32:48]
    o_ref[pl.ds(page, 1), :] = jnp.sum(acc * hrf, axis=0, keepdims=True)
    row = lax.broadcasted_iota(jnp.int32, (16, LANES), 0)
    diag = row == lax.broadcasted_iota(jnp.int32, (16, LANES), 1)
    stats = [jnp.sum(jnp.where(diag, a, 0.0), axis=0, keepdims=True) for a in (top, total)]
    stats.append(jnp.zeros((1, d - 2 * LANES), F32))
    o_ref[pl.ds(geo.pages + page, 1), :] = jnp.concatenate(stats, axis=1)


def attend_body(
    geo, own_ref, hk_ref, hv_ref, cq_ref, bias_ref, ok_ref, hm_ref, hr_ref, hrf_ref, o_ref, lse_ref,
    p_ref, c_ref,
):
    scale = BF16(1.0 / math.sqrt(geo.head))
    hm = hm_ref[...]
    lane = lax.broadcasted_iota(jnp.int32, (geo.band, LANES), 1)
    bands = range(geo.bands)
    at = [slice(b * geo.band, (b + 1) * geo.band) for b in bands]
    lses = [jnp.zeros((geo.band, LANES), F32) for _ in bands]

    def part(ref, which, g):
        lo = which * geo.width + g * geo.lanes
        return ref[0, :, lo : lo + geo.lanes]

    def score(g):
        q, k, hk = part(own_ref, 0, g), part(own_ref, 1, g), part(hk_ref, 0, g)
        return [
            dot_t(geo.stacked(q[at[b]] * scale, hm), geo.block(k, hk, b))
            + bias_ref[g]
            + ok_ref[b : b + 1]
            for b in bands
        ]

    def soften(g, scores):
        probs = []
        for b in bands:
            top = jnp.max(scores[b], axis=-1, keepdims=True)
            e = jnp.exp(scores[b] - top)
            total = jnp.sum(e, axis=-1, keepdims=True)
            lse = top + jnp.log(total)
            for h in range(geo.stack):
                rows = slice(h * geo.band, (h + 1) * geo.band)
                lses[b] = jnp.where(lane == g * geo.stack + h, lse[rows], lses[b])
            p = (e * (1.0 / total)).astype(BF16)
            p_ref[0, g, b] = p
            probs.append(p)
        return probs

    def mix(g, probs):
        v, hv = part(own_ref, 2, g), part(hv_ref, 0, g)
        for b in bands:
            rows = geo.unstacked(dot(probs[b], geo.block(v, hv, b)))
            o_ref[0, at[b], g * geo.lanes : (g + 1) * geo.lanes] = rows.astype(BF16)

    class_part(geo, own_ref, cq_ref, hr_ref, hrf_ref, c_ref)
    scores = score(0)
    for g in range(geo.groups):
        probs = soften(g, scores)
        if g + 1 < geo.groups:
            scores = score(g + 1)
        mix(g, probs)
    for b in bands:
        lse_ref[0, at[b], :] = lses[b]


def attend_call(geo, own, halo, bias, ok, hm, hr, hrf):
    G = geo.groups
    mm = 2 * geo.pages * G * geo.bands * 256 * 256 * 256
    outs = (
        jax.ShapeDtypeStruct((geo.pages, geo.own, geo.width), BF16),
        jax.ShapeDtypeStruct((geo.pages, geo.own, LANES), F32),
        jax.ShapeDtypeStruct((geo.pages, G, geo.bands, geo.lanes, geo.slots), BF16),
        jax.ShapeDtypeStruct((2 * geo.pages, geo.width), F32),
    )
    return pl.pallas_call(
        functools.partial(attend_body, geo),
        out_shape=outs,
        grid=(geo.pages,),
        in_specs=[by_page(own)]
        + [part_of(halo, i, geo.width) for i in (1, 2)]
        + [part_of(halo, 0, geo.width, 16)]
        + [hold(a.shape) for a in (bias, ok, hm, hr, hrf)],
        out_specs=[by_page(a) for a in outs[:3]] + [hold((2 * geo.pages, geo.width))],
        compiler_params=params(ROOM),
        cost_estimate=pl.CostEstimate(
            flops=2 * mm, transcendentals=geo.pages * G * geo.bands * 65536, bytes_accessed=16 * MIB
        ),
        name="attend",
    )(own, halo, halo, halo, bias, ok, hm, hr, hrf)


def mlp_body(
    tile, steps, att_ref, x_ref, og_ref, lse_ref, wout_ref, vec_ref, toh_ref, wup_ref, wdn_ref,
    out_ref, gmx_ref, gres_ref, gb_ref, dw_ref, vg_ref, dub_ref,
    n2, n2t, gm, res, branch, mlp, gn, act, dh, up_buf, dn_buf, out_buf, gmx_buf, gres_buf, gb_buf,
    og_buf, lse_buf, wup_buf, wdn_buf, sems, out_sems, in_sems, w_sems,
):
    step = pl.program_id(0)
    n, d = n2.shape
    row = lambda i: vec_ref[i : i + 1]
    tiles, few, rows_dn = n // tile, dn_buf.shape[0], dn_buf.shape[1]
    rows_up = up_buf.shape[1]
    span = lambda t: pl.ds(pl.multiple_of(t * tile, tile), tile)
    late = (
        pltpu.make_async_copy(og_ref, og_buf, in_sems.at[0]),
        pltpu.make_async_copy(lse_ref, lse_buf, in_sems.at[1]),
    )

    def weights(c):
        slot = lax.rem(c, 2)
        at = pl.ds(pl.multiple_of(c * d, d), d)
        return (
            pltpu.make_async_copy(wup_ref.at[:, at], wup_buf.at[slot], w_sems.at[slot, 0]),
            pltpu.make_async_copy(wdn_ref.at[at, :], wdn_buf.at[slot], w_sems.at[slot, 1]),
        )

    @pl.when(step == 0)
    def _():
        for copy in late + weights(0):
            copy.start()

        def one(t, carry):
            rows = span(t)
            x = unmask(x_ref[rows, :].astype(F32), row(0))
            br = dot(att_ref[rows, :], wout_ref[...]) + row(3)
            r = x + row(4) * br
            branch[rows, :] = br
            res[rows, :] = r
            unit, _ = norm_parts(r)
            n2[rows, :] = (unit * row(5) + row(6)).astype(BF16)
            mlp[rows, :] = jnp.zeros((tile, d), F32)
            gn[rows, :] = jnp.zeros((tile, d), F32)
            return carry

        lax.fori_loop(0, tiles, one, 0)
        n2t[...] = n2[...].T
        vg_ref[...] = jnp.zeros_like(vg_ref)
        for copy in late:
            copy.wait()

        def two(t, carry):
            rows = span(t)
            gm[rows, :] = (row(8) * og_buf[rows, :].astype(F32)).astype(BF16)
            return carry

        lax.fori_loop(0, tiles, two, 0)

    for copy in weights(step):
        copy.wait()

    @pl.when(step + 1 < steps)
    def _():
        for copy in weights(step + 1):
            copy.start()

    wup, wdn = wup_buf[lax.rem(step, 2)], wdn_buf[lax.rem(step, 2)]
    upb = vec_ref[pl.ds(12 + step, 1), :]
    dub_ref[...] = jnp.zeros_like(dub_ref)

    def one(t, carry):
        rows = pl.ds(pl.multiple_of(t * 2 * tile, 2 * tile), 2 * tile)
        h = dot(n2[rows, :], wup) + upb
        da = dot_t(gm[rows, :], wdn)
        cdf = 0.5 * (1.0 + lax.erf(h * math.sqrt(0.5)))
        pdf = jnp.exp(-0.5 * h * h) * (1.0 / math.sqrt(2.0 * math.pi))
        a = (h * cdf).astype(BF16)
        g = (da * (cdf + h * pdf)).astype(BF16)
        act[rows, :] = a
        dh[rows, :] = g
        mlp[rows, :] += dot(a, wdn)
        gn[rows, :] += dot_t(g, wup)
        dub_ref[0:1] += jnp.sum(g.astype(F32), axis=0, keepdims=True)
        return carry

    lax.fori_loop(0, tiles // 2, one, 0)

    def copies(c):
        at = pl.multiple_of(c * rows_up, 8)
        return (
            pltpu.make_async_copy(up_buf, dw_ref.at[:, pl.ds(at, rows_up), :], sems.at[0]),
            pltpu.make_async_copy(
                dn_buf,
                dw_ref.at[pl.ds(c * few, few), steps * rows_up : steps * rows_up + rows_dn, :],
                sems.at[1],
            ),
        )

    @pl.when(step > 0)
    def _():
        for copy in copies(step - 1):
            copy.wait()

    up_buf[...] = dot(n2t[...], dh[...]).astype(BF16).reshape(up_buf.shape)
    dn_buf[...] = dot_0(act[...], gm[...]).astype(BF16).reshape(dn_buf.shape)
    for copy in copies(step):
        copy.start()

    @pl.when(step == steps - 1)
    def _():
        outs = ((out_buf, out_ref), (gmx_buf, gmx_ref), (gres_buf, gres_ref), (gb_buf, gb_ref))

        def sends(t, slot):
            return [
                pltpu.make_async_copy(buf.at[slot], ref.at[span(t), :], out_sems.at[slot, i])
                for i, (buf, ref) in enumerate(outs)
            ]

        def add(i, v):
            vg_ref[i : i + 1] += jnp.sum(v, axis=0, keepdims=True)

        def one(t, carry):
            rows, slot = span(t), lax.rem(t, 2)

            @pl.when(t >= 2)
            def _():
                for copy in sends(t - 2, slot):
                    copy.wait()

            r, br, att = res[rows, :], branch[rows, :], att_ref[rows, :]
            og = og_buf[rows, :].astype(F32)
            mo = mlp[rows, :] + row(7)
            out_buf[slot] = (r + row(8) * mo).astype(BF16)
            add(0, og * mo)
            add(1, gm[rows, :].astype(F32))
            unit, inv = norm_parts(r)
            grad = gn[rows, :]
            add(2, grad * unit)
            add(3, grad)
            gr = og + norm_pull(grad * row(5), unit, inv)
            gres_buf[slot] = gr
            add(4, gr * br)
            gb = (row(4) * gr).astype(BF16)
            add(5, gb.astype(F32))
            gb_buf[slot] = gb
            mix = dot_t(gb, wout_ref[...]).astype(BF16)
            prod = mix.astype(F32) * att.astype(F32)
            delta = sum(dot(part, toh_ref[...]) for part in split3(prod))
            packed = jnp.zeros(delta.shape, F32)
            for i, part in enumerate(split3(lse_buf[rows, :]) + split3(delta)):
                part = part.astype(F32)
                packed += part if i == 0 else pltpu.roll(part, 16 * i, 1)
            gmx_buf[slot, :, 0:d] = mix
            gmx_buf[slot, :, d : d + LANES] = packed.astype(BF16)
            for copy in sends(t, slot):
                copy.start()
            return carry

        lax.fori_loop(0, tiles, one, 0)
        for t in (tiles - 2, tiles - 1):
            for copy in sends(t, t % 2):
                copy.wait()
        for copy in copies(step):
            copy.wait()


def mlp_call(att, x, og, lse, w_out, vec, to_head, w_up, w_down, dests, tile=256):
    n, d = x.shape
    ff = w_up.shape[1]
    steps = ff // d
    rows_up, rows_dn = d // dests, ff // dests
    anywhere = pl.BlockSpec(memory_space=pl.ANY)
    return pl.pallas_call(
        functools.partial(mlp_body, tile, steps),
        out_shape=(
            jax.ShapeDtypeStruct((n, d), BF16),
            jax.ShapeDtypeStruct((n, d + LANES), BF16),
            jax.ShapeDtypeStruct((n, d), F32),
            jax.ShapeDtypeStruct((n, d), BF16),
            jax.ShapeDtypeStruct((dests, steps * rows_up + rows_dn, d), BF16),
            jax.ShapeDtypeStruct((8, d), F32),
            jax.ShapeDtypeStruct((8, ff), F32),
        ),
        grid=(steps,),
        in_specs=[hold(att.shape), hold(x.shape), anywhere, anywhere]
        + [hold(a.shape) for a in (w_out, vec, to_head)]
        + [anywhere, anywhere],
        out_specs=[anywhere] * 5 + [hold((8, d)), pl.BlockSpec((8, d), lambda c: (0, c))],
        scratch_shapes=[
            pltpu.VMEM((n, d), BF16),
            pltpu.VMEM((d, n), BF16),
            pltpu.VMEM((n, d), BF16),
            pltpu.VMEM((n, d), F32),
            pltpu.VMEM((n, d), F32),
            pltpu.VMEM((n, d), F32),
            pltpu.VMEM((n, d), F32),
            pltpu.VMEM((n, d), BF16),
            pltpu.VMEM((n, d), BF16),
            pltpu.VMEM((dests, rows_up, d), BF16),
            pltpu.VMEM((dests // steps, rows_dn, d), BF16),
            pltpu.VMEM((2, tile, d), BF16),
            pltpu.VMEM((2, tile, d + LANES), BF16),
            pltpu.VMEM((2, tile, d), F32),
            pltpu.VMEM((2, tile, d), BF16),
            pltpu.VMEM((n, d), BF16),
            pltpu.VMEM((n, LANES), F32),
            pltpu.VMEM((2, d, d), BF16),
            pltpu.VMEM((2, d, d), BF16),
            pltpu.SemaphoreType.DMA((2,)),
            pltpu.SemaphoreType.DMA((2, 4)),
            pltpu.SemaphoreType.DMA((2,)),
            pltpu.SemaphoreType.DMA((2, 2)),
        ],
        compiler_params=params(ROOM),
        cost_estimate=pl.CostEstimate(
            flops=2 * n * d * (6 * ff + 2 * d),
            transcendentals=2 * n * ff,
            bytes_accessed=2 * (4 * d * ff + 8 * n * d),
        ),
        name="mlp",
    )(att, x, og, lse, w_out, vec, to_head, w_up, w_down)


def table_sums(geo, acc_ref, fold_ref, o_ref):
    lane = lax.broadcasted_iota(jnp.int32, (geo.cols, geo.slots), 1)
    heads = []
    for g in range(geo.groups):
        for h in range(geo.stack):
            x = acc_ref[g, h * geo.band : (h + 1) * geo.band, :]
            parts = [x[i * geo.cols : (i + 1) * geo.cols] for i in range(BAND)]
            main, side, plain = parts[0], parts[0], parts[0]
            for i in range(1, BAND):
                main = main + pltpu.roll(parts[i], geo.slots - i * geo.cols, 1)
                side = side + pltpu.roll(parts[i], geo.slots - i * SIDE, 1)
                plain = plain + parts[i]
            z = jnp.where(lane < SPAN * geo.cols, main, jnp.where(lane < geo.cls_at, side, plain))
            heads.append(z)
    pad = [jnp.zeros((geo.cols, geo.slots), F32)] * (16 - geo.heads)
    z = jnp.stack(heads + pad, axis=0)
    total = jnp.zeros((16, LANES), F32)
    which = lax.broadcasted_iota(jnp.int32, (geo.slots, LANES), 1)
    for i in range(geo.cols):
        pick = jnp.where(fold_ref[:, i : i + 1] == which, 1.0, 0.0).astype(BF16)
        for part in split3(z[:, i, :]):
            total += dot(part, pick)
    o_ref[...] = total


def query_grad_body(
    geo, p_ref, k_ref, v_ref, hk_ref, hv_ref, gm_ref, hm_ref, sm_ref, fold_ref, dq_ref, table_ref,
    rel_ref,
):
    scale = 1.0 / math.sqrt(geo.head)
    hm = hm_ref[...]
    bands = range(geo.bands)
    at = [slice(b * geo.band, (b + 1) * geo.band) for b in bands]
    ones = jnp.ones((geo.slots, LANES), BF16)
    join = lambda a, b: jnp.concatenate([a, b], axis=1)
    st = gm_ref[0, :, geo.width :]

    @pl.when(pl.program_id(0) == 0)
    def _():
        rel_ref[...] = jnp.zeros_like(rel_ref)

    def part(ref, which, g):
        lo = which * geo.width + g * geo.lanes
        return ref[0, :, lo : lo + geo.lanes]

    def pull(g):
        gm, v, hv = part(gm_ref, 0, g), part(v_ref, 0, g), part(hv_ref, 0, g)
        sm = sm_ref[g]
        return [
            dot_t(
                join(geo.stacked(gm[at[b]], hm), geo.stacked(st[at[b]], sm)),
                join(geo.block(v, hv, b), ones),
            )
            for b in bands
        ]

    dp = pull(0)
    for g in range(geo.groups):
        ds = [p_ref[0, g, b].astype(F32) * dp[b] for b in bands]
        if g + 1 < geo.groups:
            dp = pull(g + 1)
        total = ds[0]
        for d in ds[1:]:
            total = total + d
        rel_ref[g] += total
        k, hk = part(k_ref, 0, g), part(hk_ref, 0, g)
        for b in bands:
            rows = geo.unstacked(dot((ds[b] * scale).astype(BF16), geo.block(k, hk, b)))
            dq_ref[0, at[b], g * geo.lanes : (g + 1) * geo.lanes] = rows.astype(BF16)

    @pl.when(pl.program_id(0) == geo.pages - 1)
    def _():
        table_sums(geo, rel_ref, fold_ref, table_ref)


def query_grad_call(geo, probs, own, halo, gmx, hm, sm):
    G = geo.groups
    mm = 2 * geo.pages * G * geo.bands * 256 * 256 * 256
    dq = jax.ShapeDtypeStruct((geo.pages, geo.own, geo.width), BF16)
    table = jax.ShapeDtypeStruct((16, LANES), F32)
    fold = jnp.asarray(geo.fold)
    return pl.pallas_call(
        functools.partial(query_grad_body, geo),
        out_shape=(dq, table),
        grid=(geo.pages,),
        in_specs=[by_page(probs)]
        + [part_of(a, i, geo.width) for a in (own, halo) for i in (1, 2)]
        + [by_page(gmx)]
        + [hold(a.shape) for a in (hm, sm, fold)],
        out_specs=[by_page(dq), hold(table.shape)],
        scratch_shapes=[pltpu.VMEM((geo.groups, geo.stack * geo.band, geo.slots), F32)],
        compiler_params=params(ROOM),
        cost_estimate=pl.CostEstimate(
            flops=2 * mm, transcendentals=0, bytes_accessed=20 * MIB
        ),
        name="query_grad",
    )(probs, own, own, halo, halo, gmx, hm, sm, fold)


def class_grad(geo, own_ref, cls_ref, gm_ref, hr_ref, hrf_ref, sa_ref, cb_ref, o_ref, acc):
    page, d = pl.program_id(0), geo.width

    @pl.when(page == 0)
    def _():
        acc[...] = jnp.zeros_like(acc)

    scale = 1.0 / math.sqrt(geo.head)
    hr, hrf, sa = hr_ref[...], hrf_ref[...], sa_ref[...]
    q, gm, st = own_ref[0, :, 0:d], gm_ref[0, :, 0:d], gm_ref[0, :, d:]
    kc = jnp.broadcast_to(cls_ref[0, 0:1, d : 2 * d] * BF16(scale), (16, d)) * hr
    vc = jnp.broadcast_to(cls_ref[0, 0:1, 2 * d : 3 * d], (16, d)) * hr
    prob = jnp.exp(dot_t(kc, q) + dot_t(sa[0:16], st) + cb_ref[...])
    ds = prob * (dot_t(vc, gm) + dot_t(sa[16:32], st))
    row = pl.ds(page, 1)
    dk = dot((ds * scale).astype(BF16), q)
    dv = dot(prob.astype(BF16), gm)
    acc[row, 0:d] = jnp.sum(dk * hrf, axis=0, keepdims=True)
    acc[row, d : 2 * d] = jnp.sum(dv * hrf, axis=0, keepdims=True)

    @pl.when(page == geo.pages - 1)
    def _():
        o_ref[...] = acc[...].astype(BF16)


def key_grad_body(
    geo, own_ref, hq_ref, cls_ref, gm_ref, top_ref, bottom_ref, left_ref, right_ref,
    bias_ref, ok_ref, hm_ref, sa_ref, flank_ref, hr_ref, hrf_ref, cb_ref, dk_ref, dv_ref, c_ref,
    hgm, rowstat, acc,
):
    scale = 1.0 / math.sqrt(geo.head)
    hm = hm_ref[...]
    bands = range(geo.bands)
    at = [slice(b * geo.band, (b + 1) * geo.band) for b in bands]
    last = jnp.zeros((16, gm_ref.shape[2]), BF16)
    hgm[...] = geo.around(
        top_ref[0], bottom_ref[0], left_ref[0], right_ref[0], flank_ref[...], last
    )
    stats, own = hgm[:, geo.width :], gm_ref[0, :, geo.width :]
    row = lax.broadcasted_iota(jnp.int32, (32, geo.slots), 0)
    for b in bands:
        r = dot_t(sa_ref[...], geo.block(own, stats, b))
        rowstat[b] = r + jnp.where(row < 16, ok_ref[b : b + 1], 0.0)

    def part(ref, which, g):
        lo = which * geo.width + g * geo.lanes
        return ref[0, :, lo : lo + geo.lanes]

    def spread(g, b, first):
        at = first + g * geo.stack
        return jnp.concatenate(
            [
                jnp.broadcast_to(rowstat[b, at + h : at + h + 1, :], (geo.band, geo.slots))
                for h in range(geo.stack)
            ],
            axis=0,
        )

    def first(g):
        q, k, v = (part(own_ref, i, g) for i in range(3))
        hq, gm = part(hq_ref, 0, g), part(gm_ref, 0, g)
        hg = hgm[:, g * geo.lanes : (g + 1) * geo.lanes]
        qb = [geo.block(q, hq, b) for b in bands]
        gb = [geo.block(gm, hg, b) for b in bands]
        s = [dot_t(geo.stacked(k[at[b]] * BF16(scale), hm), qb[b]) for b in bands]
        dp = [dot_t(geo.stacked(v[at[b]], hm), gb[b]) for b in bands]
        return qb, gb, s, dp

    class_grad(geo, own_ref, cls_ref, gm_ref, hr_ref, hrf_ref, sa_ref, cb_ref, c_ref, acc)
    now = first(0)
    for g in range(geo.groups):
        qb, gb, s, dp = now
        p = [jnp.exp(s[b] + bias_ref[g] + spread(g, b, 0)) for b in bands]
        ds = [(p[b] * (dp[b] + spread(g, b, 16)) * scale).astype(BF16) for b in bands]
        if g + 1 < geo.groups:
            now = first(g + 1)
        lanes = slice(g * geo.lanes, (g + 1) * geo.lanes)
        for b in bands:
            dv_ref[0, at[b], lanes] = geo.unstacked(dot(p[b].astype(BF16), gb[b])).astype(BF16)
            dk_ref[0, at[b], lanes] = geo.unstacked(dot(ds[b], qb[b])).astype(BF16)


def key_grad_call(geo, own, halo, gmx, pieces, *whole):
    G = geo.groups
    mm = 2 * geo.pages * G * geo.bands * 256 * 256 * 256
    out = jax.ShapeDtypeStruct((geo.pages, geo.own, geo.width), BF16)
    return pl.pallas_call(
        functools.partial(key_grad_body, geo),
        out_shape=(out, out, jax.ShapeDtypeStruct((16, 2 * geo.width), BF16)),
        grid=(geo.pages,),
        in_specs=[by_page(own), part_of(halo, 0, geo.width), part_of(halo, 0, 3 * geo.width, 16)]
        + [by_page(a) for a in (gmx,) + pieces]
        + [hold(a.shape) for a in whole],
        out_specs=[by_page(out)] * 2 + [hold((16, 2 * geo.width))],
        scratch_shapes=[
            pltpu.VMEM((geo.halo, geo.width + LANES), BF16),
            pltpu.VMEM((geo.bands, 32, geo.slots), F32),
            pltpu.VMEM((16, 2 * geo.width), F32),
        ],
        compiler_params=params(ROOM),
        cost_estimate=pl.CostEstimate(
            flops=4 * mm, transcendentals=geo.pages * G * geo.bands * 65536, bytes_accessed=20 * MIB
        ),
        name="key_grad",
    )(own, halo, halo, gmx, *pieces, *whole)


def class_close_body(
    geo, mine_ref, parts_ref, cls_ref, x_ref, toh_ref, wout_ref, vec_ref, wup_ref, wdn_ref,
    out_ref, res, n2, acc,
):
    step = pl.program_id(0)
    d, pages = geo.width, geo.pages
    row = lambda i: vec_ref[i : i + 1]
    places = parts_ref.shape[0]

    @pl.when(step == 0)
    def _():
        mine = mine_ref[0]
        q = jnp.concatenate([cls_ref[p, 0:1, 0:d] for p in range(pages)], axis=0).astype(F32)
        k = jnp.concatenate([cls_ref[p, 0:1, d : 2 * d] for p in range(pages)], axis=0).astype(F32)
        v = jnp.concatenate([cls_ref[p, 0:1, 2 * d :] for p in range(pages)], axis=0).astype(F32)
        toh = toh_ref[...]
        own = sum(dot(part, toh) for part in split3(q * k)) * (1.0 / math.sqrt(geo.head))
        tops = [parts_ref[code ^ mine, pages:, 0:LANES] for code in range(places)]
        top = own
        for value in tops:
            top = jnp.maximum(top, value)
        weights = [jnp.exp(value - top) for value in tops] + [jnp.exp(own - top)]
        total = weights[-1]
        for code in range(places):
            total = total + weights[code] * parts_ref[code ^ mine, pages:, LANES : 2 * LANES]
        spread = jnp.concatenate([w / total for w in weights], axis=0)
        spread = sum(dot_t(part, toh) for part in split3(spread))
        mixed = spread[places * pages :] * v
        for code in range(places):
            rows = spread[code * pages : (code + 1) * pages]
            mixed = mixed + rows * parts_ref[code ^ mine, 0:pages, :]
        mixed = mixed.astype(BF16)
        mixed = jnp.concatenate([mixed, jnp.zeros((16 - pages, d), BF16)], axis=0)
        r = x_ref[...].astype(F32) + row(4) * (dot(mixed, wout_ref[...]) + row(3))
        res[...] = r
        unit, _ = norm_parts(r)
        n2[...] = (unit * row(5) + row(6)).astype(BF16)
        acc[...] = jnp.zeros_like(acc)

    h = dot(n2[...], wup_ref[...]) + vec_ref[pl.ds(12 + step, 1), :]
    a = (h * 0.5 * (1.0 + lax.erf(h * math.sqrt(0.5)))).astype(BF16)
    acc[...] += dot(a, wdn_ref[...])

    @pl.when(step == pl.num_programs(0) - 1)
    def _():
        out_ref[...] = (res[...] + row(8) * (acc[...] + row(7))).astype(BF16)[0:pages]


def class_close_call(geo, mine, parts, halo, x, to_head, w_out, vec, w_up, w_down):
    d = geo.width
    ff = w_up.shape[1]
    return pl.pallas_call(
        functools.partial(class_close_body, geo),
        out_shape=jax.ShapeDtypeStruct((geo.pages, d), BF16),
        grid=(ff // d,),
        in_specs=[pl.BlockSpec(memory_space=pltpu.SMEM)]
        + [
            full(parts.shape),
            pl.BlockSpec((geo.pages, 16, 3 * d), lambda c: (0, geo.halo // 16 - 1, 0)),
        ]
        + [full(a.shape) for a in (x, to_head, w_out, vec)]
        + [
            pl.BlockSpec((d, d), lambda c: (0, c)),
            pl.BlockSpec((d, d), lambda c: (c, 0)),
        ],
        out_specs=full((geo.pages, d)),
        scratch_shapes=[
            pltpu.VMEM((16, d), F32),
            pltpu.VMEM((16, d), BF16),
            pltpu.VMEM((16, d), F32),
        ],
        compiler_params=params(ROOM),
        cost_estimate=pl.CostEstimate(
            flops=64 * d * (2 * ff + d), transcendentals=16 * ff, bytes_accessed=12 * MIB
        ),
        name="class_close",
    )(mine, parts, halo, x, to_head, w_out, vec, w_up, w_down)


def by_place(dw, cols, core, half, column, keep_ref, send_ref):
    slab = dw.shape[0] // (4 * cols)
    for mine in range(2):

        @pl.when(core == mine)
        def _():
            for dest in range(4 * cols):
                y, b, c = dest // (2 * cols), dest // cols % 2, dest % cols
                place = (y ^ half) * cols + (c ^ column)
                ref = keep_ref if b == mine else send_ref
                ref[place] = dw[dest * slab : (dest + 1) * slab]


def early_weight_body(
    tile, cols, at_ref, x_ref, att_ref, dq_ref, gb_ref, vec_ref, keep_ref, send_ref, nt_ref, sum_ref,
    left, grad, att, gb, sems,
):
    step = pl.program_id(0)
    n, d = x_ref.shape
    copies = (
        pltpu.make_async_copy(att_ref, att, sems.at[0]),
        pltpu.make_async_copy(gb_ref, gb, sems.at[1]),
    )

    @pl.when(step == 0)
    def _():
        for copy in copies:
            copy.start()

        def one(t, carry):
            rows = pl.ds(pl.multiple_of(t * tile, tile), tile)
            unit, _ = norm_parts(unmask(x_ref[rows, :].astype(F32), vec_ref[0:1]))
            grad[rows, :] = (unit * vec_ref[1:2] + vec_ref[2:3]).astype(BF16)
            return carry

        lax.fori_loop(0, n // tile, one, 0)
        left[...] = grad[...].T
        nt_ref[...] = left[...]
        grad[...] = dq_ref[...]
        total = jnp.sum(dq_ref[...].astype(F32), axis=0, keepdims=True)
        sum_ref[...] = jnp.broadcast_to(total, sum_ref.shape)

    @pl.when(step == 1)
    def _():
        for copy in copies:
            copy.wait()
        left[...] = att[...].T
        grad[...] = gb[...]

    dw = dot(left[...], grad[...]).astype(BF16)
    by_place(dw, cols, at_ref[0], at_ref[1], at_ref[2], keep_ref, send_ref)


def late_weight_body(
    cols, at_ref, nt_ref, dk_ref, dv_ref, c_ref, cg_ref, vec_ref, keep_ref, send_ref, sum_ref, grad,
    sem,
):
    step = pl.program_id(0)
    copy = pltpu.make_async_copy(dv_ref, grad.at[1], sem)
    extra = cg_ref[...]

    @pl.when(step == 0)
    def _():
        copy.start()
        grad[0] = dk_ref[...]

    @pl.when(step == 1)
    def _():
        copy.wait()
        total = jnp.sum(grad[1].astype(F32), axis=0, keepdims=True)
        total = total + jnp.sum(extra.astype(F32), axis=0, keepdims=True)
        sum_ref[...] = jnp.broadcast_to(total, sum_ref.shape)

    unit, _ = norm_parts(c_ref[...].astype(F32))
    left = (unit * vec_ref[1:2] + vec_ref[2:3]).astype(BF16)
    dw = (dot(nt_ref[...], grad[step]) + dot_0(left, extra)).astype(BF16)
    by_place(dw, cols, at_ref[0], at_ref[1], at_ref[2], keep_ref, send_ref)


def weight_call(body, where, cols, ins, in_specs, n, d, more, more_specs, scratch, name):
    slab = d // (4 * cols)
    out = jax.ShapeDtypeStruct((2 * cols, slab, 2 * d), BF16)
    block = pl.BlockSpec((2 * cols, slab, d), lambda i, p: (0, 0, i))
    return pl.pallas_call(
        body,
        out_shape=(out, out) + more,
        grid_spec=pltpu.PrefetchScalarGridSpec(
            num_scalar_prefetch=1,
            grid=(2,),
            in_specs=in_specs,
            out_specs=[block, block] + more_specs,
            scratch_shapes=scratch,
        ),
        compiler_params=params(ROOM),
        cost_estimate=pl.CostEstimate(
            flops=4 * n * d * d, transcendentals=n, bytes_accessed=2 * (5 * n * d + 2 * d * d)
        ),
        name=name,
    )(where, *ins)


def early_weight_call(where, cols, x, att, dq, gb, vec, tile=256):
    n, d = x.shape
    return weight_call(
        functools.partial(early_weight_body, tile, cols), where, cols, (x, att, dq, gb, vec),
        [hold(x.shape), ANYWHERE, hold(dq.shape), ANYWHERE, hold(vec.shape)], n, d,
        (jax.ShapeDtypeStruct((d, n), BF16), jax.ShapeDtypeStruct((8, d), F32)),
        [hold((d, n)), hold((8, d))],
        [pltpu.VMEM((d, n), BF16)]
        + [pltpu.VMEM((n, d), BF16)] * 3
        + [pltpu.SemaphoreType.DMA((2,))],
        "early_weight",
    )


def late_weight_call(where, cols, nt, dk, dv, cls_rows, cls_grad, vec):
    n, d = dk.shape
    ins = (nt, dk, dv, cls_rows)
    return weight_call(
        functools.partial(late_weight_body, cols), where, cols, ins + (cls_grad, vec),
        [hold(nt.shape), hold(dk.shape), ANYWHERE, hold(cls_rows.shape)]
        + [pl.BlockSpec((16, d), lambda i, p: (0, i)), hold(vec.shape)],
        n, d, (jax.ShapeDtypeStruct((8, d), F32),), [hold((8, d))],
        [pltpu.VMEM((2, n, d), BF16), pltpu.SemaphoreType.DMA(())],
        "late_weight",
    )


def fold_body(
    cols, at_ref, k1_ref, r1_ref, k2_ref, r2_ref, own_ref, to_x_ref, to_y_ref, held_x_ref, held_y_ref
):
    d = k1_ref.shape[2] // 2
    add = lambda a, b, lo, hi: (a[:, :, lo:hi].astype(F32) + b[:, :, lo:hi].astype(F32)).astype(BF16)
    one = lambda lo, hi: add(k1_ref, r1_ref, lo, hi)
    two = lambda lo, hi: add(k2_ref, r2_ref, lo, hi)
    h, n = d // 2, cols // 2
    for page in range(2):

        @pl.when(at_ref[3] == page)
        def _():
            for mine in (True, False):
                if (page == 0) == mine:
                    parts = ((one(0, d), 0), (two(0, h), d), (one(d, d + h), d + h))
                else:
                    parts = ((two(h, 2 * d), 0), (one(d + h, 2 * d), d + h))
                for value, lo in parts:
                    at = slice(lo, lo + value.shape[2])
                    near, far = value[:cols], value[cols:]
                    if mine:
                        own_ref[:, :, at] = near
                        to_y_ref[:n, :, at] = far[:n]
                        held_y_ref[:, :, at] = far[n:]
                    else:
                        held_x_ref[:, :, at] = near[:n]
                        to_x_ref[:n, :, at] = near[n:]
                        to_y_ref[n:, :, at] = far[:n]
                        to_x_ref[n:, :, at] = far[n:]


def fold_call(where, cols, keep1, got1, keep2, got2):
    _, slab, d2 = keep1.shape
    out = lambda k: jax.ShapeDtypeStruct((k, slab, d2), BF16)
    sizes = (cols, cols, cols, cols // 2, cols // 2)
    rows = slab // 3
    spec = lambda k: pl.BlockSpec((k, rows, d2), lambda i, p: (0, i, 0))
    return pl.pallas_call(
        functools.partial(fold_body, cols),
        out_shape=tuple(out(k) for k in sizes),
        grid_spec=pltpu.PrefetchScalarGridSpec(
            num_scalar_prefetch=1,
            grid=(3,),
            in_specs=[spec(2 * cols)] * 4,
            out_specs=[spec(k) for k in sizes],
        ),
        compiler_params=params(LESS),
        name="fold",
    )(where, keep1, got1, keep2, got2)


def token_grad_body(
    pages, heads, x_ref, dq_ref, dk_ref, dv_ref, gres_ref, w_ref, c_ref, cg_ref, vec_ref, part_ref,
    mlp_ref, up_ref, table_ref, sq_ref, sv_ref, dt_ref, o_ref,
):
    d = x_ref.shape[1]
    wq, wk, wv = w_ref[:, 0:d], w_ref[:, d : 2 * d], w_ref[:, 2 * d : 3 * d]
    gain = vec_ref[1:2]
    lead = 2 * pages
    at = lead + pages

    @pl.when(pl.program_id(0) == 0)
    def _():
        o_ref[...] = jnp.zeros_like(o_ref)
        unit, inv = norm_parts(c_ref[...].astype(F32))
        gn = dot_t(cg_ref[:, 0:d], wk) + dot_t(cg_ref[:, d : 2 * d], wv)
        o_ref[0:lead] = part_ref[...]
        o_ref[lead:at] = norm_pull(gn * gain, unit, inv)[0:pages]
        o_ref[at + 1 : at + 2] = jnp.sum(gn * unit, axis=0, keepdims=True)
        o_ref[at + 2 : at + 3] = jnp.sum(gn, axis=0, keepdims=True)
        o_ref[at + 3 : at + 4] = sq_ref[0:1]
        o_ref[at + 4 : at + 5] = sv_ref[0:1]
        o_ref[at + 5 : at + 11] = mlp_ref[0:6]
        ups = up_ref.shape[1] // d
        for i in range(ups):
            o_ref[at + 11 + i : at + 12 + i] = up_ref[0:1, i * d : (i + 1) * d]
        for h in range(heads):
            r, c = divmod(h * LANES, d)
            o_ref[at + 11 + ups + r : at + 12 + ups + r, c : c + LANES] = table_ref[h : h + 1]

    raw = x_ref[...].astype(F32)
    masked = raw > FLAG / 2
    unit, inv = norm_parts(jnp.where(masked, vec_ref[0:1], raw))
    gn = dot_t(dq_ref[...], wq) + dot_t(dk_ref[...], wk) + dot_t(dv_ref[...], wv)
    gs = gres_ref[...] + norm_pull(gn * gain, unit, inv)
    dt_ref[...] = jnp.where(masked, 0.0, gs)
    o_ref[at : at + 1] += jnp.sum(jnp.where(masked, gs, 0.0), axis=0, keepdims=True)
    o_ref[at + 1 : at + 2] += jnp.sum(gn * unit, axis=0, keepdims=True)
    o_ref[at + 2 : at + 3] += jnp.sum(gn, axis=0, keepdims=True)


def token_grad_call(pages, heads, rows_in, whole, tile=256):
    n, d = rows_in[0].shape
    up = whole[6]
    count = 3 * pages + 11 + up.shape[1] // d - (-heads * LANES // d)
    height = -(-count // 8) * 8
    rows = pl.BlockSpec((tile, d), lambda i: (i, 0))
    return pl.pallas_call(
        functools.partial(token_grad_body, pages, heads),
        out_shape=(jax.ShapeDtypeStruct((n, d), F32), jax.ShapeDtypeStruct((height, d), F32)),
        grid=(n // tile,),
        in_specs=[rows] * 5 + [hold(a.shape) for a in whole],
        out_specs=[rows, hold((height, d))],
        compiler_params=params(ROOM),
        cost_estimate=pl.CostEstimate(
            flops=2 * n * d * 3 * d, transcendentals=n, bytes_accessed=2 * (8 * n * d + 3 * d * d)
        ),
        name="token_grad",
    )(*rows_in, *whole)


def passed_along(value, axis, steps):
    count = lax.axis_size(axis)
    first, last = max(0, -steps), min(count, count - steps)
    return lax.ppermute(value, axis, [(i, i + steps) for i in range(first, last)])


def swap(value, axis, bit):
    return lax.ppermute(value, axis, [(i, i ^ bit) for i in range(lax.axis_size(axis))])


def halo_pieces(geo, x, filler):
    top = passed_along(x[:, geo.own - geo.edge :], "row", 1)
    bottom = passed_along(x[:, : geo.edge], "row", -1)
    if filler is not None:
        top, bottom, filler = join((top, bottom, filler))
    to_right, to_left = strips_call(geo, x, top, bottom)
    pieces = top, bottom, passed_along(to_right, "col", 1), passed_along(to_left, "col", -1)
    return pieces, filler


def page_sum(part, by):
    return lax.psum_scatter(part, "dp", scatter_dimension=by, tiled=True)


def spread_sum(grad):
    part = lax.psum_scatter(grad, ("row", "col"), scatter_dimension=0, tiled=True)
    return page_sum(part, 1).astype(F32)


def join(values):
    return lax.optimization_barrier(values)


def shards(
    tokens, cls_token, patch_mask, loss_mask, mask_emb, ln1_gain, ln1_bias, w_qkv, q_bias, v_bias,
    rel_table, w_out, out_bias, scale_attn, ln2_gain, ln2_bias, w_up, up_bias, w_down, down_bias,
    scale_mlp, out_grad,
):
    pages, rows, cols, width = tokens.shape
    heads = rel_table.shape[0]
    geo = Geometry(pages, rows, cols, width, heads)
    count = pages * rows * cols
    row_peers, col_peers = lax.axis_size("row"), lax.axis_size("col")
    grid_rows, grid_cols = rows * row_peers, cols * col_peers
    row_at, col_at, page_at = (lax.axis_index(a) for a in ("row", "col", "dp"))

    ups = w_up.shape[1] // width
    vec = jnp.concatenate(
        [
            mask_emb, ln1_gain, ln1_bias, out_bias, scale_attn, ln2_gain, ln2_bias, down_bias,
            scale_mlp, q_bias, jnp.zeros((width,), F32), v_bias, up_bias,
        ]
    ).reshape(12 + ups, width)
    hm = jnp.asarray(geo.head_mask, BF16)
    hr, hrf = jnp.asarray(geo.head_rows, BF16), jnp.asarray(geo.head_rows, F32)
    sm, sa = jnp.asarray(geo.stat_mask, BF16), jnp.asarray(geo.stat_all, BF16)
    to_head, flank = jnp.asarray(geo.to_head, BF16), jnp.asarray(geo.flank_of, BF16)

    at_row = row_at * rows + BAND * np.arange(8)[:, None] - REACH + geo.slot_row[None, :]
    at_col = col_at * cols + geo.slot_col[None, :]
    inside = (at_row >= 0) & (at_row < grid_rows) & (at_col >= 0) & (at_col < grid_cols)
    inside = inside | (np.arange(geo.slots) >= geo.cls_at)[None, :]
    ok = jnp.where(inside, 0.0, NEG).astype(F32)

    masked = (patch_mask == 1)[..., None]
    x = jnp.where(masked, jnp.asarray(FLAG, BF16), tokens).reshape(pages, geo.own, width)
    pieces, _ = halo_pieces(geo, x, None)
    bias_a = bias_table(geo, rel_table, 0)
    own = qkv_call(qkv_own_body, geo.own, (x,), (w_qkv, vec), "qkv_own")
    first = np.arange(16)[:, None] == 0
    cls_block = jnp.where(first, cls_token[:, None, :], jnp.zeros((), BF16))
    halo = qkv_call(
        functools.partial(qkv_halo_body, geo), geo.halo, pieces + (cls_block,),
        (flank, w_qkv, vec), "qkv_halo",
    )
    att, lse, probs, cls_part = attend_call(geo, own, halo, bias_a, ok, hm, hr, hrf)
    att, lse, x = att.reshape(count, width), lse.reshape(count, LANES), x.reshape(count, width)
    counted = (patch_mask * loss_mask == 1)[..., None]
    out_g = jnp.where(counted, out_grad, jnp.zeros((), BF16)).reshape(count, width)
    out, gmx, gres, gb, d_mlp, vg_mlp, d_upb = mlp_call(
        att, x, out_g, lse, w_out, vec, to_head, w_up, w_down, row_peers * col_peers
    )
    d_mlp = lax.psum_scatter(d_mlp, ("row", "col"), scatter_dimension=0, tiled=True)[0]
    gmx = gmx.reshape(pages, geo.own, width + LANES)
    rel_late, _ = join((rel_table, gb))
    pieces, bias_b = halo_pieces(geo, gmx, bias_table(geo, rel_late, 1))
    dq, d_table = query_grad_call(geo, probs, own, halo, gmx, hm, sm)
    class_bias = jnp.concatenate([rel_table[:, SPAN * SPAN], jnp.zeros((16 - heads,), F32)])
    class_bias = jnp.broadcast_to(class_bias[:, None], (16, geo.own))
    cls_rows = jnp.concatenate([cls_token, jnp.zeros((16 - pages, width), BF16)], axis=0)
    direct = (lax.axis_size("dp"), row_peers, col_peers) == (2, 4, 4)
    if direct:
        where = jnp.stack([row_at % 2, row_at // 2, col_at, page_at]).astype(jnp.int32)
    else:
        where = jnp.zeros((4,), jnp.int32)
    dq = dq.reshape(count, width)
    keep1, send1, nt, sum_q = early_weight_call(where, col_peers, x, att, dq, gb, vec)
    pieces, bias_b, nt = join((pieces, bias_b, nt))
    if direct:
        got1 = swap(send1, "row", 1)
    dk, dv, cls_low = key_grad_call(
        geo, own, halo, gmx, pieces, bias_b, ok, hm, sa, flank, hr, hrf, class_bias
    )
    dk, dv = dk.reshape(count, width), dv.reshape(count, width)
    keep2, send2, sum_v = late_weight_call(where, col_peers, nt, dk, dv, cls_rows, cls_low, vec)
    wide = lambda a: a.astype(F32)
    if direct:
        got2 = swap(send2, "row", 1)
        mine, to_x, to_y, held_x, held_y = fold_call(where, col_peers, keep1, got1, keep2, got2)
        mine, dq = join((mine, dq))
        near_x = swap(to_x, "dp", 1)
        near_y = swap(to_y, "row", 2)
    d_tok, block = token_grad_call(
        pages, heads, (x, dq, dk, dv, gres),
        (w_qkv, cls_rows, cls_low, vec, cls_part, vg_mlp, d_upb, d_table, sum_q, sum_v),
    )
    slab = width // (row_peers * col_peers)
    if direct:
        near_x, near_y, block = join((near_x, near_y, block))
        n = col_peers // 2
        last_x = swap((wide(held_x) + wide(near_y[n:])).astype(BF16), "dp", 1)
        last_y = swap((wide(held_y) + wide(near_x[n:])).astype(BF16), "row", 2)
        late = [
            (wide(mine[:n]) + wide(near_y[:n]) + wide(last_x)).astype(BF16),
            (wide(mine[n:]) + wide(near_x[:n]) + wide(last_y)).astype(BF16),
        ]
        late = [a[i] for a in late for i in range(n)]
        up, down = d_mlp[: ups * slab], d_mlp[ups * slab :]
        cut_up, cut_down = ups * slab // 2, width // 2

        def halves(place):
            return jnp.concatenate(
                [
                    lax.dynamic_slice_in_dim(up, place * cut_up, cut_up, 0),
                    lax.dynamic_slice_in_dim(down, place * cut_down, cut_down, 1).reshape(
                        -1, width
                    ),
                ],
                axis=0,
            )

        other = swap(halves(1 - page_at), "dp", 1)

    lead = 2 * pages
    vectors = block[lead:]
    parts, mine_at, place = block[:lead], jnp.zeros((), jnp.int32), 1
    sent = block
    for axis in ("col", "row"):
        peers, rows_in = lax.axis_size(axis), parts.shape[0]
        if direct and axis == "row":
            sent, *late = join((sent, *late))
            beside = [swap(late[step], "col", step) for step in range(1, col_peers)]
        got = [swap(sent, axis, bit) for bit in range(1, peers)]
        level = [vectors] + [g[rows_in:] for g in got]
        while len(level) > 1:
            level = [a + b for a, b in zip(level[0::2], level[1::2])]
        vectors = level[0]
        parts = jnp.concatenate([parts] + [g[:rows_in] for g in got], axis=0)
        mine_at = mine_at + place * lax.axis_index(axis).astype(jnp.int32)
        place = place * peers
        sent = jnp.concatenate([parts, vectors], axis=0)

    if direct:
        beside, parts = join((beside, parts))
    d_cls, v = vectors[:pages], vectors[pages:]
    bit = 1
    while bit < lax.axis_size("dp"):
        v, bit = v + swap(v, "dp", bit), 2 * bit
    out_cls = class_close_call(
        geo, mine_at[None], parts.reshape(-1, 2 * pages, width), halo, cls_rows, to_head, w_out, vec, w_up,
        w_down,
    )

    half = 3 * width // 2
    if direct:
        other, v, out_cls = join((other, v, out_cls))
        late = wide(late[0])
        for part in beside:
            late = late + wide(part)
        d_qkv, d_wout = late[:, :half], late[:, half:]
        both = wide(halves(page_at)) + wide(other)
        d_up = jnp.transpose(both[:cut_up].reshape(-1, slab, width), (1, 0, 2)).reshape(slab, -1)
        d_down = both[cut_up:].reshape(-1, cut_down)
    else:
        def whole(keep, send):
            both = jnp.stack([keep, send]).reshape(2, 2, col_peers, slab, 2 * width)
            return jnp.transpose(both, (1, 0, 2, 3, 4)).reshape(width, 2 * width)

        early, late = whole(keep1, send1), whole(keep2, send2)
        d_qkv = spread_sum(jnp.concatenate([early[:, :width], late], axis=1))
        d_wout = spread_sum(early[:, width:])
        d_up = jnp.transpose(d_mlp[: ups * slab].reshape(ups, slab, width), (1, 0, 2))
        d_up = page_sum(d_up.reshape(slab, ups * width), 1).astype(F32)
        d_down = page_sum(d_mlp[ups * slab :], 1).astype(F32)

    d_rel = v[11 + ups : 13 + ups].reshape(-1)[: heads * LANES].reshape(heads, LANES)[:, : SPAN * SPAN + 1]
    return (
        out.reshape(tokens.shape),
        out_cls,
        d_tok.reshape(tokens.shape),
        d_cls,
        d_qkv,
        d_wout,
        d_up,
        d_down,
        v[0],
        v[1],
        v[2],
        v[3],
        v[4],
        d_rel,
        v[10],
        v[9],
        v[7],
        v[8],
        v[11 : 11 + ups].reshape(-1),
        v[6],
        v[5],
    )


def solution(mesh):
    tile = P("dp", "row", "col", None)
    flat = P("dp", "row", "col")
    weights = P(("row", "col"), "dp")
    return jax.shard_map(
        shards,
        mesh=mesh,
        in_specs=(tile, P("dp", None), flat, flat) + (P(),) * 17 + (tile,),
        out_specs=(tile, P("dp", None), tile, P("dp", None)) + (weights,) * 4 + (P(),) * 13,
        check_vma=False,
    )
```

```python
import functools
import math

import jax
import jax.numpy as jnp
import numpy as np
from jax import lax
from jax.experimental import pallas as pl
from jax.experimental.pallas import tpu as pltpu
from jax.sharding import PartitionSpec as P

F32 = jnp.float32
BF16 = jnp.bfloat16
NEG = -1e30
REACH = 3
SPAN = 7
BAND = 4
SIDE = 8
LANES = 128
FLAG = 1024.0
ROOM, LESS = 56, 28
EPS = 1e-06
MIB = 1 << 20
ANYWHERE = pl.BlockSpec(memory_space=pl.ANY)


def dot(a, b):
    return jnp.dot(a, b, preferred_element_type=F32)


def dot_t(a, b):
    return lax.dot_general(a, b, (((1,), (1,)), ((), ())), preferred_element_type=F32)


def dot_0(a, b):
    return lax.dot_general(a, b, (((0,), (0,)), ((), ())), preferred_element_type=F32)


def split3(x):
    hi = x.astype(BF16)
    rest = x - hi.astype(F32)
    mid = rest.astype(BF16)
    low = (rest - mid.astype(F32)).astype(BF16)
    return hi, mid, low


def norm_parts(x):
    c = x - jnp.mean(x, axis=-1, keepdims=True)
    inv = lax.rsqrt(jnp.mean(c * c, axis=-1, keepdims=True) + EPS)
    return c * inv, inv


def norm_pull(e, unit, inv):
    return inv * (
        e
        - jnp.mean(e, axis=-1, keepdims=True)
        - unit * jnp.mean(e * unit, axis=-1, keepdims=True)
    )


def unmask(x, emb):
    return jnp.where(x > FLAG / 2, emb, x)


class Geometry:
    def __init__(self, pages, rows, cols, width, heads):
        self.pages, self.rows, self.cols = pages, rows, cols
        self.width, self.heads = width, heads
        self.head = width // heads
        self.lanes = 256
        self.stack = self.lanes // self.head
        self.groups = width // self.lanes
        self.own = rows * cols
        self.edge = REACH * cols
        self.side = (rows + 2 * REACH) * SIDE
        self.halo = 2 * self.edge + self.side + 16
        self.bands = rows // BAND
        self.band = BAND * cols
        self.main = (BAND + 2 * REACH) * cols
        self.flank = (BAND + 2 * REACH) * SIDE
        self.slots = self.main + self.flank + 16
        self.cls_at = self.main + self.flank
        slot = np.arange(self.slots)
        r = np.where(slot < self.main, slot // cols, (slot - self.main) // SIDE)
        s = (slot - self.main) % SIDE
        c = np.where(
            slot < self.main,
            slot % cols,
            np.where(s < REACH, s - REACH, np.where(s < 2 * REACH, cols + s - REACH, -1000)),
        )
        is_cls = slot >= self.cls_at
        r = np.where(is_cls, -1000, r)
        c = np.where(is_cls, -1000, c)
        self.slot_row, self.slot_col = r, c
        q = np.arange(self.band)
        a = r[None, :] - (q // cols)[:, None]
        b = c[None, :] - (q % cols)[:, None] + REACH
        ok = (a >= 0) & (a < SPAN) & (b >= 0) & (b < SPAN)
        offset = np.where(ok, a * SPAN + b, -1)
        mirror = np.where(ok, SPAN * SPAN - 1 - offset, -1)
        offset[:, self.cls_at] = SPAN * SPAN
        self.offset = offset.astype(np.int32)
        self.mirror = mirror.astype(np.int32)
        fold = np.full((cols, self.slots), -1, np.int32)
        for i in range(cols):
            for lane in range(SPAN * cols):
                d = lane % cols - i + REACH
                if 0 <= d < SPAN:
                    fold[i, lane] = lane // cols * SPAN + d
            for lane in range(SPAN * SIDE):
                s1 = lane % SIDE
                if s1 < 2 * REACH:
                    col = s1 - REACH if s1 < REACH else cols + s1 - REACH
                    d = col - i + REACH
                    if 0 <= d < SPAN:
                        fold[i, self.main + lane] = lane // SIDE * SPAN + d
            fold[i, self.cls_at] = SPAN * SPAN
        self.fold = fold.T.copy()
        lane = np.arange(self.lanes) // self.head
        self.head_mask = (np.arange(16)[:, None] == lane[None, :]).astype(np.float32)
        stat = np.zeros((self.groups, 8, LANES), np.float32)
        every = np.zeros((32, LANES), np.float32)
        for h in range(heads):
            g, k = divmod(h, self.stack)
            for part in range(3):
                stat[g, k, 48 + 16 * part + h] = -1.0
                every[h, 16 * part + h] = -1.0
                every[16 + h, 48 + 16 * part + h] = -1.0
        self.stat_mask = stat
        self.stat_all = every
        self.to_head = (np.arange(width)[:, None] // self.head == np.arange(LANES)[None, :]).astype(
            np.float32
        )
        self.head_rows = self.to_head.T[:16].copy()
        base = np.full((2, cols, self.slots), -1, np.int32)
        for i in range(cols):
            for lane in range(self.slots):
                o = fold[i, lane]
                base[0, i, lane] = o
                base[1, i, lane] = SPAN * SPAN - 1 - o if 0 <= o < SPAN * SPAN else -1
        self.base = base
        tall = rows + 2 * REACH
        self.strip = -(-REACH * tall // 8) * 8
        flank = np.zeros((2, self.side, self.strip), np.float32)
        for r in range(tall):
            for i in range(REACH):
                flank[0, r * SIDE + i, r * REACH + i] = 1.0
                flank[1, r * SIDE + REACH + i, r * REACH + i] = 1.0
        self.flank_of = flank

    def block(self, own, halo, b):
        lo, hi = b * self.band, b * self.band + self.main
        e, o = self.edge, self.own
        parts = []
        if lo < e:
            parts.append(halo[lo : min(hi, e)])
        parts.append(own[max(lo - e, 0) : min(hi - e, o)])
        if hi > e + o:
            parts.append(halo[e + max(lo - e - o, 0) : e + hi - e - o])
        at = 2 * e + b * BAND * SIDE
        parts.append(halo[at : at + self.flank])
        parts.append(halo[2 * e + self.side : 2 * e + self.side + 16])
        return jnp.concatenate(parts, axis=0)

    def around(self, top, bottom, left, right, flank, last):
        side = dot(flank[0], left) + dot(flank[1], right)
        return jnp.concatenate([top, bottom, side.astype(BF16), last], axis=0)

    def stacked(self, x, mask):
        return jnp.concatenate([x * mask[h : h + 1] for h in range(self.stack)], axis=0)

    def unstacked(self, r):
        rows = r.shape[0] // self.stack
        lane = lax.broadcasted_iota(jnp.int32, (rows, self.lanes), 1) // self.head
        out = r[(self.stack - 1) * rows :]
        for h in range(self.stack - 1):
            out = jnp.where(lane == h, r[h * rows : (h + 1) * rows], out)
        return out


def full(shape):
    return pl.BlockSpec(shape, lambda *_: (0,) * len(shape))


def hold(shape):
    return pl.BlockSpec(shape, lambda *_: (0,) * len(shape), pipeline_mode=pl.Buffered(1))


def params(limit, sem=1):
    return pltpu.CompilerParams(
        dimension_semantics=("arbitrary",) * sem, vmem_limit_bytes=limit * MIB
    )


def bias_body(geo, table, index_ref, out_ref):
    lane = lax.broadcasted_iota(jnp.int32, (geo.cols, geo.slots), 1)
    low = jnp.full((geo.cols, geo.slots), NEG, F32)
    index = index_ref[...]
    pair = 2

    def head(i, carry):
        acc = [low] * (2 * pair)
        for o in range(SPAN * SPAN + 1):
            hit = index == o
            for j in range(pair):
                at = 2 * j + o % 2
                acc[at] = jnp.where(hit, table[i * pair + j, o], acc[at])
        for j in range(pair):
            both = jnp.maximum(acc[2 * j], acc[2 * j + 1])
            main = jnp.where(lane < geo.main, both, low)
            side = jnp.where((lane >= geo.main) & (lane < geo.cls_at), both, low)
            last = jnp.where(lane >= geo.cls_at, both, low)
            h = i * pair + j
            for r in range(BAND):
                if r:
                    both = jnp.maximum(
                        pltpu.roll(main, r * geo.cols, 1), pltpu.roll(side, r * SIDE, 1)
                    )
                else:
                    both = jnp.maximum(main, side)
                at = pl.multiple_of(h % geo.stack * geo.band + r * geo.cols, 8)
                out_ref[h // geo.stack, pl.ds(at, geo.cols), :] = jnp.maximum(both, last)
        return carry

    lax.fori_loop(0, geo.heads // pair, head, 0)


def bias_table(geo, rel_table, which):
    return pl.pallas_call(
        functools.partial(bias_body, geo),
        out_shape=jax.ShapeDtypeStruct((geo.groups, geo.stack * geo.band, geo.slots), F32),
        in_specs=[
            pl.BlockSpec(memory_space=pltpu.SMEM),
            pl.BlockSpec(memory_space=pltpu.VMEM),
        ],
        out_specs=pl.BlockSpec(memory_space=pltpu.VMEM),
        compiler_params=pltpu.CompilerParams(vmem_limit_bytes=ROOM * MIB),
        name="bias_table",
    )(rel_table, jnp.asarray(geo.base[which]))


def qkv_rows(pages, w_ref, vec_ref, o_ref):
    d = pages[0].shape[1]

    def normed(raw):
        unit, _ = norm_parts(unmask(raw.astype(F32), vec_ref[0:1]))
        return (unit * vec_ref[1:2] + vec_ref[2:3]).astype(BF16)

    now = normed(pages[0])
    for k in range(len(pages)):
        rows = dot(now, w_ref[...])
        if k + 1 < len(pages):
            now = normed(pages[k + 1])
        for i in range(3):
            cols = slice(i * d, (i + 1) * d)
            o_ref[k, :, cols] = (rows[:, cols] + vec_ref[9 + i : 10 + i]).astype(BF16)


def qkv_own_body(x_ref, w_ref, vec_ref, o_ref):
    span = x_ref.shape[0]
    qkv_rows([x_ref[k] for k in range(span)], w_ref, vec_ref, o_ref)


def qkv_halo_body(geo, top_ref, bottom_ref, left_ref, right_ref, last_ref, flank_ref, w_ref, vec_ref, o_ref):
    span = top_ref.shape[0]
    raw = [
        geo.around(
            top_ref[k], bottom_ref[k], left_ref[k], right_ref[k], flank_ref[...], last_ref[k]
        )
        for k in range(span)
    ]
    qkv_rows(raw, w_ref, vec_ref, o_ref)


def part_of(a, i, d, rows=None):
    rows = rows or a.shape[1]
    return pl.BlockSpec((1, rows, d), lambda p: (p, a.shape[1] // rows - 1, i))


def by_page(a, span=1):
    return pl.BlockSpec((span,) + a.shape[1:], lambda p: (p,) + (0,) * (len(a.shape) - 1))


def qkv_call(body, rows, paged, whole, name):
    pages, _, d = paged[0].shape
    span = 2 if pages % 2 == 0 else 1
    n = pages * rows
    return pl.pallas_call(
        body,
        out_shape=jax.ShapeDtypeStruct((pages, rows, 3 * d), BF16),
        grid=(pages // span,),
        in_specs=[by_page(a, span) for a in paged] + [hold(a.shape) for a in whole],
        out_specs=pl.BlockSpec((span, rows, 3 * d), lambda p: (p, 0, 0)),
        compiler_params=params(ROOM),
        cost_estimate=pl.CostEstimate(
            flops=6 * n * d * d, transcendentals=n, bytes_accessed=2 * (4 * n * d + 3 * d * d)
        ),
        name=name,
    )(*paged, *whole)


def strips_body(geo, x_ref, top_ref, bottom_ref, right_ref, left_ref, tall, near):
    e, o = geo.edge, geo.own
    near[...] = jnp.zeros_like(near)

    def page(p, carry):
        tall[0:e, :] = top_ref[p].astype(F32)
        tall[e : e + o, :] = x_ref[p].astype(F32)
        tall[e + o :, :] = bottom_ref[p].astype(F32)
        for r in range(geo.rows + 2 * REACH):
            to, at = r * REACH, r * geo.cols
            near[0, to : to + REACH, :] = tall[at + geo.cols - REACH : at + geo.cols, :]
            near[1, to : to + REACH, :] = tall[at : at + REACH, :]
        right_ref[p] = near[0].astype(BF16)
        left_ref[p] = near[1].astype(BF16)
        return carry

    lax.fori_loop(0, geo.pages, page, 0)


def strips_call(geo, x, top, bottom):
    width = x.shape[2]
    shape = jax.ShapeDtypeStruct((geo.pages, geo.strip, width), BF16)
    return pl.pallas_call(
        functools.partial(strips_body, geo),
        out_shape=(shape, shape),
        scratch_shapes=[
            pltpu.VMEM((2 * geo.edge + geo.own, width), F32),
            pltpu.VMEM((2, geo.strip, width), F32),
        ],
        compiler_params=pltpu.CompilerParams(vmem_limit_bytes=ROOM * MIB),
        name="strips",
    )(x, top, bottom)


def class_part(geo, own_ref, cq_ref, hr_ref, hrf_ref, o_ref):
    page, d = pl.program_id(0), geo.width

    @pl.when(page == 0)
    def _():
        o_ref[...] = jnp.zeros_like(o_ref)

    scale = BF16(1.0 / math.sqrt(geo.head))
    hr, hrf = hr_ref[...], hrf_ref[...]
    qc = jnp.broadcast_to(cq_ref[0, 0:1, :] * scale, (16, d)) * hr
    s = dot_t(qc, own_ref[0, :, d : 2 * d])
    top = jnp.max(s, axis=-1, keepdims=True)
    e = jnp.exp(s - top)
    total = jnp.sum(e, axis=-1, keepdims=True)
    acc = dot(jnp.concatenate(split3(e), axis=0), own_ref[0, :, 2 * d : 3 * d])
    acc = acc[0:16] + acc[16:32] + acc[32:48]
    o_ref[pl.ds(page, 1), :] = jnp.sum(acc * hrf, axis=0, keepdims=True)
    row = lax.broadcasted_iota(jnp.int32, (16, LANES), 0)
    diag = row == lax.broadcasted_iota(jnp.int32, (16, LANES), 1)
    stats = [jnp.sum(jnp.where(diag, a, 0.0), axis=0, keepdims=True) for a in (top, total)]
    stats.append(jnp.zeros((1, d - 2 * LANES), F32))
    o_ref[pl.ds(geo.pages + page, 1), :] = jnp.concatenate(stats, axis=1)


def attend_body(
    geo, own_ref, hk_ref, hv_ref, cq_ref, bias_ref, ok_ref, hm_ref, hr_ref, hrf_ref, o_ref, lse_ref,
    p_ref, c_ref,
):
    scale = BF16(1.0 / math.sqrt(geo.head))
    hm = hm_ref[...]
    lane = lax.broadcasted_iota(jnp.int32, (geo.band, LANES), 1)
    bands = range(geo.bands)
    at = [slice(b * geo.band, (b + 1) * geo.band) for b in bands]
    lses = [jnp.zeros((geo.band, LANES), F32) for _ in bands]

    def part(ref, which, g):
        lo = which * geo.width + g * geo.lanes
        return ref[0, :, lo : lo + geo.lanes]

    def score(g):
        q, k, hk = part(own_ref, 0, g), part(own_ref, 1, g), part(hk_ref, 0, g)
        return [
            dot_t(geo.stacked(q[at[b]] * scale, hm), geo.block(k, hk, b))
            + bias_ref[g]
            + ok_ref[b : b + 1]
            for b in bands
        ]

    def soften(g, scores):
        probs = []
        for b in bands:
            top = jnp.max(scores[b], axis=-1, keepdims=True)
            e = jnp.exp(scores[b] - top)
            total = jnp.sum(e, axis=-1, keepdims=True)
            lse = top + jnp.log(total)
            for h in range(geo.stack):
                rows = slice(h * geo.band, (h + 1) * geo.band)
                lses[b] = jnp.where(lane == g * geo.stack + h, lse[rows], lses[b])
            p = (e * (1.0 / total)).astype(BF16)
            p_ref[0, g, b] = p
            probs.append(p)
        return probs

    def mix(g, probs):
        v, hv = part(own_ref, 2, g), part(hv_ref, 0, g)
        for b in bands:
            rows = geo.unstacked(dot(probs[b], geo.block(v, hv, b)))
            o_ref[0, at[b], g * geo.lanes : (g + 1) * geo.lanes] = rows.astype(BF16)

    class_part(geo, own_ref, cq_ref, hr_ref, hrf_ref, c_ref)
    scores = score(0)
    for g in range(geo.groups):
        probs = soften(g, scores)
        if g + 1 < geo.groups:
            scores = score(g + 1)
        mix(g, probs)
    for b in bands:
        lse_ref[0, at[b], :] = lses[b]


def attend_call(geo, own, halo, bias, ok, hm, hr, hrf):
    G = geo.groups
    mm = 2 * geo.pages * G * geo.bands * 256 * 256 * 256
    outs = (
        jax.ShapeDtypeStruct((geo.pages, geo.own, geo.width), BF16),
        jax.ShapeDtypeStruct((geo.pages, geo.own, LANES), F32),
        jax.ShapeDtypeStruct((geo.pages, G, geo.bands, geo.lanes, geo.slots), BF16),
        jax.ShapeDtypeStruct((2 * geo.pages, geo.width), F32),
    )
    return pl.pallas_call(
        functools.partial(attend_body, geo),
        out_shape=outs,
        grid=(geo.pages,),
        in_specs=[by_page(own)]
        + [part_of(halo, i, geo.width) for i in (1, 2)]
        + [part_of(halo, 0, geo.width, 16)]
        + [hold(a.shape) for a in (bias, ok, hm, hr, hrf)],
        out_specs=[by_page(a) for a in outs[:3]] + [hold((2 * geo.pages, geo.width))],
        compiler_params=params(ROOM),
        cost_estimate=pl.CostEstimate(
            flops=2 * mm, transcendentals=geo.pages * G * geo.bands * 65536, bytes_accessed=16 * MIB
        ),
        name="attend",
    )(own, halo, halo, halo, bias, ok, hm, hr, hrf)


def hidden_body(
    tile, steps, att_ref, x_ref, og_ref, wout_ref, vec_ref, wup_ref, wdn_ref,
    act_ref, dh_ref, dw_ref, dub_ref, n2, n2t, gm, up_buf, dn_buf, sems,
):
    step = pl.program_id(0)
    n, d = n2.shape
    row = lambda i: vec_ref[i : i + 1]
    tiles = n // tile
    dests, rows_up, _ = up_buf.shape
    few, rows_dn, _ = dn_buf.shape

    @pl.when(step == 0)
    def _():
        def one(t, carry):
            rows = pl.ds(pl.multiple_of(t * tile, tile), tile)
            x = unmask(x_ref[rows, :].astype(F32), row(0))
            unit, _ = norm_parts(x + row(4) * (dot(att_ref[rows, :], wout_ref[...]) + row(3)))
            n2[rows, :] = (unit * row(5) + row(6)).astype(BF16)
            gm[rows, :] = (row(8) * og_ref[rows, :].astype(F32)).astype(BF16)
            return carry

        lax.fori_loop(0, tiles, one, 0)
        n2t[...] = n2[...].T

    wup, wdn = wup_ref[...], wdn_ref[...]
    upb = vec_ref[pl.ds(12 + step, 1), :]

    def one(t, total):
        rows = pl.ds(pl.multiple_of(t * tile, tile), tile)
        h = dot(n2[rows, :], wup) + upb
        da = dot_t(gm[rows, :], wdn)
        cdf = 0.5 * (1.0 + lax.erf(h * math.sqrt(0.5)))
        pdf = jnp.exp(-0.5 * h * h) * (1.0 / math.sqrt(2.0 * math.pi))
        act_ref[rows, :] = (h * cdf).astype(BF16)
        g = (da * (cdf + h * pdf)).astype(BF16)
        dh_ref[rows, :] = g
        return total + jnp.sum(g.astype(F32), axis=0, keepdims=True)

    total = lax.fori_loop(0, tiles, one, jnp.zeros((1, wup.shape[1]), F32))
    dub_ref[...] = jnp.broadcast_to(total, dub_ref.shape)

    def copies(c):
        at = pl.multiple_of(c * rows_up, 8)
        return (
            pltpu.make_async_copy(up_buf, dw_ref.at[:, pl.ds(at, rows_up), :], sems.at[0]),
            pltpu.make_async_copy(
                dn_buf,
                dw_ref.at[pl.ds(c * few, few), steps * rows_up : steps * rows_up + rows_dn, :],
                sems.at[1],
            ),
        )

    @pl.when(step > 0)
    def _():
        for copy in copies(step - 1):
            copy.wait()

    up_buf[...] = dot(n2t[...], dh_ref[...]).astype(BF16).reshape(up_buf.shape)
    dn_buf[...] = dot_0(act_ref[...], gm[...]).astype(BF16).reshape(dn_buf.shape)
    for copy in copies(step):
        copy.start()

    @pl.when(step == steps - 1)
    def _():
        for copy in copies(step):
            copy.wait()


def hidden_call(att, x, og, w_out, vec, w_up, w_down, dests, tile=512):
    n, d = x.shape
    ff = w_up.shape[1]
    steps = ff // d
    rows_up, rows_dn = d // dests, ff // dests
    return pl.pallas_call(
        functools.partial(hidden_body, tile, steps),
        out_shape=(
            jax.ShapeDtypeStruct((n, ff), BF16),
            jax.ShapeDtypeStruct((n, ff), BF16),
            jax.ShapeDtypeStruct((dests, steps * rows_up + rows_dn, d), BF16),
            jax.ShapeDtypeStruct((8, ff), F32),
        ),
        grid=(steps,),
        in_specs=[hold((n, d))] * 3
        + [
            hold((d, d)),
            hold(vec.shape),
            pl.BlockSpec((d, d), lambda c: (0, c)),
            pl.BlockSpec((d, d), lambda c: (c, 0)),
        ],
        out_specs=[
            pl.BlockSpec((n, d), lambda c: (0, c)),
            pl.BlockSpec((n, d), lambda c: (0, c)),
            pl.BlockSpec(memory_space=pl.ANY),
            pl.BlockSpec((8, d), lambda c: (0, c)),
        ],
        scratch_shapes=[
            pltpu.VMEM((n, d), BF16),
            pltpu.VMEM((d, n), BF16),
            pltpu.VMEM((n, d), BF16),
            pltpu.VMEM((dests, rows_up, d), BF16),
            pltpu.VMEM((dests // steps, rows_dn, d), BF16),
            pltpu.SemaphoreType.DMA((2,)),
        ],
        compiler_params=params(ROOM),
        cost_estimate=pl.CostEstimate(
            flops=2 * n * d * (4 * ff + d),
            transcendentals=2 * n * ff,
            bytes_accessed=2 * (4 * d * ff + 2 * n * ff + 3 * n * d),
        ),
        name="hidden",
    )(att, x, og, w_out, vec, w_up, w_down)


def close_body(
    att_ref, x_ref, og_ref, lse_ref, act_ref, dh_ref, wout_ref, vec_ref, wup_ref, wdn_ref, toh_ref,
    out_ref, gmx_ref, gres_ref, gb_ref, vg_ref,
):
    step = pl.program_id(0)
    d = x_ref.shape[1]
    row = lambda i: vec_ref[i : i + 1]

    @pl.when(step == 0)
    def _():
        vg_ref[...] = jnp.zeros_like(vg_ref)

    def add(i, v):
        vg_ref[i : i + 1] += jnp.sum(v, axis=0, keepdims=True)

    att = att_ref[...]
    br = dot(att, wout_ref[...]) + row(3)
    res = unmask(x_ref[...].astype(F32), row(0)) + row(4) * br
    og = og_ref[...].astype(F32)
    mo = dot(act_ref[...], wdn_ref[...]) + row(7)
    out_ref[...] = (res + row(8) * mo).astype(BF16)
    add(0, og * mo)
    add(1, (row(8) * og).astype(BF16).astype(F32))
    unit, inv = norm_parts(res)
    gn = dot_t(dh_ref[...], wup_ref[...])
    add(2, gn * unit)
    add(3, gn)
    gr = og + norm_pull(gn * row(5), unit, inv)
    gres_ref[...] = gr
    add(4, gr * br)
    gb = (row(4) * gr).astype(BF16)
    add(5, gb.astype(F32))
    gb_ref[...] = gb
    mix = dot_t(gb, wout_ref[...]).astype(BF16)
    gmx_ref[:, 0:d] = mix
    prod = mix.astype(F32) * att.astype(F32)
    toh = toh_ref[...]
    delta = sum(dot(part, toh) for part in split3(prod))
    packed = jnp.zeros(delta.shape, F32)
    for i, part in enumerate(split3(lse_ref[...]) + split3(delta)):
        part = part.astype(F32)
        packed += part if i == 0 else pltpu.roll(part, 16 * i, 1)
    gmx_ref[:, d : d + LANES] = packed.astype(BF16)


def close_call(att, x, og, lse, act, dh, w_out, vec, w_up, w_down, to_head, tile=256):
    n, d = x.shape
    ff = w_up.shape[1]
    rows = lambda width: pl.BlockSpec((tile, width), lambda i: (i, 0))
    return pl.pallas_call(
        close_body,
        out_shape=(
            jax.ShapeDtypeStruct((n, d), BF16),
            jax.ShapeDtypeStruct((n, d + LANES), BF16),
            jax.ShapeDtypeStruct((n, d), F32),
            jax.ShapeDtypeStruct((n, d), BF16),
            jax.ShapeDtypeStruct((8, d), F32),
        ),
        grid=(n // tile,),
        in_specs=[rows(d), rows(d), rows(d), rows(LANES), rows(ff), rows(ff)]
        + [hold(a.shape) for a in (w_out, vec, w_up, w_down, to_head)],
        out_specs=[rows(d), rows(d + LANES), rows(d), rows(d), hold((8, d))],
        compiler_params=params(ROOM),
        cost_estimate=pl.CostEstimate(
            flops=2 * n * d * (2 * ff + 3 * d),
            transcendentals=n,
            bytes_accessed=2 * (2 * d * ff + 2 * n * ff + 8 * n * d),
        ),
        name="close",
    )(att, x, og, lse, act, dh, w_out, vec, w_up, w_down, to_head)


def table_sums(geo, acc_ref, fold_ref, o_ref):
    lane = lax.broadcasted_iota(jnp.int32, (geo.cols, geo.slots), 1)
    heads = []
    for g in range(geo.groups):
        for h in range(geo.stack):
            x = acc_ref[g, h * geo.band : (h + 1) * geo.band, :]
            parts = [x[i * geo.cols : (i + 1) * geo.cols] for i in range(BAND)]
            main, side, plain = parts[0], parts[0], parts[0]
            for i in range(1, BAND):
                main = main + pltpu.roll(parts[i], geo.slots - i * geo.cols, 1)
                side = side + pltpu.roll(parts[i], geo.slots - i * SIDE, 1)
                plain = plain + parts[i]
            z = jnp.where(lane < SPAN * geo.cols, main, jnp.where(lane < geo.cls_at, side, plain))
            heads.append(z)
    pad = [jnp.zeros((geo.cols, geo.slots), F32)] * (16 - geo.heads)
    z = jnp.stack(heads + pad, axis=0)
    total = jnp.zeros((16, LANES), F32)
    which = lax.broadcasted_iota(jnp.int32, (geo.slots, LANES), 1)
    for i in range(geo.cols):
        pick = jnp.where(fold_ref[:, i : i + 1] == which, 1.0, 0.0).astype(BF16)
        for part in split3(z[:, i, :]):
            total += dot(part, pick)
    o_ref[...] = total


def query_grad_body(
    geo, p_ref, k_ref, v_ref, hk_ref, hv_ref, gm_ref, hm_ref, sm_ref, fold_ref, dq_ref, table_ref,
    rel_ref,
):
    scale = 1.0 / math.sqrt(geo.head)
    hm = hm_ref[...]
    bands = range(geo.bands)
    at = [slice(b * geo.band, (b + 1) * geo.band) for b in bands]
    ones = jnp.ones((geo.slots, LANES), BF16)
    join = lambda a, b: jnp.concatenate([a, b], axis=1)
    st = gm_ref[0, :, geo.width :]

    @pl.when(pl.program_id(0) == 0)
    def _():
        rel_ref[...] = jnp.zeros_like(rel_ref)

    def part(ref, which, g):
        lo = which * geo.width + g * geo.lanes
        return ref[0, :, lo : lo + geo.lanes]

    def pull(g):
        gm, v, hv = part(gm_ref, 0, g), part(v_ref, 0, g), part(hv_ref, 0, g)
        sm = sm_ref[g]
        return [
            dot_t(
                join(geo.stacked(gm[at[b]], hm), geo.stacked(st[at[b]], sm)),
                join(geo.block(v, hv, b), ones),
            )
            for b in bands
        ]

    dp = pull(0)
    for g in range(geo.groups):
        ds = [p_ref[0, g, b].astype(F32) * dp[b] for b in bands]
        if g + 1 < geo.groups:
            dp = pull(g + 1)
        total = ds[0]
        for d in ds[1:]:
            total = total + d
        rel_ref[g] += total
        k, hk = part(k_ref, 0, g), part(hk_ref, 0, g)
        for b in bands:
            rows = geo.unstacked(dot((ds[b] * scale).astype(BF16), geo.block(k, hk, b)))
            dq_ref[0, at[b], g * geo.lanes : (g + 1) * geo.lanes] = rows.astype(BF16)

    @pl.when(pl.program_id(0) == geo.pages - 1)
    def _():
        table_sums(geo, rel_ref, fold_ref, table_ref)


def query_grad_call(geo, probs, own, halo, gmx, hm, sm):
    G = geo.groups
    mm = 2 * geo.pages * G * geo.bands * 256 * 256 * 256
    dq = jax.ShapeDtypeStruct((geo.pages, geo.own, geo.width), BF16)
    table = jax.ShapeDtypeStruct((16, LANES), F32)
    fold = jnp.asarray(geo.fold)
    return pl.pallas_call(
        functools.partial(query_grad_body, geo),
        out_shape=(dq, table),
        grid=(geo.pages,),
        in_specs=[by_page(probs)]
        + [part_of(a, i, geo.width) for a in (own, halo) for i in (1, 2)]
        + [by_page(gmx)]
        + [hold(a.shape) for a in (hm, sm, fold)],
        out_specs=[by_page(dq), hold(table.shape)],
        scratch_shapes=[pltpu.VMEM((geo.groups, geo.stack * geo.band, geo.slots), F32)],
        compiler_params=params(ROOM),
        cost_estimate=pl.CostEstimate(
            flops=2 * mm, transcendentals=0, bytes_accessed=20 * MIB
        ),
        name="query_grad",
    )(probs, own, own, halo, halo, gmx, hm, sm, fold)


def class_grad(geo, own_ref, cls_ref, gm_ref, hr_ref, hrf_ref, sa_ref, cb_ref, o_ref, acc):
    page, d = pl.program_id(0), geo.width

    @pl.when(page == 0)
    def _():
        acc[...] = jnp.zeros_like(acc)

    scale = 1.0 / math.sqrt(geo.head)
    hr, hrf, sa = hr_ref[...], hrf_ref[...], sa_ref[...]
    q, gm, st = own_ref[0, :, 0:d], gm_ref[0, :, 0:d], gm_ref[0, :, d:]
    kc = jnp.broadcast_to(cls_ref[0, 0:1, d : 2 * d] * BF16(scale), (16, d)) * hr
    vc = jnp.broadcast_to(cls_ref[0, 0:1, 2 * d : 3 * d], (16, d)) * hr
    prob = jnp.exp(dot_t(kc, q) + dot_t(sa[0:16], st) + cb_ref[...])
    ds = prob * (dot_t(vc, gm) + dot_t(sa[16:32], st))
    row = pl.ds(page, 1)
    dk = dot((ds * scale).astype(BF16), q)
    dv = dot(prob.astype(BF16), gm)
    acc[row, 0:d] = jnp.sum(dk * hrf, axis=0, keepdims=True)
    acc[row, d : 2 * d] = jnp.sum(dv * hrf, axis=0, keepdims=True)

    @pl.when(page == geo.pages - 1)
    def _():
        o_ref[...] = acc[...].astype(BF16)


def key_grad_body(
    geo, own_ref, hq_ref, cls_ref, gm_ref, top_ref, bottom_ref, left_ref, right_ref,
    bias_ref, ok_ref, hm_ref, sa_ref, flank_ref, hr_ref, hrf_ref, cb_ref, dk_ref, dv_ref, c_ref,
    hgm, rowstat, acc,
):
    scale = 1.0 / math.sqrt(geo.head)
    hm = hm_ref[...]
    bands = range(geo.bands)
    at = [slice(b * geo.band, (b + 1) * geo.band) for b in bands]
    last = jnp.zeros((16, gm_ref.shape[2]), BF16)
    hgm[...] = geo.around(
        top_ref[0], bottom_ref[0], left_ref[0], right_ref[0], flank_ref[...], last
    )
    stats, own = hgm[:, geo.width :], gm_ref[0, :, geo.width :]
    row = lax.broadcasted_iota(jnp.int32, (32, geo.slots), 0)
    for b in bands:
        r = dot_t(sa_ref[...], geo.block(own, stats, b))
        rowstat[b] = r + jnp.where(row < 16, ok_ref[b : b + 1], 0.0)

    def part(ref, which, g):
        lo = which * geo.width + g * geo.lanes
        return ref[0, :, lo : lo + geo.lanes]

    def spread(g, b, first):
        at = first + g * geo.stack
        return jnp.concatenate(
            [
                jnp.broadcast_to(rowstat[b, at + h : at + h + 1, :], (geo.band, geo.slots))
                for h in range(geo.stack)
            ],
            axis=0,
        )

    def first(g):
        q, k, v = (part(own_ref, i, g) for i in range(3))
        hq, gm = part(hq_ref, 0, g), part(gm_ref, 0, g)
        hg = hgm[:, g * geo.lanes : (g + 1) * geo.lanes]
        qb = [geo.block(q, hq, b) for b in bands]
        gb = [geo.block(gm, hg, b) for b in bands]
        s = [dot_t(geo.stacked(k[at[b]] * BF16(scale), hm), qb[b]) for b in bands]
        dp = [dot_t(geo.stacked(v[at[b]], hm), gb[b]) for b in bands]
        return qb, gb, s, dp

    class_grad(geo, own_ref, cls_ref, gm_ref, hr_ref, hrf_ref, sa_ref, cb_ref, c_ref, acc)
    now = first(0)
    for g in range(geo.groups):
        qb, gb, s, dp = now
        p = [jnp.exp(s[b] + bias_ref[g] + spread(g, b, 0)) for b in bands]
        ds = [(p[b] * (dp[b] + spread(g, b, 16)) * scale).astype(BF16) for b in bands]
        if g + 1 < geo.groups:
            now = first(g + 1)
        lanes = slice(g * geo.lanes, (g + 1) * geo.lanes)
        for b in bands:
            dv_ref[0, at[b], lanes] = geo.unstacked(dot(p[b].astype(BF16), gb[b])).astype(BF16)
            dk_ref[0, at[b], lanes] = geo.unstacked(dot(ds[b], qb[b])).astype(BF16)


def key_grad_call(geo, own, halo, gmx, pieces, *whole):
    G = geo.groups
    mm = 2 * geo.pages * G * geo.bands * 256 * 256 * 256
    out = jax.ShapeDtypeStruct((geo.pages, geo.own, geo.width), BF16)
    return pl.pallas_call(
        functools.partial(key_grad_body, geo),
        out_shape=(out, out, jax.ShapeDtypeStruct((16, 2 * geo.width), BF16)),
        grid=(geo.pages,),
        in_specs=[by_page(own), part_of(halo, 0, geo.width), part_of(halo, 0, 3 * geo.width, 16)]
        + [by_page(a) for a in (gmx,) + pieces]
        + [hold(a.shape) for a in whole],
        out_specs=[by_page(out)] * 2 + [hold((16, 2 * geo.width))],
        scratch_shapes=[
            pltpu.VMEM((geo.halo, geo.width + LANES), BF16),
            pltpu.VMEM((geo.bands, 32, geo.slots), F32),
            pltpu.VMEM((16, 2 * geo.width), F32),
        ],
        compiler_params=params(36),
        cost_estimate=pl.CostEstimate(
            flops=4 * mm, transcendentals=geo.pages * G * geo.bands * 65536, bytes_accessed=20 * MIB
        ),
        name="key_grad",
    )(own, halo, halo, gmx, *pieces, *whole)


def class_close_body(
    geo, mine_ref, parts_ref, cls_ref, x_ref, toh_ref, wout_ref, vec_ref, wup_ref, wdn_ref,
    out_ref, res, n2, acc,
):
    step = pl.program_id(0)
    d, pages = geo.width, geo.pages
    row = lambda i: vec_ref[i : i + 1]
    places = parts_ref.shape[0]

    @pl.when(step == 0)
    def _():
        mine = mine_ref[0]
        q = jnp.concatenate([cls_ref[p, 0:1, 0:d] for p in range(pages)], axis=0).astype(F32)
        k = jnp.concatenate([cls_ref[p, 0:1, d : 2 * d] for p in range(pages)], axis=0).astype(F32)
        v = jnp.concatenate([cls_ref[p, 0:1, 2 * d :] for p in range(pages)], axis=0).astype(F32)
        toh = toh_ref[...]
        own = sum(dot(part, toh) for part in split3(q * k)) * (1.0 / math.sqrt(geo.head))
        tops = [parts_ref[code ^ mine, pages:, 0:LANES] for code in range(places)]
        top = own
        for value in tops:
            top = jnp.maximum(top, value)
        weights = [jnp.exp(value - top) for value in tops] + [jnp.exp(own - top)]
        total = weights[-1]
        for code in range(places):
            total = total + weights[code] * parts_ref[code ^ mine, pages:, LANES : 2 * LANES]
        spread = jnp.concatenate([w / total for w in weights], axis=0)
        spread = sum(dot_t(part, toh) for part in split3(spread))
        mixed = spread[places * pages :] * v
        for code in range(places):
            rows = spread[code * pages : (code + 1) * pages]
            mixed = mixed + rows * parts_ref[code ^ mine, 0:pages, :]
        mixed = mixed.astype(BF16)
        mixed = jnp.concatenate([mixed, jnp.zeros((16 - pages, d), BF16)], axis=0)
        r = x_ref[...].astype(F32) + row(4) * (dot(mixed, wout_ref[...]) + row(3))
        res[...] = r
        unit, _ = norm_parts(r)
        n2[...] = (unit * row(5) + row(6)).astype(BF16)
        acc[...] = jnp.zeros_like(acc)

    h = dot(n2[...], wup_ref[...]) + vec_ref[pl.ds(12 + step, 1), :]
    a = (h * 0.5 * (1.0 + lax.erf(h * math.sqrt(0.5)))).astype(BF16)
    acc[...] += dot(a, wdn_ref[...])

    @pl.when(step == pl.num_programs(0) - 1)
    def _():
        out_ref[...] = (res[...] + row(8) * (acc[...] + row(7))).astype(BF16)[0:pages]


def class_close_call(geo, mine, parts, halo, x, to_head, w_out, vec, w_up, w_down):
    d = geo.width
    ff = w_up.shape[1]
    return pl.pallas_call(
        functools.partial(class_close_body, geo),
        out_shape=jax.ShapeDtypeStruct((geo.pages, d), BF16),
        grid=(ff // d,),
        in_specs=[pl.BlockSpec(memory_space=pltpu.SMEM)]
        + [
            full(parts.shape),
            pl.BlockSpec((geo.pages, 16, 3 * d), lambda c: (0, geo.halo // 16 - 1, 0)),
        ]
        + [full(a.shape) for a in (x, to_head, w_out, vec)]
        + [
            pl.BlockSpec((d, d), lambda c: (0, c)),
            pl.BlockSpec((d, d), lambda c: (c, 0)),
        ],
        out_specs=full((geo.pages, d)),
        scratch_shapes=[
            pltpu.VMEM((16, d), F32),
            pltpu.VMEM((16, d), BF16),
            pltpu.VMEM((16, d), F32),
        ],
        compiler_params=params(ROOM),
        cost_estimate=pl.CostEstimate(
            flops=64 * d * (2 * ff + d), transcendentals=16 * ff, bytes_accessed=12 * MIB
        ),
        name="class_close",
    )(mine, parts, halo, x, to_head, w_out, vec, w_up, w_down)


def by_place(dw, cols, core, half, column, keep_ref, send_ref):
    slab = dw.shape[0] // (4 * cols)
    for mine in range(2):

        @pl.when(core == mine)
        def _():
            for dest in range(4 * cols):
                y, b, c = dest // (2 * cols), dest // cols % 2, dest % cols
                place = (y ^ half) * cols + (c ^ column)
                ref = keep_ref if b == mine else send_ref
                ref[place] = dw[dest * slab : (dest + 1) * slab]


def early_weight_body(
    tile, cols, at_ref, x_ref, att_ref, dq_ref, gb_ref, vec_ref, keep_ref, send_ref, nt_ref, sum_ref,
    left, grad, att, gb, sems,
):
    step = pl.program_id(0)
    n, d = x_ref.shape
    copies = (
        pltpu.make_async_copy(att_ref, att, sems.at[0]),
        pltpu.make_async_copy(gb_ref, gb, sems.at[1]),
    )

    @pl.when(step == 0)
    def _():
        for copy in copies:
            copy.start()

        def one(t, carry):
            rows = pl.ds(pl.multiple_of(t * tile, tile), tile)
            unit, _ = norm_parts(unmask(x_ref[rows, :].astype(F32), vec_ref[0:1]))
            grad[rows, :] = (unit * vec_ref[1:2] + vec_ref[2:3]).astype(BF16)
            return carry

        lax.fori_loop(0, n // tile, one, 0)
        left[...] = grad[...].T
        nt_ref[...] = left[...]
        grad[...] = dq_ref[...]
        total = jnp.sum(dq_ref[...].astype(F32), axis=0, keepdims=True)
        sum_ref[...] = jnp.broadcast_to(total, sum_ref.shape)

    @pl.when(step == 1)
    def _():
        for copy in copies:
            copy.wait()
        left[...] = att[...].T
        grad[...] = gb[...]

    dw = dot(left[...], grad[...]).astype(BF16)
    by_place(dw, cols, at_ref[0], at_ref[1], at_ref[2], keep_ref, send_ref)


def late_weight_body(
    cols, at_ref, nt_ref, dk_ref, dv_ref, c_ref, cg_ref, vec_ref, keep_ref, send_ref, sum_ref, grad,
    sem,
):
    step = pl.program_id(0)
    copy = pltpu.make_async_copy(dv_ref, grad.at[1], sem)
    extra = cg_ref[...]

    @pl.when(step == 0)
    def _():
        copy.start()
        grad[0] = dk_ref[...]

    @pl.when(step == 1)
    def _():
        copy.wait()
        total = jnp.sum(grad[1].astype(F32), axis=0, keepdims=True)
        total = total + jnp.sum(extra.astype(F32), axis=0, keepdims=True)
        sum_ref[...] = jnp.broadcast_to(total, sum_ref.shape)

    unit, _ = norm_parts(c_ref[...].astype(F32))
    left = (unit * vec_ref[1:2] + vec_ref[2:3]).astype(BF16)
    dw = (dot(nt_ref[...], grad[step]) + dot_0(left, extra)).astype(BF16)
    by_place(dw, cols, at_ref[0], at_ref[1], at_ref[2], keep_ref, send_ref)


def weight_call(body, where, cols, ins, in_specs, n, d, more, more_specs, scratch, name):
    slab = d // (4 * cols)
    out = jax.ShapeDtypeStruct((2 * cols, slab, 2 * d), BF16)
    block = pl.BlockSpec((2 * cols, slab, d), lambda i, p: (0, 0, i))
    return pl.pallas_call(
        body,
        out_shape=(out, out) + more,
        grid_spec=pltpu.PrefetchScalarGridSpec(
            num_scalar_prefetch=1,
            grid=(2,),
            in_specs=in_specs,
            out_specs=[block, block] + more_specs,
            scratch_shapes=scratch,
        ),
        compiler_params=params(LESS),
        cost_estimate=pl.CostEstimate(
            flops=4 * n * d * d, transcendentals=n, bytes_accessed=2 * (5 * n * d + 2 * d * d)
        ),
        name=name,
    )(where, *ins)


def early_weight_call(where, cols, x, att, dq, gb, vec, tile=256):
    n, d = x.shape
    return weight_call(
        functools.partial(early_weight_body, tile, cols), where, cols, (x, att, dq, gb, vec),
        [hold(x.shape), ANYWHERE, hold(dq.shape), ANYWHERE, hold(vec.shape)], n, d,
        (jax.ShapeDtypeStruct((d, n), BF16), jax.ShapeDtypeStruct((8, d), F32)),
        [hold((d, n)), hold((8, d))],
        [pltpu.VMEM((d, n), BF16)]
        + [pltpu.VMEM((n, d), BF16)] * 3
        + [pltpu.SemaphoreType.DMA((2,))],
        "early_weight",
    )


def late_weight_call(where, cols, nt, dk, dv, cls_rows, cls_grad, vec):
    n, d = dk.shape
    ins = (nt, dk, dv, cls_rows)
    return weight_call(
        functools.partial(late_weight_body, cols), where, cols, ins + (cls_grad, vec),
        [hold(nt.shape), hold(dk.shape), ANYWHERE, hold(cls_rows.shape)]
        + [pl.BlockSpec((16, d), lambda i, p: (0, i)), hold(vec.shape)],
        n, d, (jax.ShapeDtypeStruct((8, d), F32),), [hold((8, d))],
        [pltpu.VMEM((2, n, d), BF16), pltpu.SemaphoreType.DMA(())],
        "late_weight",
    )


def fold_body(
    cols, at_ref, k1_ref, r1_ref, k2_ref, r2_ref, own_ref, to_x_ref, to_y_ref, held_x_ref, held_y_ref
):
    d = k1_ref.shape[2] // 2
    add = lambda a, b, lo, hi: (a[:, :, lo:hi].astype(F32) + b[:, :, lo:hi].astype(F32)).astype(BF16)
    one = lambda lo, hi: add(k1_ref, r1_ref, lo, hi)
    two = lambda lo, hi: add(k2_ref, r2_ref, lo, hi)
    h, n = d // 2, cols // 2
    for page in range(2):

        @pl.when(at_ref[3] == page)
        def _():
            for mine in (True, False):
                if (page == 0) == mine:
                    parts = ((one(0, d), 0), (two(0, h), d), (one(d, d + h), d + h))
                else:
                    parts = ((two(h, 2 * d), 0), (one(d + h, 2 * d), d + h))
                for value, lo in parts:
                    at = slice(lo, lo + value.shape[2])
                    near, far = value[:cols], value[cols:]
                    if mine:
                        own_ref[:, :, at] = near
                        to_y_ref[:n, :, at] = far[:n]
                        held_y_ref[:, :, at] = far[n:]
                    else:
                        held_x_ref[:, :, at] = near[:n]
                        to_x_ref[:n, :, at] = near[n:]
                        to_y_ref[n:, :, at] = far[:n]
                        to_x_ref[n:, :, at] = far[n:]


def fold_call(where, cols, keep1, got1, keep2, got2):
    _, slab, d2 = keep1.shape
    out = lambda k: jax.ShapeDtypeStruct((k, slab, d2), BF16)
    sizes = (cols, cols, cols, cols // 2, cols // 2)
    rows = slab // 3
    spec = lambda k: pl.BlockSpec((k, rows, d2), lambda i, p: (0, i, 0))
    return pl.pallas_call(
        functools.partial(fold_body, cols),
        out_shape=tuple(out(k) for k in sizes),
        grid_spec=pltpu.PrefetchScalarGridSpec(
            num_scalar_prefetch=1,
            grid=(3,),
            in_specs=[spec(2 * cols)] * 4,
            out_specs=[spec(k) for k in sizes],
        ),
        compiler_params=params(LESS),
        name="fold",
    )(where, keep1, got1, keep2, got2)


def token_grad_body(
    pages, heads, x_ref, dq_ref, dk_ref, dv_ref, gres_ref, w_ref, c_ref, cg_ref, vec_ref, part_ref,
    mlp_ref, up_ref, table_ref, sq_ref, sv_ref, dt_ref, o_ref,
):
    d = x_ref.shape[1]
    wq, wk, wv = w_ref[:, 0:d], w_ref[:, d : 2 * d], w_ref[:, 2 * d : 3 * d]
    gain = vec_ref[1:2]
    lead = 2 * pages
    at = lead + pages

    @pl.when(pl.program_id(0) == 0)
    def _():
        o_ref[...] = jnp.zeros_like(o_ref)
        unit, inv = norm_parts(c_ref[...].astype(F32))
        gn = dot_t(cg_ref[:, 0:d], wk) + dot_t(cg_ref[:, d : 2 * d], wv)
        o_ref[0:lead] = part_ref[...]
        o_ref[lead:at] = norm_pull(gn * gain, unit, inv)[0:pages]
        o_ref[at + 1 : at + 2] = jnp.sum(gn * unit, axis=0, keepdims=True)
        o_ref[at + 2 : at + 3] = jnp.sum(gn, axis=0, keepdims=True)
        o_ref[at + 3 : at + 4] = sq_ref[0:1]
        o_ref[at + 4 : at + 5] = sv_ref[0:1]
        o_ref[at + 5 : at + 11] = mlp_ref[0:6]
        ups = up_ref.shape[1] // d
        for i in range(ups):
            o_ref[at + 11 + i : at + 12 + i] = up_ref[0:1, i * d : (i + 1) * d]
        for h in range(heads):
            r, c = divmod(h * LANES, d)
            o_ref[at + 11 + ups + r : at + 12 + ups + r, c : c + LANES] = table_ref[h : h + 1]

    raw = x_ref[...].astype(F32)
    masked = raw > FLAG / 2
    unit, inv = norm_parts(jnp.where(masked, vec_ref[0:1], raw))
    gn = dot_t(dq_ref[...], wq) + dot_t(dk_ref[...], wk) + dot_t(dv_ref[...], wv)
    gs = gres_ref[...] + norm_pull(gn * gain, unit, inv)
    dt_ref[...] = jnp.where(masked, 0.0, gs)
    o_ref[at : at + 1] += jnp.sum(jnp.where(masked, gs, 0.0), axis=0, keepdims=True)
    o_ref[at + 1 : at + 2] += jnp.sum(gn * unit, axis=0, keepdims=True)
    o_ref[at + 2 : at + 3] += jnp.sum(gn, axis=0, keepdims=True)


def token_grad_call(pages, heads, rows_in, whole, tile=256):
    n, d = rows_in[0].shape
    up = whole[6]
    count = 3 * pages + 11 + up.shape[1] // d - (-heads * LANES // d)
    height = -(-count // 8) * 8
    rows = pl.BlockSpec((tile, d), lambda i: (i, 0))
    return pl.pallas_call(
        functools.partial(token_grad_body, pages, heads),
        out_shape=(jax.ShapeDtypeStruct((n, d), F32), jax.ShapeDtypeStruct((height, d), F32)),
        grid=(n // tile,),
        in_specs=[rows] * 5 + [hold(a.shape) for a in whole],
        out_specs=[rows, hold((height, d))],
        compiler_params=params(ROOM),
        cost_estimate=pl.CostEstimate(
            flops=2 * n * d * 3 * d, transcendentals=n, bytes_accessed=2 * (8 * n * d + 3 * d * d)
        ),
        name="token_grad",
    )(*rows_in, *whole)


def passed_along(value, axis, steps):
    count = lax.axis_size(axis)
    first, last = max(0, -steps), min(count, count - steps)
    return lax.ppermute(value, axis, [(i, i + steps) for i in range(first, last)])


def swap(value, axis, bit):
    return lax.ppermute(value, axis, [(i, i ^ bit) for i in range(lax.axis_size(axis))])


def halo_pieces(geo, x, filler):
    top = passed_along(x[:, geo.own - geo.edge :], "row", 1)
    bottom = passed_along(x[:, : geo.edge], "row", -1)
    if filler is not None:
        top, bottom, filler = join((top, bottom, filler))
    to_right, to_left = strips_call(geo, x, top, bottom)
    pieces = top, bottom, passed_along(to_right, "col", 1), passed_along(to_left, "col", -1)
    return pieces, filler


def page_sum(part, by):
    return lax.psum_scatter(part, "dp", scatter_dimension=by, tiled=True)


def spread_sum(grad):
    part = lax.psum_scatter(grad, ("row", "col"), scatter_dimension=0, tiled=True)
    return page_sum(part, 1).astype(F32)


def join(values):
    return lax.optimization_barrier(values)


def shards(
    tokens, cls_token, patch_mask, loss_mask, mask_emb, ln1_gain, ln1_bias, w_qkv, q_bias, v_bias,
    rel_table, w_out, out_bias, scale_attn, ln2_gain, ln2_bias, w_up, up_bias, w_down, down_bias,
    scale_mlp, out_grad,
):
    pages, rows, cols, width = tokens.shape
    heads = rel_table.shape[0]
    geo = Geometry(pages, rows, cols, width, heads)
    count = pages * rows * cols
    row_peers, col_peers = lax.axis_size("row"), lax.axis_size("col")
    grid_rows, grid_cols = rows * row_peers, cols * col_peers
    row_at, col_at, page_at = (lax.axis_index(a) for a in ("row", "col", "dp"))

    ups = w_up.shape[1] // width
    vec = jnp.concatenate(
        [
            mask_emb, ln1_gain, ln1_bias, out_bias, scale_attn, ln2_gain, ln2_bias, down_bias,
            scale_mlp, q_bias, jnp.zeros((width,), F32), v_bias, up_bias,
        ]
    ).reshape(12 + ups, width)
    hm = jnp.asarray(geo.head_mask, BF16)
    hr, hrf = jnp.asarray(geo.head_rows, BF16), jnp.asarray(geo.head_rows, F32)
    sm, sa = jnp.asarray(geo.stat_mask, BF16), jnp.asarray(geo.stat_all, BF16)
    to_head, flank = jnp.asarray(geo.to_head, BF16), jnp.asarray(geo.flank_of, BF16)

    at_row = row_at * rows + BAND * np.arange(8)[:, None] - REACH + geo.slot_row[None, :]
    at_col = col_at * cols + geo.slot_col[None, :]
    inside = (at_row >= 0) & (at_row < grid_rows) & (at_col >= 0) & (at_col < grid_cols)
    inside = inside | (np.arange(geo.slots) >= geo.cls_at)[None, :]
    ok = jnp.where(inside, 0.0, NEG).astype(F32)

    masked = (patch_mask == 1)[..., None]
    x = jnp.where(masked, jnp.asarray(FLAG, BF16), tokens).reshape(pages, geo.own, width)
    pieces, _ = halo_pieces(geo, x, None)
    bias_a = bias_table(geo, rel_table, 0)
    own = qkv_call(qkv_own_body, geo.own, (x,), (w_qkv, vec), "qkv_own")
    first = np.arange(16)[:, None] == 0
    cls_block = jnp.where(first, cls_token[:, None, :], jnp.zeros((), BF16))
    halo = qkv_call(
        functools.partial(qkv_halo_body, geo), geo.halo, pieces + (cls_block,),
        (flank, w_qkv, vec), "qkv_halo",
    )
    att, lse, probs, cls_part = attend_call(geo, own, halo, bias_a, ok, hm, hr, hrf)
    att, lse, x = att.reshape(count, width), lse.reshape(count, LANES), x.reshape(count, width)
    counted = (patch_mask * loss_mask == 1)[..., None]
    out_g = jnp.where(counted, out_grad, jnp.zeros((), BF16)).reshape(count, width)
    act, dh, d_mlp, d_upb = hidden_call(
        att, x, out_g, w_out, vec, w_up, w_down, row_peers * col_peers
    )
    d_mlp = lax.psum_scatter(d_mlp, ("row", "col"), scatter_dimension=0, tiled=True)[0]
    out, gmx, gres, gb, vg_mlp = close_call(
        att, x, out_g, lse, act, dh, w_out, vec, w_up, w_down, to_head
    )
    gmx = gmx.reshape(pages, geo.own, width + LANES)
    rel_late, _ = join((rel_table, gb))
    pieces, bias_b = halo_pieces(geo, gmx, bias_table(geo, rel_late, 1))
    dq, d_table = query_grad_call(geo, probs, own, halo, gmx, hm, sm)
    class_bias = jnp.concatenate([rel_table[:, SPAN * SPAN], jnp.zeros((16 - heads,), F32)])
    class_bias = jnp.broadcast_to(class_bias[:, None], (16, geo.own))
    cls_rows = jnp.concatenate([cls_token, jnp.zeros((16 - pages, width), BF16)], axis=0)
    direct = (lax.axis_size("dp"), row_peers, col_peers) == (2, 4, 4)
    if direct:
        where = jnp.stack([row_at % 2, row_at // 2, col_at, page_at]).astype(jnp.int32)
    else:
        where = jnp.zeros((4,), jnp.int32)
    dq = dq.reshape(count, width)
    keep1, send1, nt, sum_q = early_weight_call(where, col_peers, x, att, dq, gb, vec)
    pieces, bias_b, nt = join((pieces, bias_b, nt))
    if direct:
        got1 = swap(send1, "row", 1)
    dk, dv, cls_low = key_grad_call(
        geo, own, halo, gmx, pieces, bias_b, ok, hm, sa, flank, hr, hrf, class_bias
    )
    dk, dv = dk.reshape(count, width), dv.reshape(count, width)
    keep2, send2, sum_v = late_weight_call(where, col_peers, nt, dk, dv, cls_rows, cls_low, vec)
    wide = lambda a: a.astype(F32)
    if direct:
        got2 = swap(send2, "row", 1)
        mine, to_x, to_y, held_x, held_y = fold_call(where, col_peers, keep1, got1, keep2, got2)
        mine, dq = join((mine, dq))
        near_x = swap(to_x, "dp", 1)
        near_y = swap(to_y, "row", 2)
    d_tok, block = token_grad_call(
        pages, heads, (x, dq, dk, dv, gres),
        (w_qkv, cls_rows, cls_low, vec, cls_part, vg_mlp, d_upb, d_table, sum_q, sum_v),
    )
    slab = width // (row_peers * col_peers)
    if direct:
        near_x, near_y, block = join((near_x, near_y, block))
        n = col_peers // 2
        last_x = swap((wide(held_x) + wide(near_y[n:])).astype(BF16), "dp", 1)
        last_y = swap((wide(held_y) + wide(near_x[n:])).astype(BF16), "row", 2)
        late = [
            (wide(mine[:n]) + wide(near_y[:n]) + wide(last_x)).astype(BF16),
            (wide(mine[n:]) + wide(near_x[:n]) + wide(last_y)).astype(BF16),
        ]
        late = [a[i] for a in late for i in range(n)]
        up, down = d_mlp[: ups * slab], d_mlp[ups * slab :]
        cut_up, cut_down = ups * slab // 2, width // 2

        def halves(place):
            return jnp.concatenate(
                [
                    lax.dynamic_slice_in_dim(up, place * cut_up, cut_up, 0),
                    lax.dynamic_slice_in_dim(down, place * cut_down, cut_down, 1).reshape(
                        -1, width
                    ),
                ],
                axis=0,
            )

        other = swap(halves(1 - page_at), "dp", 1)

    lead = 2 * pages
    vectors = block[lead:]
    parts, mine_at, place = block[:lead], jnp.zeros((), jnp.int32), 1
    sent = block
    for axis in ("col", "row"):
        peers, rows_in = lax.axis_size(axis), parts.shape[0]
        if direct and axis == "row":
            sent, *late = join((sent, *late))
            beside = [swap(late[step], "col", step) for step in range(1, col_peers)]
        got = [swap(sent, axis, bit) for bit in range(1, peers)]
        level = [vectors] + [g[rows_in:] for g in got]
        while len(level) > 1:
            level = [a + b for a, b in zip(level[0::2], level[1::2])]
        vectors = level[0]
        parts = jnp.concatenate([parts] + [g[:rows_in] for g in got], axis=0)
        mine_at = mine_at + place * lax.axis_index(axis).astype(jnp.int32)
        place = place * peers
        sent = jnp.concatenate([parts, vectors], axis=0)

    if direct:
        beside, parts = join((beside, parts))
    d_cls, v = vectors[:pages], vectors[pages:]
    bit = 1
    while bit < lax.axis_size("dp"):
        v, bit = v + swap(v, "dp", bit), 2 * bit
    out_cls = class_close_call(
        geo, mine_at[None], parts.reshape(-1, 2 * pages, width), halo, cls_rows, to_head, w_out, vec, w_up,
        w_down,
    )

    half = 3 * width // 2
    if direct:
        other, v, out_cls = join((other, v, out_cls))
        late = wide(late[0])
        for part in beside:
            late = late + wide(part)
        d_qkv, d_wout = late[:, :half], late[:, half:]
        both = wide(halves(page_at)) + wide(other)
        d_up = jnp.transpose(both[:cut_up].reshape(-1, slab, width), (1, 0, 2)).reshape(slab, -1)
        d_down = both[cut_up:].reshape(-1, cut_down)
    else:
        def whole(keep, send):
            both = jnp.stack([keep, send]).reshape(2, 2, col_peers, slab, 2 * width)
            return jnp.transpose(both, (1, 0, 2, 3, 4)).reshape(width, 2 * width)

        early, late = whole(keep1, send1), whole(keep2, send2)
        d_qkv = spread_sum(jnp.concatenate([early[:, :width], late], axis=1))
        d_wout = spread_sum(early[:, width:])
        d_up = jnp.transpose(d_mlp[: ups * slab].reshape(ups, slab, width), (1, 0, 2))
        d_up = page_sum(d_up.reshape(slab, ups * width), 1).astype(F32)
        d_down = page_sum(d_mlp[ups * slab :], 1).astype(F32)

    d_rel = v[11 + ups : 13 + ups].reshape(-1)[: heads * LANES].reshape(heads, LANES)[:, : SPAN * SPAN + 1]
    return (
        out.reshape(tokens.shape),
        out_cls,
        d_tok.reshape(tokens.shape),
        d_cls,
        d_qkv,
        d_wout,
        d_up,
        d_down,
        v[0],
        v[1],
        v[2],
        v[3],
        v[4],
        d_rel,
        v[10],
        v[9],
        v[7],
        v[8],
        v[11 : 11 + ups].reshape(-1),
        v[6],
        v[5],
    )


def solution(mesh):
    tile = P("dp", "row", "col", None)
    flat = P("dp", "row", "col")
    weights = P(("row", "col"), "dp")
    return jax.shard_map(
        shards,
        mesh=mesh,
        in_specs=(tile, P("dp", None), flat, flat) + (P(),) * 17 + (tile,),
        out_specs=(tile, P("dp", None), tile, P("dp", None)) + (weights,) * 4 + (P(),) * 13,
        check_vma=False,
    )
```
